256 devices in a mesh: band: 8 (over y, core), sub: 32 (over x, z).
Axes of the slice: x: 4, y: 4, z: 8, core: 2. Of those that a mesh axis runs over, the one named last changes fastest.
Arguments:
- background: float32 [64, 4, 768, 1536], P('band', None, 'sub'), may hold values from -18 to 18
- obs_columns: float32 [64, 4, 131072], P('band', None, 'sub'), may hold values from -18 to 18
- obs_owner: int32 [131072, 1], P('sub'), may hold values from 0 to 31; in each aligned block of 4096 rows (0 to 4095, 4096 to 8191, ...) at most 256 rows name the same one
- obs_cell: int32 [131072], P('sub'), may hold values from 0 to 36863
- lat_length: float32 [64, 4, 768], P('band'), may hold values from 1 to 2200
- lon_length: float32 [64, 4], P('band'), may hold values from 2 to 48
- vert_length: float32 [64, 4], P('band'), may hold values from 1 to 720
Outputs:
- filtered: float32 [64, 4, 768, 1536], P('band', None, 'sub')
The draws below stay inside these ranges and needn't reach their ends.
Inputs may be any that keep to these rules, and one draw needn't show every extreme that they name: `obs_owner`: among the 4096 observations of one device no subdomain is named more than 256 times, and in every draw some device names some subdomain exactly 256 times.
All inputs are finite; a program needn't handle non-finite values.
Results may differ from the reference program's by a relative error of at most 0.0003.
Values sent between devices are 32-bit elements; how exact they have to be, the bound alone decides.
A program may use at most 128 MiB of HBM per device.

```python
import math
import jax
import jax.numpy as jnp
import numpy as np
from jax import lax

VARIABLE_TOTAL = 4
LATITUDE_ROWS = 768
NLON = 1536
OBS_DEV = 4096
LEVEL_TOTAL = 64
NOBS = 131072
CAP = 256
N_SUB = 32


def draw_background(key, part):
    jagged_key = jax.random.fold_in(jax.random.fold_in(key, 17), 0)
    return 3.0 * jax.random.truncated_normal(jagged_key, -6.0, 6.0, (LEVEL_TOTAL, VARIABLE_TOTAL, LATITUDE_ROWS, NLON), jnp.float32)


def draw_lat_length(key, part):
    root_key, jagged_key, spike_key = jax.random.split(jax.random.fold_in(key, 11), 3)
    log_base = jax.random.uniform(root_key, (LEVEL_TOTAL, VARIABLE_TOTAL, 1), jnp.float32, math.log(6.0), math.log(1536.0))
    rough = jax.random.uniform(jagged_key, (LEVEL_TOTAL, VARIABLE_TOTAL, LATITUDE_ROWS), jnp.float32, math.log(0.7), math.log(1.4))
    spike_sample = jax.random.uniform(spike_key, (2, LEVEL_TOTAL, VARIABLE_TOTAL, LATITUDE_ROWS), jnp.float32)
    spike_length = 1.5 + 1.5 * spike_sample[1]
    scale_length = jnp.exp(log_base + rough)
    return jnp.where(spike_sample[0] < 2.0 / LATITUDE_ROWS, spike_length, scale_length)


def draw_vert_length(key, part):
    sequence_key, location_key, jagged_key, spike_key = jax.random.split(jax.random.fold_in(key, 13), 4)
    ladder = jax.random.permutation(sequence_key, VARIABLE_TOTAL).astype(jnp.float32)
    spot = jax.random.uniform(location_key, (VARIABLE_TOTAL,), jnp.float32)
    share = (ladder + spot) / VARIABLE_TOTAL
    log_base = (math.log(2.0) + share * (math.log(512.0) - math.log(2.0)))[None, :]
    rough = jax.random.uniform(jagged_key, (LEVEL_TOTAL, VARIABLE_TOTAL), jnp.float32, math.log(0.7), math.log(1.4))
    spike_sample = jax.random.uniform(spike_key, (2, LEVEL_TOTAL, VARIABLE_TOTAL), jnp.float32)
    spike_length = 1.5 + 1.5 * spike_sample[1]
    scale_length = jnp.exp(log_base + rough)
    return jnp.where(spike_sample[0] < 2.0 / LEVEL_TOTAL, spike_length, scale_length)


def set_ends(entries, rng, least, top_value):
    place = [jax.random.randint(jax.random.fold_in(rng, axis), (), 0, length) for axis, length in enumerate(entries.shape)]
    main_axis = entries.shape.index(max(entries.shape))
    neighbour = place[:main_axis] + [(place[main_axis] + 1) % entries.shape[main_axis]] + place[main_axis + 1:]
    return entries.at[tuple(place)].set(least).at[tuple(neighbour)].set(top_value)


def level_of(key, shape, cuts, least, top_value):
    level, own = 1.0, jax.random.fold_in(key, 6)
    for axis_at, shards_of in cuts:
        steps = jnp.exp(jax.random.uniform(jax.random.fold_in(own, axis_at), (shards_of,), jnp.float32, least / len(cuts), top_value / len(cuts)))
        level = level * jnp.repeat(steps, shape[axis_at] // shards_of).reshape([-1 if axis == axis_at else 1 for axis in range(len(shape))])
    return level


def assign_block(stream_key, own, number, rows, count, top, limit, slope):
    ranking = jax.random.permutation(stream_key, count)
    heavy_load, common = load_shares(count, rows * top, limit, slope, True), load_shares(count, rows * top, limit, slope, False)
    places = jnp.arange(count)

    def named(lengths, offset_by):
        used = int((lengths > 0).sum())
        fixed = max(1, used // 4)
        passed = fixed + (places - fixed + offset_by * (used - fixed)) % max(1, count - fixed)
        return jnp.zeros((count,), jnp.int32).at[ranking[jnp.where(places < fixed, places, passed)]].set(jnp.asarray(lengths, jnp.int32))

    lengths = jnp.where(number % 4 == 0, named(heavy_load, number // 4), named(common, number - number // 4 - 1))
    mixed = jax.random.permutation(jax.random.fold_in(own, 3), count)
    source_of, receiver = mixed[0:count // 2 * 2:2], mixed[1:count // 2 * 2:2]
    room = jnp.minimum(lengths[source_of] - 1, limit - lengths[receiver]) // 2
    room = jnp.where((source_of == ranking[0]) | (receiver == ranking[0]) | (lengths[receiver] == 0), 0, jnp.maximum(room, 0))
    passed = jax.random.randint(jax.random.fold_in(own, 4), (count // 2,), 0, 1 << 20) % (room + 1)
    lengths = lengths.at[source_of].add(-passed).at[receiver].add(passed)
    items = jnp.searchsorted(jnp.cumsum(lengths), jnp.arange(rows * top), side="right").astype(jnp.int32)
    grid = items.reshape(top, rows).T
    grid = grid[jax.random.permutation(jax.random.fold_in(own, 1), rows)]
    offset_by = jax.random.randint(jax.random.fold_in(own, 2), (rows, 1), 0, top)
    return jnp.take_along_axis(grid, (jnp.arange(top)[None, :] + offset_by) % top, axis=1)


def load_shares(count, total, reach, skew, full):
    loads = [(1 << 20) // math.isqrt(standing ** skew) + 1 for standing in range(1, count + 1)]
    largest = reach if full else min(reach, max(-(-total // count), total * loads[0] // sum(loads)))
    least = 1 if total - largest >= count - 1 else 0
    given, spare = [largest] + [least] * (count - 1), total - largest - least * (count - 1)
    while spare > 0:
        movable = [i for i in range(1, count) if given[i] < largest] or [i for i in range(1, count) if given[i] < reach]
        mass, budget = sum([loads[i] for i in movable]), spare
        for i in movable:
            more = min(reach - given[i], max(1, budget * loads[i] // mass), spare)
            given[i] = given[i] + more
            spare = spare - more
    return np.array(given)


def noise(own_key, extent, deviation, reach, cuts=(), kind=jnp.bfloat16):
    values = jax.random.normal(own_key, extent, jnp.float32) * deviation
    if len(cuts) > 0:
        values = level_of(own_key, extent, cuts, -0.22, 0.18) * values
    return jnp.clip(values, min=-reach, max=reach).astype(kind)


def setup_inputs(seed: int = 0) -> dict:
    streams_of = jax.random.split(jax.random.key(seed), 8)
    background = draw_background(jax.random.fold_in(streams_of[7], 71), 0)
    obs_columns = noise(streams_of[1], (LEVEL_TOTAL, VARIABLE_TOTAL, NOBS), 3.0, 18.0, ((0, 8), (2, 32)), jnp.float32)
    obs_owner_keys = jax.random.split(jax.random.fold_in(streams_of[2], 1), NOBS // OBS_DEV)
    obs_owner_turns = jax.random.permutation(jax.random.fold_in(streams_of[2], 3), NOBS // OBS_DEV)
    obs_owner = jax.vmap(lambda own, number: assign_block(jax.random.fold_in(streams_of[2], 2), own, number, OBS_DEV, N_SUB, 1, CAP, 2))(obs_owner_keys, obs_owner_turns).reshape((NOBS, 1))
    obs_cell = set_ends(jax.random.randint(streams_of[3], (NOBS,), 0, LATITUDE_ROWS // N_SUB * NLON), jax.random.fold_in(streams_of[3], 1), 0, (LATITUDE_ROWS // N_SUB * NLON) - 1).astype(jnp.int32)
    lat_length = draw_lat_length(jax.random.fold_in(streams_of[7], 71), 0)
    lon_length = jnp.clip(jnp.exp(math.log(48.0) - 3.1780538 * jax.random.uniform(streams_of[5], (LEVEL_TOTAL, VARIABLE_TOTAL), jnp.float32) ** level_of(streams_of[5], (LEVEL_TOTAL, VARIABLE_TOTAL), ((0, 8),), -0.2, 0.2)), 2.0, 48.0)
    vert_length = draw_vert_length(jax.random.fold_in(streams_of[7], 71), 0)
    return {"background": background, "obs_columns": obs_columns, "obs_owner": obs_owner, "obs_cell": obs_cell, "lat_length": lat_length, "lon_length": lon_length, "vert_length": vert_length}


def decay_of(scale_length):
    return jnp.exp(-1.0 / scale_length)


def sweep(values, decays, reverse):
    def advance(carry_state, inputs):
        column, factor = inputs
        output = factor * carry_state + (1.0 - factor) * column
        return output, output

    _, result = lax.scan(advance, jnp.zeros_like(values[0]), (values, decays), reverse=reverse)
    return result


def cycle_sweep(values, decay_row, reverse):
    scale_length = values.shape[0]
    factors = jnp.broadcast_to(decay_row, (scale_length,) + decay_row.shape)
    zero_start = sweep(values, factors, reverse)
    log_decay = jnp.log(decay_row)
    powers = jnp.exp(jnp.arange(1, scale_length + 1, dtype=jnp.float32).reshape(scale_length, 1, 1) * log_decay[None])
    full_turn = 1.0 - jnp.exp(scale_length * log_decay)
    if reverse:
        wrapped = zero_start[0] / full_turn
        return zero_start + jnp.flip(powers, 0) * wrapped[None]
    wrapped = zero_start[scale_length - 1] / full_turn
    return zero_start + powers * wrapped[None]


def horizontal(level_field, lat_decay, lon_decay):
    moved = jnp.transpose(level_field, (1, 0, 2))
    lat_factors = jnp.transpose(lat_decay, (1, 0))[:, :, None]
    for reverse in (False, True, False, True):
        moved = sweep(moved, lat_factors, reverse)
    moved = jnp.transpose(moved, (2, 1, 0))
    lon_factor = lon_decay[:, None]
    for reverse in (False, True, False, True):
        moved = cycle_sweep(moved, lon_factor, reverse)
    return jnp.transpose(moved, (1, 2, 0))


def reference(background, obs_columns, obs_owner, obs_cell, lat_length, lon_length, vert_length):
    strip_cells = (LATITUDE_ROWS // N_SUB) * NLON
    grid_cell = (obs_owner[:, 0] * strip_cells + obs_cell).astype(jnp.int32)
    flat = background.reshape(LEVEL_TOTAL, VARIABLE_TOTAL, LATITUDE_ROWS * NLON)
    flat = flat.at[:, :, grid_cell].add(obs_columns)
    forced = flat.reshape(LEVEL_TOTAL, VARIABLE_TOTAL, LATITUDE_ROWS, NLON)
    lat_decay = decay_of(lat_length)
    lon_decay = decay_of(lon_length)
    vert_decay = decay_of(vert_length)

    def one_level(inputs):
        return horizontal(inputs[0], inputs[1], inputs[2])

    smoothed = lax.map(one_level, (forced, lat_decay, lon_decay))
    vert_factors = vert_decay[:, :, None, None]
    smoothed = sweep(smoothed, vert_factors, False)
    smoothed = sweep(smoothed, vert_factors, True)
    return smoothed
```

```python
import functools

import jax
import jax.numpy as jnp
from jax import lax
from jax.experimental import pallas as pl
from jax.experimental.pallas import tpu as pltpu
from jax.sharding import PartitionSpec as P

LANE = 128
f32 = jnp.float32
bf16 = jnp.bfloat16


def vmem(mib):
    return pltpu.CompilerParams(vmem_limit_bytes=mib << 20)


def cost(flops, moved):
    return pl.CostEstimate(flops=flops, bytes_accessed=moved, transcendentals=0)


def route_slots(owners, sub_count, capacity):
    count = owners.shape[0]
    block = 128
    owner_block = owners.reshape(count // block, block)
    match = (owner_block[:, :, None] == jnp.arange(sub_count, dtype=jnp.int32)).astype(bf16)
    position = jnp.arange(block)
    lower = (position[:, None] > position[None, :]).astype(bf16)
    ahead = jnp.einsum("ij,bjo->bio", lower, match, preferred_element_type=f32)
    totals = jnp.sum(match.astype(f32), axis=1)
    base = jnp.cumsum(totals, axis=0) - totals
    rank = jnp.sum((ahead + base[:, None, :]) * match.astype(f32), axis=2)
    return owners * capacity + rank.reshape(count).astype(jnp.int32)


def pack_kernel(slots, cells, zeros, values, packed, sent_cells, rows, big, sem):
    clear = pltpu.make_async_copy(zeros, sent_cells, sem)
    clear.start()
    count = values.shape[1]
    total = big.shape[0]

    @pl.loop(0, total // 64)
    def _(i):
        big[pl.ds(pl.multiple_of(i * 64, 64), 64), :] = jnp.zeros((64, LANE), f32)

    for j in range(count // LANE):
        part = values[:, j * LANE : (j + 1) * LANE]
        rows[j * LANE : (j + 1) * LANE, :] = jnp.concatenate([part] * 4, axis=0).T
    clear.wait()

    step = 16

    @pl.loop(0, count // step)
    def _(i):
        for u in range(step):
            j = i * step + u
            slot = slots[j]
            big[pl.ds(slot, 1), :] = rows[pl.ds(j, 1), :]
            sent_cells[slot] = cells[j]

    quarter = lax.broadcasted_iota(jnp.int32, (64, LANE), 1) // 32

    @pl.loop(0, total // 256)
    def _(d):
        start = pl.multiple_of(d * 256, 256)
        out = big[pl.ds(start, 64), :]
        for k in range(1, 4):
            out = jnp.where(quarter == k, big[pl.ds(start + 64 * k, 64), :], out)
        packed[pl.ds(pl.multiple_of(d * 64, 64), 64), :] = out


def pack(slots, cells, values, total):
    count = values.shape[1]
    smem = pl.BlockSpec(memory_space=pltpu.SMEM)
    return pl.pallas_call(
        pack_kernel,
        out_shape=(
            jax.ShapeDtypeStruct((total // 4, LANE), f32),
            jax.ShapeDtypeStruct((total,), jnp.int32),
        ),
        in_specs=[smem, smem, pl.BlockSpec(memory_space=pl.ANY), pl.BlockSpec(memory_space=pltpu.VMEM)],
        out_specs=(pl.BlockSpec(memory_space=pltpu.VMEM), smem),
        scratch_shapes=[
            pltpu.VMEM((count, LANE), f32),
            pltpu.VMEM((total, LANE), f32),
            pltpu.SemaphoreType.DMA,
        ],
        compiler_params=vmem(32),
        cost_estimate=cost(0, 4 << 20),
        name="pack",
    )(slots, cells, jnp.zeros((total,), jnp.int32), values)


def deposit_kernel(places, got, field, spread, f1, f2, f3, masks):
    total = spread.shape[0]
    chains = [field, f1, f2, f3]
    depth = field.shape[0]

    @pl.loop(0, depth // 64)
    def _(i):
        at = pl.ds(pl.multiple_of(i * 64, 64), 64)
        for chain in chains:
            chain[at, :] = jnp.zeros((64, LANE), f32)

    lane_quarter = lax.broadcasted_iota(jnp.int32, (8, LANE), 1) // 32
    masks[...] = (lane_quarter == lax.broadcasted_iota(jnp.int32, (8, LANE), 0)).astype(f32)
    quarter = lax.broadcasted_iota(jnp.int32, (64, LANE), 1) // 32

    @pl.loop(0, total // 256)
    def _(d):
        part = got[pl.ds(pl.multiple_of(d * 64, 64), 64), :]
        for k in range(4):
            one = jnp.where(quarter == k, part, 0.0)
            one = one + pltpu.roll(one, 32, 1)
            one = one + pltpu.roll(one, 64, 1)
            spread[pl.ds(pl.multiple_of(d * 256 + k * 64, 64), 64), :] = one

    step = 4

    @pl.loop(0, total // (4 * step))
    def _(i):
        for u in range(step):
            loads = []
            for c in range(4):
                j = (i * step + u) * 4 + c
                place = places[j]
                row = lax.shift_right_logical(place, 2)
                mask = masks[pl.ds(place & 3, 1), :]
                loads.append((row, spread[pl.ds(j, 1), :] * mask))
            olds = [chains[c][pl.ds(loads[c][0], 1), :] for c in range(4)]
            for c in range(4):
                chains[c][pl.ds(loads[c][0], 1), :] = olds[c] + loads[c][1]

    @pl.loop(0, depth // 64)
    def _(i):
        at = pl.ds(pl.multiple_of(i * 64, 64), 64)
        field[at, :] = (field[at, :] + f1[at, :]) + (f2[at, :] + f3[at, :])


def deposit(places, got, depth):
    total = places.shape[0]
    return pl.pallas_call(
        deposit_kernel,
        out_shape=jax.ShapeDtypeStruct((depth, LANE), f32),
        in_specs=[pl.BlockSpec(memory_space=pltpu.SMEM), pl.BlockSpec(memory_space=pltpu.VMEM)],
        out_specs=pl.BlockSpec(memory_space=pltpu.VMEM),
        scratch_shapes=[pltpu.VMEM((total, LANE), f32)]
        + [pltpu.VMEM((depth, LANE), f32)] * 3
        + [pltpu.VMEM((8, LANE), f32)],
        compiler_params=vmem(40),
        cost_estimate=cost(0, 16 << 20),
        name="deposit",
    )(places, got)


def lat_sweeps(rows, decay, starts):
    count = len(rows)
    ends = []
    for sweep in range(4):
        order = range(count) if sweep % 2 == 0 else range(count - 1, -1, -1)
        state = starts[sweep]
        out = [None] * count
        for r in order:
            state = rows[r] + decay(r) * (state - rows[r])
            out[r] = state
        ends.append(state)
        rows = out
    return rows, ends


def lat_moments_kernel(row_count, groups, field, background, decay, forced, moments):
    ct = pl.program_id(0)
    tiles = background.shape[1] // LANE
    for rr in range(row_count // 4):
        turned = field[rr].T
        for q in range(4):
            for o in range(groups // 8):
                at = pl.ds(o * 8 * row_count + rr * 4 + q, 8, stride=row_count)
                first = q * groups + o * 8
                forced[at, :] = background[at, :] + turned[first : first + 8, :]
    zero = jnp.zeros((8, LANE), f32)
    for o in range(groups // 8):
        rows = [
            forced[pl.ds(o * 8 * row_count + r, 8, stride=row_count), :] for r in range(row_count)
        ]
        _, ends = lat_sweeps(
            rows, lambda r: decay[r * groups + o * 8 : r * groups + o * 8 + 8, :], [zero] * 4
        )
        per_group = moments.shape[0] // groups
        for k in range(4):
            start = o * 8 * per_group + k * (per_group // 4) + ct
            moments[pl.ds(start, 8, stride=per_group), :] = ends[k]


def lat_moments(field, background, decay, row_count, groups):
    rows, columns = background.shape
    tiles = columns // LANE
    block = pl.BlockSpec((rows, LANE), lambda i: (0, i))
    whole = pl.BlockSpec((rows, LANE), lambda i: (0, 0))
    return pl.pallas_call(
        functools.partial(lat_moments_kernel, row_count, groups),
        grid=(tiles,),
        out_shape=(
            jax.ShapeDtypeStruct(background.shape, f32),
            jax.ShapeDtypeStruct((groups * 4 * tiles, LANE), f32),
        ),
        in_specs=[pl.BlockSpec((row_count // 4, LANE, LANE), lambda i: (0, i, 0)), block, whole],
        out_specs=(block, pl.BlockSpec((groups * 4 * tiles, LANE), lambda i: (0, 0))),
        compiler_params=vmem(32),
        cost_estimate=cost(0, 16 << 20),
        name="lat_moments",
    )(field.reshape(row_count // 4, columns, LANE), background, decay)


def lon_weights(length, columns):
    blocks = columns // LANE
    length = length[:, None, None]
    kappa = jnp.tanh(0.5 / length)
    beta = kappa * kappa
    alpha = beta / jnp.tanh(1.0 / length)
    i = jnp.arange(LANE, dtype=f32)

    def power(n):
        return jnp.exp(-n / length)

    gap = jnp.abs(i[:, None] - i[None, :])[None]
    local = (alpha + beta * gap) * power(gap)
    up, down = i[None, :, None], (LANE - 1.0) - i[None, :, None]
    sums = jnp.concatenate(
        [power(down), down * power(down), power(up), up * power(up)], axis=2
    )
    sums = jnp.pad(sums, ((0, 0), (0, 0), (0, LANE - 4)))
    first = jnp.concatenate([local, sums], axis=2)
    index = jnp.arange(LANE)
    src, dst = index[:, None], index[None, :]
    source, target = src // 4, dst // 4
    backward = (src % 4) >= 2
    steps = jnp.where(backward, source - target - 1, target - source - 1) % blocks
    gap = (LANE * steps).astype(f32)[None]
    turn = power(float(columns))
    left = -jnp.expm1(-float(columns) / length)
    same = power(gap) / left
    cross = (gap + columns * turn / left) * same
    used = (source < blocks) & (target < blocks)
    mix = jnp.where((used & (src % 4 == dst % 4))[None], same, 0.0)
    mix = jnp.where((used & (src % 2 == 0) & (dst % 4 == src % 4 + 1))[None], cross, mix)
    near, far = i[None, None, :] + 1.0, LANE - i[None, None, :]
    back = jnp.concatenate(
        [
            (alpha + beta * near) * power(near),
            beta * power(near),
            (alpha + beta * far) * power(far),
            beta * power(far),
        ],
        axis=1,
    )
    back = jnp.pad(back, ((0, 0), (0, LANE - 4), (0, 0)))
    return first, mix, back


def split(x):
    high = x.astype(bf16)
    return high, (x - high.astype(f32)).astype(bf16)


def dot3(x, w):
    xh, xl = split(x)
    wh, wl = split(w)

    def dot(a, b):
        return jnp.dot(a, b, preferred_element_type=f32)

    return dot(xh, wh) + (dot(xh, wl) + dot(xl, wh))


def lon_apply(x, first, mix, back):
    count, columns = x.shape
    blocks = columns // LANE
    stacked = jnp.concatenate([x[:, b * LANE : (b + 1) * LANE] for b in range(blocks)], axis=0)
    both = dot3(stacked, first)
    local, sums = both[:, :LANE], both[:, LANE:]
    line = sums[:count]
    for b in range(1, blocks):
        line = line + pltpu.roll(sums[b * count : (b + 1) * count], 4 * b, 1)
    states = dot3(line, mix)
    spread = jnp.concatenate(
        [states] + [pltpu.roll(states, LANE - 4 * b, 1) for b in range(1, blocks)], axis=0
    )
    out = local + dot3(spread, back)
    return jnp.concatenate([out[b * count : (b + 1) * count] for b in range(blocks)], axis=1)


def lon_kernel(x, first, mix, back, out):
    out[...] = lon_apply(x[...], first[0], mix[0], back[0])


def lon_filter(x, weights, row_count):
    rows, columns = x.shape
    block = pl.BlockSpec((row_count, columns), lambda i: (i, 0))
    return pl.pallas_call(
        lon_kernel,
        grid=(rows // row_count,),
        out_shape=jax.ShapeDtypeStruct(x.shape, f32),
        in_specs=[
            block,
            pl.BlockSpec((1, LANE, 2 * LANE), lambda i: (i, 0, 0)),
            pl.BlockSpec((1, LANE, LANE), lambda i: (i, 0, 0)),
            pl.BlockSpec((1, LANE, LANE), lambda i: (i, 0, 0)),
        ],
        out_specs=block,
        compiler_params=vmem(32),
        cost_estimate=cost(6 * rows * columns * 3 * LANE, 60 << 20),
        name="lon",
    )(x, *weights)


def hub_kernel(decay, moments, first, mix, back, states, work):
    blocks = 32
    depth = moments.shape[0] // blocks
    tiles = depth // 4
    count = decay.shape[0]
    coef = [decay[r : r + 1, :] for r in range(count)]

    def forward(rows):
        state, out = jnp.zeros((1, LANE), f32), []
        for r in range(count):
            state = rows[r] + coef[r] * (state - rows[r])
            out.append(state)
        return out

    def backward(rows):
        state, out = jnp.zeros((1, LANE), f32), [None] * count
        for r in range(count - 1, -1, -1):
            state = rows[r] + coef[r] * (state - rows[r])
            out[r] = state
        return out

    state, down = jnp.ones((1, LANE), f32), []
    for r in range(count):
        state = coef[r] * state
        down.append(state)
    full = state
    state, up = jnp.ones((1, LANE), f32), [None] * count
    for r in range(count - 1, -1, -1):
        state = coef[r] * state
        up[r] = state
    bp = backward(down)
    fbp = forward(bp)
    bfbp = backward(fbp)
    fq = forward(up)
    bfq = backward(fq)
    t21, t31, t41, t32, t42 = bp[0], fbp[-1], bfbp[0], fq[-1], bfq[0]

    def at(table, d):
        return jnp.broadcast_to(table[:, d : d + 1], (tiles, LANE))

    def moment(d, k):
        return moments[d * depth + k * tiles : d * depth + (k + 1) * tiles, :]

    def put(d, k, value):
        for t in range(tiles):
            work[k * blocks + d, t * LANE : (t + 1) * LANE] = value[t]

    zero = jnp.zeros((tiles, LANE), f32)
    s = [[None] * blocks for _ in range(4)]
    carry = zero
    for d in range(blocks):
        s[0][d] = carry
        carry = at(full, d) * carry + moment(d, 0)
    carry = zero
    for d in range(blocks - 1, -1, -1):
        s[1][d] = carry
        carry = at(full, d) * carry + (moment(d, 1) + at(t21, d) * s[0][d])
    carry = zero
    for d in range(blocks):
        s[2][d] = carry
        carry = at(full, d) * carry + (
            moment(d, 2) + at(t31, d) * s[0][d] + at(t32, d) * s[1][d]
        )
    carry = zero
    for d in range(blocks - 1, -1, -1):
        s[3][d] = carry
        carry = at(full, d) * carry + (
            moment(d, 3) + at(t41, d) * s[0][d] + at(t42, d) * s[1][d] + at(t21, d) * s[2][d]
        )
    for k in range(4):
        for d in range(blocks):
            put(d, k, s[k][d])
    done = lon_apply(work[...], first[0], mix[0], back[0])
    for k in range(4):
        for d in range(blocks):
            row = done[k * blocks + d : k * blocks + d + 1]
            for t in range(tiles):
                base = d * depth + k * tiles + t
                states[base : base + 1, :] = row[:, t * LANE : (t + 1) * LANE]


def hub(decay, moments, weights):
    depth = moments.shape[0] // 32
    return pl.pallas_call(
        hub_kernel,
        out_shape=jax.ShapeDtypeStruct(moments.shape, f32),
        in_specs=[pl.BlockSpec(memory_space=pltpu.VMEM)] * 5,
        out_specs=pl.BlockSpec(memory_space=pltpu.VMEM),
        scratch_shapes=[pltpu.VMEM((128, depth // 4 * LANE), f32)],
        compiler_params=vmem(32),
        cost_estimate=cost(0, 4 << 20),
        name="hub",
    )(decay, moments, *weights)


def level_sweeps(rows, decay, starts):
    count = len(rows)
    ends = []
    for sweep in range(2):
        order = range(count) if sweep == 0 else range(count - 1, -1, -1)
        state = starts[sweep]
        out = [None] * count
        for r in order:
            state = rows[r] + decay(r) * (state - rows[r])
            out[r] = state
        ends.append(state)
        rows = out
    return rows, ends


def lat_states_kernel(row_count, groups, variables, x, decay, states, vert, out, sums):
    ct = pl.program_id(0)
    per_group = states.shape[0] // groups
    for o in range(groups // 8):
        rows = [x[pl.ds(o * 8 * row_count + r, 8, stride=row_count), :] for r in range(row_count)]
        starts = [
            states[pl.ds(o * 8 * per_group + k * (per_group // 4) + ct, 8, stride=per_group), :]
            for k in range(4)
        ]
        rows, _ = lat_sweeps(
            rows, lambda r: decay[r * groups + o * 8 : r * groups + o * 8 + 8, :], starts
        )
        for r in range(row_count):
            out[pl.ds(o * 8 * row_count + r, 8, stride=row_count), :] = rows[r]
    zero = jnp.zeros((8, LANE), f32)
    levels = groups // variables
    for var in range(variables):
        for t in range(row_count // 8):
            rows = []
            for lev in range(levels):
                base = (lev * variables + var) * row_count + t * 8
                rows.append(out[base : base + 8, :])
            _, ends = level_sweeps(rows, lambda lev: vert[lev * variables + var], [zero, zero])
            for k in range(2):
                sums[var, 0, k, 0, t * 8 : t * 8 + 8, :] = ends[k]


def lat_states(x, decay, states, vert, row_count, groups, variables):
    rows, columns = x.shape
    tiles = columns // LANE
    half = tiles // 2
    block = pl.BlockSpec((rows, LANE), lambda i: (0, i))
    return pl.pallas_call(
        functools.partial(lat_states_kernel, row_count, groups, variables),
        grid=(tiles,),
        out_shape=(
            jax.ShapeDtypeStruct(x.shape, f32),
            jax.ShapeDtypeStruct((variables, 2, 2, half, row_count, LANE), f32),
        ),
        in_specs=[
            block,
            pl.BlockSpec((rows, LANE), lambda i: (0, 0)),
            pl.BlockSpec(states.shape, lambda i: (0, 0)),
            pl.BlockSpec(memory_space=pltpu.SMEM),
        ],
        out_specs=(
            block,
            pl.BlockSpec(
                (variables, 1, 2, 1, row_count, LANE),
                lambda i: (0, i // half, 0, i % half, 0, 0),
            ),
        ),
        compiler_params=vmem(32),
        cost_estimate=cost(0, 12 << 20),
        name="lat_states",
    )(x, decay, states, vert)


def level_hub_kernel(coef, sums, states):
    bands = sums.shape[0]
    depth = sums.shape[2]
    for t in range(depth // 8):
        at = slice(t * 8, t * 8 + 8)
        state = jnp.zeros((8, LANE), f32)
        entering = []
        for b in range(bands):
            entering.append(state)
            states[b, 0, at, :] = state
            state = coef[0, b] * state + sums[b, 0, at, :]
        state = jnp.zeros((8, LANE), f32)
        for b in range(bands - 1, -1, -1):
            states[b, 1, at, :] = state
            state = coef[0, b] * state + (sums[b, 1, at, :] + coef[1, b] * entering[b])


def level_hub(coef, sums):
    return pl.pallas_call(
        level_hub_kernel,
        out_shape=jax.ShapeDtypeStruct(sums.shape, f32),
        in_specs=[pl.BlockSpec(memory_space=pltpu.SMEM), pl.BlockSpec(memory_space=pltpu.VMEM)],
        out_specs=pl.BlockSpec(memory_space=pltpu.VMEM),
        compiler_params=vmem(16),
        cost_estimate=cost(0, 3 << 20),
        name="level_hub",
    )(coef, sums)


def level_states_kernel(row_count, groups, variables, x, vert, states, out):
    levels = groups // variables
    for var in range(variables):
        for t in range(row_count // 8):
            spots = [
                slice((lev * variables + var) * row_count + t * 8, (lev * variables + var) * row_count + t * 8 + 8)
                for lev in range(levels)
            ]
            rows = [x[spot, :] for spot in spots]
            starts = [states[var, 0, k, 0, t * 8 : t * 8 + 8, :] for k in range(2)]
            rows, _ = level_sweeps(rows, lambda lev: vert[lev * variables + var], starts)
            for lev in range(levels):
                out[spots[lev], :] = rows[lev]


def level_states(x, vert, states, row_count, groups, variables):
    rows, columns = x.shape
    tiles = columns // LANE
    half = tiles // 2
    block = pl.BlockSpec((rows, LANE), lambda i: (0, i))
    return pl.pallas_call(
        functools.partial(level_states_kernel, row_count, groups, variables),
        grid=(tiles,),
        out_shape=jax.ShapeDtypeStruct(x.shape, f32),
        in_specs=[
            block,
            pl.BlockSpec(memory_space=pltpu.SMEM),
            pl.BlockSpec(
                (variables, 1, 2, 1, row_count, LANE),
                lambda i: (0, i // half, 0, i % half, 0, 0),
            ),
        ],
        out_specs=block,
        compiler_params=vmem(32),
        cost_estimate=cost(0, 11 << 20),
        name="level_states",
    )(x, vert, states)


def level_coefficients(decays):
    levels = decays.shape[1]
    state, down = jnp.ones_like(decays[:, 0]), []
    for r in range(levels):
        state = decays[:, r] * state
        down.append(state)
    full = state
    state = jnp.zeros_like(full)
    for r in range(levels - 1, -1, -1):
        state = down[r] + decays[:, r] * (state - down[r])
    return jnp.stack([full, state])


def per_device(background, obs_columns, obs_owner, obs_cell, lat_length, lon_length, vert_length):
    level_count, var_count, row_count, lon_count = background.shape
    sub_count = lax.axis_size("sub")
    band_count = lax.axis_size("band")
    sub_index = lax.axis_index("sub")
    band_index = lax.axis_index("band")
    groups = level_count * var_count
    tiles = lon_count // LANE
    tile_field = background.reshape(groups * row_count, lon_count)
    obs_values = obs_columns.reshape(groups, -1)
    owners = obs_owner[:, 0]
    capacity = 2 * owners.shape[0] // sub_count

    slots = route_slots(owners, sub_count, capacity)
    row, column = obs_cell // lon_count, obs_cell % lon_count
    place = ((row // 4) * lon_count + column) * 4 + row % 4
    packed, sent = pack(slots, place, obs_values, sub_count * capacity)
    got = lax.all_to_all(
        packed.reshape(sub_count, capacity // 4, LANE), "sub", 0, 0, tiled=True
    )
    places = lax.all_to_all(sent.reshape(sub_count, capacity), "sub", 0, 0, tiled=True)

    all_vert = lax.all_gather(vert_length, "band")
    vert_decay = jnp.exp(-1.0 / vert_length).reshape(groups)
    own_var = band_index // 2
    hub_vert = lax.dynamic_index_in_dim(jnp.exp(-1.0 / all_vert), own_var, 2, False)
    coef = level_coefficients(hub_vert)

    lat_all = jnp.exp(-1.0 / lat_length).reshape(groups, sub_count, row_count)
    own_lat = lax.dynamic_index_in_dim(lat_all, sub_index, 1, False)
    decay = jnp.broadcast_to(own_lat.T.reshape(row_count * groups, 1), (row_count * groups, LANE))
    hub_lat = lax.dynamic_index_in_dim(lat_all, sub_index, 0, False)
    hub_lat = jnp.pad(hub_lat.T, ((0, 0), (0, LANE - sub_count)))

    lengths = lon_length.reshape(groups)
    weights = lon_weights(lengths, lon_count)
    own_weights = [lax.dynamic_slice_in_dim(w, sub_index, 1, 0) for w in weights]

    field = deposit(places.reshape(-1), got.reshape(-1, LANE), groups * row_count * lon_count // LANE)
    forced, moments = lat_moments(field, tile_field, decay, row_count, groups)
    moments = lax.all_to_all(
        moments.reshape(sub_count, 4 * tiles, LANE), "sub", 0, 0, tiled=True
    )
    smooth = lon_filter(forced, weights, row_count)
    states = hub(hub_lat, moments.reshape(-1, LANE), own_weights)
    states = lax.all_to_all(states.reshape(sub_count, 4 * tiles, LANE), "sub", 0, 0, tiled=True)
    smooth, sums = lat_states(
        smooth, decay, states.reshape(-1, LANE), vert_decay, row_count, groups, var_count
    )
    depth = tiles // 2 * row_count
    sums = lax.all_to_all(
        sums.reshape(band_count, 2, depth, LANE), "band", 0, 0, tiled=True
    )
    entering = level_hub(coef, sums)
    entering = lax.all_to_all(entering, "band", 0, 0, tiled=True)
    result = level_states(
        smooth,
        vert_decay,
        entering.reshape(var_count, 2, 2, tiles // 2, row_count, LANE),
        row_count,
        groups,
        var_count,
    )
    return result.reshape(background.shape)


def solution(mesh):
    placed = (
        P("band", None, "sub", None),
        P("band", None, "sub"),
        P("sub", None),
        P("sub"),
        P("band", None, None),
        P("band", None),
        P("band", None),
    )
    return jax.shard_map(
        per_device,
        mesh=mesh,
        in_specs=placed,
        out_specs=P("band", None, "sub", None),
        check_vma=False,
    )
```

```python
import functools

import jax
import jax.numpy as jnp
from jax import lax
from jax.experimental import pallas as pl
from jax.experimental.pallas import tpu as pltpu
from jax.sharding import PartitionSpec as P

LANE = 128
f32 = jnp.float32
bf16 = jnp.bfloat16


def vmem(mib):
    return pltpu.CompilerParams(vmem_limit_bytes=mib << 20)


def cost(flops, moved):
    return pl.CostEstimate(flops=flops, bytes_accessed=moved, transcendentals=0)


def route_slots(owners, sub_count, capacity):
    count = owners.shape[0]
    block = 128
    owner_block = owners.reshape(count // block, block)
    match = (owner_block[:, :, None] == jnp.arange(sub_count, dtype=jnp.int32)).astype(bf16)
    position = jnp.arange(block)
    lower = (position[:, None] > position[None, :]).astype(bf16)
    ahead = jnp.einsum("ij,bjo->bio", lower, match, preferred_element_type=f32)
    totals = jnp.sum(match.astype(f32), axis=1)
    base = jnp.cumsum(totals, axis=0) - totals
    rank = jnp.sum((ahead + base[:, None, :]) * match.astype(f32), axis=2)
    return owners * capacity + rank.reshape(count).astype(jnp.int32)


def pack_kernel(slots, cells, zeros, values, packed, sent_cells, rows, big, sem):
    clear = pltpu.make_async_copy(zeros, sent_cells, sem)
    clear.start()
    count = values.shape[1]
    total = big.shape[0]

    @pl.loop(0, total // 64)
    def _(i):
        big[pl.ds(pl.multiple_of(i * 64, 64), 64), :] = jnp.zeros((64, LANE), f32)

    for j in range(count // LANE):
        part = values[:, j * LANE : (j + 1) * LANE]
        rows[j * LANE : (j + 1) * LANE, :] = jnp.concatenate([part] * 4, axis=0).T
    clear.wait()

    step = 16

    @pl.loop(0, count // step)
    def _(i):
        for u in range(step):
            j = i * step + u
            slot = slots[j]
            big[pl.ds(slot, 1), :] = rows[pl.ds(j, 1), :]
            sent_cells[slot] = cells[j]

    quarter = lax.broadcasted_iota(jnp.int32, (64, LANE), 1) // 32

    @pl.loop(0, total // 256)
    def _(d):
        start = pl.multiple_of(d * 256, 256)
        out = big[pl.ds(start, 64), :]
        for k in range(1, 4):
            out = jnp.where(quarter == k, big[pl.ds(start + 64 * k, 64), :], out)
        packed[pl.ds(pl.multiple_of(d * 64, 64), 64), :] = out


def pack(slots, cells, values, total):
    count = values.shape[1]
    smem = pl.BlockSpec(memory_space=pltpu.SMEM)
    return pl.pallas_call(
        pack_kernel,
        out_shape=(
            jax.ShapeDtypeStruct((total // 4, LANE), f32),
            jax.ShapeDtypeStruct((total,), jnp.int32),
        ),
        in_specs=[smem, smem, pl.BlockSpec(memory_space=pl.ANY), pl.BlockSpec(memory_space=pltpu.VMEM)],
        out_specs=(pl.BlockSpec(memory_space=pltpu.VMEM), smem),
        scratch_shapes=[
            pltpu.VMEM((count, LANE), f32),
            pltpu.VMEM((total, LANE), f32),
            pltpu.SemaphoreType.DMA,
        ],
        compiler_params=vmem(60),
        cost_estimate=cost(0, 4 << 20),
        name="pack",
    )(slots, cells, jnp.zeros((total,), jnp.int32), values)


def lat_sweeps(rows, decay, starts):
    count = len(rows)
    ends = []
    for sweep in range(4):
        order = range(count) if sweep % 2 == 0 else range(count - 1, -1, -1)
        state = starts[sweep]
        out = [None] * count
        for r in order:
            state = rows[r] + decay(r) * (state - rows[r])
            out[r] = state
        ends.append(state)
        rows = out
    return rows, ends


CHAINS = 8


def forced_kernel(row_count, groups, places, got, quarters, background, decay, forced, moments, spread, *chains):
    step_id = pl.program_id(0)
    total = spread.shape[0]
    depth = chains[0].shape[0]
    sources = got.shape[0]

    @pl.when(step_id == 0)
    def _():
        @pl.loop(0, depth // 64)
        def _(i):
            at = pl.ds(pl.multiple_of(i * 64, 64), 64)
            for chain in chains:
                chain[at, :] = jnp.zeros((64, LANE), f32)

        lane = lax.broadcasted_iota(jnp.int32, (8, LANE), 1) // 32
        pick = (lane == lax.broadcasted_iota(jnp.int32, (8, LANE), 0)).astype(bf16)
        quarter = lax.broadcasted_iota(jnp.int32, (64, LANE), 1) // 32
        wanted = quarter.astype(f32)

        def turns(x):
            return [x] + [pltpu.roll(x, 32 * k, 1) for k in range(1, 4)]

        def repeat(turned, k):
            out = turned[(3 - k) % 4]
            for q in range(3):
                out = jnp.where(quarter == q, turned[(q - k) % 4], out)
            return out

        @pl.loop(0, sources)
        def _(d):
            part = turns(got[d, :64, :])
            mark = turns(
                lax.dot_general(
                    quarters[d].astype(bf16), pick, (((0,), (0,)), ((), ())), preferred_element_type=f32
                )
            )
            for k in range(4):
                one = jnp.where(repeat(mark, k) == wanted, repeat(part, k), 0.0)
                spread[pl.ds(pl.multiple_of(d * 256 + k * 64, 64), 64), :] = one

        step = 4

        @pl.loop(0, total // (CHAINS * step))
        def _(i):
            for u in range(step):
                spots = [(i * step + u) * CHAINS + c for c in range(CHAINS)]
                where = [pl.ds(places[j], 1) for j in spots]
                adds = [spread[pl.ds(j, 1), :] for j in spots]
                olds = [chains[c][where[c], :] for c in range(CHAINS)]
                for c in range(CHAINS):
                    chains[c][where[c], :] = olds[c] + adds[c]

    @pl.when(step_id > 0)
    def _():
        ct = step_id - 1
        columns = depth // (row_count // 4)
        for rr in range(row_count // 4):
            at = pl.ds(pl.multiple_of(rr * columns + ct * LANE, LANE), LANE)
            parts = [chain[at, :] for chain in chains]
            while len(parts) > 1:
                parts = [a + b for a, b in zip(parts[::2], parts[1::2])]
            turned = parts[0].T
            for q in range(4):
                for o in range(groups // 8):
                    at = pl.ds(o * 8 * row_count + rr * 4 + q, 8, stride=row_count)
                    first = q * groups + o * 8
                    forced[at, :] = background[at, :] + turned[first : first + 8, :]
        zero = jnp.zeros((8, LANE), f32)
        per_group = moments.shape[0] // groups
        for o in range(groups // 8):
            rows = [
                forced[pl.ds(o * 8 * row_count + r, 8, stride=row_count), :]
                for r in range(row_count)
            ]
            _, ends = lat_sweeps(
                rows, lambda r: decay[r * groups + o * 8 : r * groups + o * 8 + 8, :], [zero] * 4
            )
            for k in range(4):
                start = o * 8 * per_group + k * (per_group // 4) + ct
                moments[pl.ds(start, 8, stride=per_group), :] = ends[k]


def force(places, got, quarters, background, decay, row_count, groups):
    rows, columns = background.shape
    tiles = columns // LANE
    total = places.shape[0]
    depth = rows * columns // LANE
    block = pl.BlockSpec((rows, LANE), lambda i: (0, jnp.maximum(i - 1, 0)))
    return pl.pallas_call(
        functools.partial(forced_kernel, row_count, groups),
        grid=(tiles + 1,),
        out_shape=(
            jax.ShapeDtypeStruct(background.shape, f32),
            jax.ShapeDtypeStruct((groups * 4 * tiles, LANE), f32),
        ),
        in_specs=[
            pl.BlockSpec(memory_space=pltpu.SMEM),
            pl.BlockSpec(got.shape, lambda i: (0, 0, 0), pipeline_mode=pl.Buffered(1)),
            pl.BlockSpec(quarters.shape, lambda i: (0, 0, 0), pipeline_mode=pl.Buffered(1)),
            block,
            pl.BlockSpec((rows, LANE), lambda i: (0, 0), pipeline_mode=pl.Buffered(1)),
        ],
        out_specs=(block, pl.BlockSpec((groups * 4 * tiles, LANE), lambda i: (0, 0))),
        scratch_shapes=[pltpu.VMEM((total, LANE), f32)] + [pltpu.VMEM((depth, LANE), f32)] * CHAINS,
        compiler_params=vmem(60),
        cost_estimate=cost(0, 16 << 20),
        name="force",
    )(places, got, quarters, background, decay)


def lon_weights(length, columns):
    blocks = columns // LANE
    length = length[:, None, None]
    kappa = jnp.tanh(0.5 / length)
    beta = kappa * kappa
    alpha = beta / jnp.tanh(1.0 / length)
    i = jnp.arange(LANE, dtype=f32)

    def power(n):
        return jnp.exp(-n / length)

    gap = jnp.abs(i[:, None] - i[None, :])[None]
    local = (alpha + beta * gap) * power(gap)
    up, down = i[None, :, None], (LANE - 1.0) - i[None, :, None]
    sums = jnp.concatenate(
        [power(down), down * power(down), power(up), up * power(up)], axis=2
    )
    sums = jnp.pad(sums, ((0, 0), (0, 0), (0, LANE - 4)))
    first = jnp.concatenate([local, sums], axis=2)
    index = jnp.arange(LANE)
    src, dst = index[:, None], index[None, :]
    source, target = src // 4, dst // 4
    backward = (src % 4) >= 2
    steps = jnp.where(backward, source - target - 1, target - source - 1) % blocks
    gap = (LANE * steps).astype(f32)[None]
    turn = power(float(columns))
    left = -jnp.expm1(-float(columns) / length)
    same = power(gap) / left
    cross = (gap + columns * turn / left) * same
    used = (source < blocks) & (target < blocks)
    mix = jnp.where((used & (src % 4 == dst % 4))[None], same, 0.0)
    mix = jnp.where((used & (src % 2 == 0) & (dst % 4 == src % 4 + 1))[None], cross, mix)
    near, far = i[None, None, :] + 1.0, LANE - i[None, None, :]
    back = jnp.concatenate(
        [
            (alpha + beta * near) * power(near),
            beta * power(near),
            (alpha + beta * far) * power(far),
            beta * power(far),
        ],
        axis=1,
    )
    back = jnp.pad(back, ((0, 0), (0, LANE - 4), (0, 0)))
    return thirds(first), thirds(mix), thirds(back)


def thirds(w):
    high = lax.reduce_precision(w, 8, 7)
    low = (w - high).astype(bf16)
    high = high.astype(bf16)
    return jnp.concatenate([high, high, low], axis=1)


def dot3(x, w):
    high = x.astype(bf16)
    low = (x - high.astype(f32)).astype(bf16)
    return jnp.dot(jnp.concatenate([high, low, high], axis=1), w, preferred_element_type=f32)


def lon_apply(x, first, mix, back):
    count, columns = x.shape
    blocks = columns // LANE
    stacked = jnp.concatenate([x[:, b * LANE : (b + 1) * LANE] for b in range(blocks)], axis=0)
    both = dot3(stacked, first)
    local, sums = both[:, :LANE], both[:, LANE:]
    line = sums[:count]
    for b in range(1, blocks):
        line = line + pltpu.roll(sums[b * count : (b + 1) * count], 4 * b, 1)
    states = dot3(line, mix)
    spread = jnp.concatenate(
        [states] + [pltpu.roll(states, LANE - 4 * b, 1) for b in range(1, blocks)], axis=0
    )
    out = local + dot3(spread, back)
    return jnp.concatenate([out[b * count : (b + 1) * count] for b in range(blocks)], axis=1)


def lon_kernel(x, first, mix, back, out):
    count = x.shape[0] // first.shape[0]
    for g in range(first.shape[0]):
        at = slice(g * count, (g + 1) * count)
        out[at, :] = lon_apply(x[at, :], first[g], mix[g], back[g])


def lon_filter(x, weights, row_count, half):
    rows, columns = x.shape
    per_step = 4
    steps = rows // row_count // per_step // 2
    block = pl.BlockSpec((per_step * row_count, columns), lambda i: (i + half * steps, 0))
    return pl.pallas_call(
        lon_kernel,
        grid=(steps,),
        out_shape=jax.ShapeDtypeStruct((rows // 2, columns), f32),
        in_specs=[block]
        + [
            pl.BlockSpec((per_step,) + w.shape[1:], lambda i: (i + half * steps, 0, 0))
            for w in weights
        ],
        out_specs=pl.BlockSpec((per_step * row_count, columns), lambda i: (i, 0)),
        compiler_params=vmem(60),
        cost_estimate=cost(3 * rows * columns * 3 * LANE, 30 << 20),
        name="lon",
    )(x, *weights)


def hub_kernel(decay, moments, first, mix, back, states, work):
    blocks = 32
    depth = moments.shape[0] // blocks
    tiles = depth // 4
    count = decay.shape[0]
    coef = [decay[r : r + 1, :] for r in range(count)]

    def forward(rows):
        state, out = jnp.zeros((1, LANE), f32), []
        for r in range(count):
            state = rows[r] + coef[r] * (state - rows[r])
            out.append(state)
        return out

    def backward(rows):
        state, out = jnp.zeros((1, LANE), f32), [None] * count
        for r in range(count - 1, -1, -1):
            state = rows[r] + coef[r] * (state - rows[r])
            out[r] = state
        return out

    state, down = jnp.ones((1, LANE), f32), []
    for r in range(count):
        state = coef[r] * state
        down.append(state)
    full = state
    state, up = jnp.ones((1, LANE), f32), [None] * count
    for r in range(count - 1, -1, -1):
        state = coef[r] * state
        up[r] = state
    bp = backward(down)
    fbp = forward(bp)
    bfbp = backward(fbp)
    fq = forward(up)
    bfq = backward(fq)
    t21, t31, t41, t32, t42 = bp[0], fbp[-1], bfbp[0], fq[-1], bfq[0]

    def at(table, d):
        return jnp.broadcast_to(table[:, d : d + 1], (tiles, LANE))

    def moment(d, k):
        return moments[d * depth + k * tiles : d * depth + (k + 1) * tiles, :]

    def put(d, k, value):
        for t in range(tiles):
            work[k * blocks + d, t * LANE : (t + 1) * LANE] = value[t]

    zero = jnp.zeros((tiles, LANE), f32)
    s = [[None] * blocks for _ in range(4)]
    carry = zero
    for d in range(blocks):
        s[0][d] = carry
        carry = at(full, d) * carry + moment(d, 0)
    carry = zero
    for d in range(blocks - 1, -1, -1):
        s[1][d] = carry
        carry = at(full, d) * carry + (moment(d, 1) + at(t21, d) * s[0][d])
    carry = zero
    for d in range(blocks):
        s[2][d] = carry
        carry = at(full, d) * carry + (
            moment(d, 2) + at(t31, d) * s[0][d] + at(t32, d) * s[1][d]
        )
    carry = zero
    for d in range(blocks - 1, -1, -1):
        s[3][d] = carry
        carry = at(full, d) * carry + (
            moment(d, 3) + at(t41, d) * s[0][d] + at(t42, d) * s[1][d] + at(t21, d) * s[2][d]
        )
    for k in range(4):
        for d in range(blocks):
            put(d, k, s[k][d])
    done = lon_apply(work[...], first[0], mix[0], back[0])
    for k in range(4):
        for d in range(blocks):
            row = done[k * blocks + d : k * blocks + d + 1]
            for t in range(tiles):
                base = d * depth + k * tiles + t
                states[base : base + 1, :] = row[:, t * LANE : (t + 1) * LANE]


def hub(decay, moments, weights):
    depth = moments.shape[0] // 32
    return pl.pallas_call(
        hub_kernel,
        out_shape=jax.ShapeDtypeStruct(moments.shape, f32),
        in_specs=[pl.BlockSpec(memory_space=pltpu.VMEM)] * 5,
        out_specs=pl.BlockSpec(memory_space=pltpu.VMEM),
        scratch_shapes=[pltpu.VMEM((128, depth // 4 * LANE), f32)],
        compiler_params=vmem(60),
        cost_estimate=cost(0, 4 << 20),
        name="hub",
    )(decay, moments, *weights)


def level_sweeps(rows, decay, starts):
    count = len(rows)
    ends = []
    for sweep in range(2):
        order = range(count) if sweep == 0 else range(count - 1, -1, -1)
        state = starts[sweep]
        out = [None] * count
        for r in order:
            state = rows[r] + decay(r) * (state - rows[r])
            out[r] = state
        ends.append(state)
        rows = out
    return rows, ends


def lat_states_kernel(row_count, groups, variables, low, high, decay, states, vert, coef, out, sums):
    ct = pl.program_id(0)
    per_group = states.shape[0] // groups
    half = low.shape[0]
    for o in range(groups // 8):
        base = o * 8 * row_count
        x, first = (low, base) if base < half else (high, base - half)
        rows = [x[pl.ds(first + r, 8, stride=row_count), :] for r in range(row_count)]
        starts = [
            states[pl.ds(o * 8 * per_group + k * (per_group // 4) + ct, 8, stride=per_group), :]
            for k in range(4)
        ]
        rows, _ = lat_sweeps(
            rows, lambda r: decay[r * groups + o * 8 : r * groups + o * 8 + 8, :], starts
        )
        for r in range(row_count):
            out[pl.ds(base + r, 8, stride=row_count), :] = rows[r]
    zero = jnp.zeros((8, LANE), f32)
    levels = groups // variables
    halves = pl.num_programs(0) // 2
    depth = halves * row_count
    size = sums.shape[0] // (2 * variables)
    for var in range(variables):
        for t in range(row_count // 8):
            rows = []
            for lev in range(levels):
                base = (lev * variables + var) * row_count + t * 8
                rows.append(out[base : base + 8, :])
            _, ends = level_sweeps(rows, lambda lev: vert[lev * variables + var], [zero, zero])
            for k in range(2):
                start = (var * 2 + ct // halves) * size + k * depth + (ct % halves) * row_count + t * 8
                sums[pl.ds(pl.multiple_of(start, 8), 8), :] = ends[k]

    @pl.when(ct == 0)
    def _():
        for target in range(2 * variables):
            start = target * size + 2 * depth
            sums[start : start + 8, :] = coef[target // 2]


def lat_states(low, high, decay, states, vert, coef, row_count, groups, variables):
    rows, columns = 2 * low.shape[0], low.shape[1]
    tiles = columns // LANE
    part = pl.BlockSpec((rows // 2, LANE), lambda i: (0, i))
    block = pl.BlockSpec((rows, LANE), lambda i: (0, i))
    size = 2 * variables * (tiles * row_count + 8)
    return pl.pallas_call(
        functools.partial(lat_states_kernel, row_count, groups, variables),
        grid=(tiles,),
        out_shape=(
            jax.ShapeDtypeStruct((rows, columns), f32),
            jax.ShapeDtypeStruct((size, LANE), f32),
        ),
        in_specs=[
            part,
            part,
            pl.BlockSpec((rows, LANE), lambda i: (0, 0)),
            pl.BlockSpec(states.shape, lambda i: (0, 0)),
            pl.BlockSpec(memory_space=pltpu.SMEM),
            pl.BlockSpec(coef.shape, lambda i: (0, 0, 0)),
        ],
        out_specs=(block, pl.BlockSpec((size, LANE), lambda i: (0, 0))),
        compiler_params=vmem(60),
        cost_estimate=cost(0, 12 << 20),
        name="lat_states",
    )(low, high, decay, states, vert, coef)


def level_hub_kernel(sums, states):
    bands = sums.shape[0]
    depth = states.shape[2]
    full = [jnp.broadcast_to(sums[b, 2 * depth : 2 * depth + 1, :], (8, LANE)) for b in range(bands)]
    both = [
        jnp.broadcast_to(sums[b, 2 * depth + 1 : 2 * depth + 2, :], (8, LANE)) for b in range(bands)
    ]
    for t in range(depth // 8):
        at = slice(t * 8, t * 8 + 8)
        later = slice(depth + t * 8, depth + t * 8 + 8)
        state = jnp.zeros((8, LANE), f32)
        entering = []
        for b in range(bands):
            entering.append(state)
            states[b, 0, at, :] = state
            state = full[b] * state + sums[b, at, :]
        state = jnp.zeros((8, LANE), f32)
        for b in range(bands - 1, -1, -1):
            states[b, 1, at, :] = state
            state = full[b] * state + (sums[b, later, :] + both[b] * entering[b])


def level_hub(sums):
    bands, size, _ = sums.shape
    return pl.pallas_call(
        level_hub_kernel,
        out_shape=jax.ShapeDtypeStruct((bands, 2, (size - 8) // 2, LANE), f32),
        in_specs=[pl.BlockSpec(memory_space=pltpu.VMEM)],
        out_specs=pl.BlockSpec(memory_space=pltpu.VMEM),
        compiler_params=vmem(60),
        cost_estimate=cost(0, 3 << 20),
        name="level_hub",
    )(sums)


def level_states_kernel(row_count, groups, variables, x, vert, states, out):
    levels = groups // variables
    for var in range(variables):
        for t in range(row_count // 8):
            spots = [
                slice((lev * variables + var) * row_count + t * 8, (lev * variables + var) * row_count + t * 8 + 8)
                for lev in range(levels)
            ]
            rows = [x[spot, :] for spot in spots]
            starts = [states[var, 0, k, 0, t * 8 : t * 8 + 8, :] for k in range(2)]
            rows, _ = level_sweeps(rows, lambda lev: vert[lev * variables + var], starts)
            for lev in range(levels):
                out[spots[lev], :] = rows[lev]


def level_states(x, vert, states, row_count, groups, variables):
    rows, columns = x.shape
    tiles = columns // LANE
    half = tiles // 2
    block = pl.BlockSpec((rows, LANE), lambda i: (0, i))
    return pl.pallas_call(
        functools.partial(level_states_kernel, row_count, groups, variables),
        grid=(tiles,),
        out_shape=jax.ShapeDtypeStruct(x.shape, f32),
        in_specs=[
            block,
            pl.BlockSpec(memory_space=pltpu.SMEM),
            pl.BlockSpec(
                (variables, 1, 2, 1, row_count, LANE),
                lambda i: (0, i // half, 0, i % half, 0, 0),
            ),
        ],
        out_specs=block,
        compiler_params=vmem(60),
        cost_estimate=cost(0, 11 << 20),
        name="level_states",
    )(x, vert, states)


def level_coefficients(decays):
    levels = decays.shape[0]
    state, down = jnp.ones_like(decays[0]), []
    for r in range(levels):
        state = decays[r] * state
        down.append(state)
    full = state
    state = jnp.zeros_like(full)
    for r in range(levels - 1, -1, -1):
        state = down[r] + decays[r] * (state - down[r])
    both = jnp.stack([full, state], axis=1)
    both = jnp.pad(both, ((0, 0), (0, 6)))
    return jnp.broadcast_to(both[:, :, None], both.shape + (LANE,))


def per_device(background, obs_columns, obs_owner, obs_cell, lat_length, lon_length, vert_length):
    level_count, var_count, row_count, lon_count = background.shape
    sub_count = lax.axis_size("sub")
    band_count = lax.axis_size("band")
    sub_index = lax.axis_index("sub")
    groups = level_count * var_count
    tiles = lon_count // LANE
    tile_field = background.reshape(groups * row_count, lon_count)
    obs_values = obs_columns.reshape(groups, -1)
    owners = obs_owner[:, 0]
    capacity = 2 * owners.shape[0] // sub_count

    slots = route_slots(owners, sub_count, capacity)
    row, column = obs_cell // lon_count, obs_cell % lon_count
    place = ((row // 4) * lon_count + column) * 4 + row % 4
    packed, sent = pack(slots, place, obs_values, sub_count * capacity)
    lines = capacity // LANE
    message = jnp.concatenate(
        [
            packed.reshape(sub_count, capacity // 4, LANE),
            sent.astype(f32).reshape(sub_count, lines, LANE),
            jnp.zeros((sub_count, 8 - lines, LANE), f32),
        ],
        axis=1,
    )
    got = lax.all_to_all(message, "sub", 0, 0, tiled=True)

    vert_decay = jnp.exp(-1.0 / vert_length)
    coef = level_coefficients(vert_decay)
    vert_decay = vert_decay.reshape(groups)

    lat_all = jnp.exp(-1.0 / lat_length).reshape(groups, sub_count, row_count)
    own_lat = lax.dynamic_index_in_dim(lat_all, sub_index, 1, False)
    decay = jnp.broadcast_to(own_lat.T.reshape(row_count * groups, 1), (row_count * groups, LANE))
    hub_lat = lax.dynamic_index_in_dim(lat_all, sub_index, 0, False)
    hub_lat = jnp.pad(hub_lat.T, ((0, 0), (0, LANE - sub_count)))

    lengths = lon_length.reshape(groups)
    weights = lon_weights(lengths, lon_count)
    own_weights = [lax.dynamic_slice_in_dim(w, sub_index, 1, 0) for w in weights]

    places = got[:, capacity // 4 : capacity // 4 + lines, :].reshape(-1).astype(jnp.int32)
    quarters = (places & 3).astype(f32).reshape(sub_count, 4, capacity // 4)
    quarters = jnp.pad(quarters, ((0, 0), (0, 4), (0, 0)))
    forced, moments = force(places >> 2, got, quarters, tile_field, decay, row_count, groups)
    moments = lax.all_to_all(
        moments.reshape(sub_count, 4 * tiles, LANE), "sub", 0, 0, tiled=True
    )
    low = lon_filter(forced, weights, row_count, 0)
    moments, low = lax.optimization_barrier((moments, low))
    states = hub(hub_lat, moments.reshape(-1, LANE), own_weights)
    states, forced = lax.optimization_barrier((states, forced))
    states = lax.all_to_all(states.reshape(sub_count, 4 * tiles, LANE), "sub", 0, 0, tiled=True)
    high = lon_filter(forced, weights, row_count, 1)
    smooth, sums = lat_states(
        low, high, decay, states.reshape(-1, LANE), vert_decay, coef, row_count, groups, var_count
    )
    sums = lax.all_to_all(
        sums.reshape(band_count, -1, LANE), "band", 0, 0, tiled=True
    )
    entering = lax.all_to_all(level_hub(sums), "band", 0, 0, tiled=True)
    result = level_states(
        smooth,
        vert_decay,
        entering.reshape(var_count, 2, 2, tiles // 2, row_count, LANE),
        row_count,
        groups,
        var_count,
    )
    return result.reshape(background.shape)


def solution(mesh):
    placed = (
        P("band", None, "sub", None),
        P("band", None, "sub"),
        P("sub", None),
        P("sub"),
        P("band", None, None),
        P("band", None),
        P("band", None),
    )
    return jax.shard_map(
        per_device,
        mesh=mesh,
        in_specs=placed,
        out_specs=P("band", None, "sub", None),
        check_vma=False,
    )
```

```python
import functools

import jax
import jax.numpy as jnp
from jax import lax
from jax.experimental import pallas as pl
from jax.experimental.pallas import tpu as pltpu
from jax.sharding import PartitionSpec as P

LANE = 128
f32 = jnp.float32
bf16 = jnp.bfloat16


def vmem(mib):
    return pltpu.CompilerParams(vmem_limit_bytes=mib << 20)


def cost(flops, moved):
    return pl.CostEstimate(flops=flops, bytes_accessed=moved, transcendentals=0)


def route_ranks(owners, sub_count):
    count = owners.shape[0]
    block = 128
    owner_block = owners.reshape(count // block, block)
    match = (owner_block[:, :, None] == jnp.arange(sub_count, dtype=jnp.int32)).astype(bf16)
    position = jnp.arange(block)
    lower = (position[:, None] > position[None, :]).astype(bf16)
    ahead = jnp.einsum("ij,bjo->bio", lower, match, preferred_element_type=f32)
    totals = jnp.sum(match.astype(f32), axis=1)
    base = jnp.cumsum(totals, axis=0) - totals
    rank = jnp.sum((ahead + base[:, None, :]) * match.astype(f32), axis=2)
    return rank.reshape(count).astype(jnp.int32)


def pack_kernel(slots, table, values, packed, rows, big):
    count = values.shape[1]
    total = big.shape[0]
    targets = total // 256
    size = packed.shape[0] // targets

    @pl.loop(0, total // 64)
    def _(i):
        big[pl.ds(pl.multiple_of(i * 64, 64), 64), :] = jnp.zeros((64, LANE), f32)

    for j in range(count // LANE):
        part = values[:, j * LANE : (j + 1) * LANE]
        rows[j * LANE : (j + 1) * LANE, :] = jnp.concatenate([part] * 4, axis=0).T

    owner, rank, place = table[0:1, :], table[1:2, :], table[2:3, :]
    mine = owner == lax.broadcasted_iota(jnp.int32, (targets, count), 0)
    spot = (rank == lax.broadcasted_iota(jnp.int32, (256, count), 0)).astype(f32).astype(bf16)

    def put(half):
        left = jnp.where(mine, half, 0).astype(f32).astype(bf16)
        return lax.dot_general(
            left, spot, (((1,), (1,)), ((), ())), preferred_element_type=f32
        )

    cells = put(lax.shift_right_logical(place, 8)) * 256.0 + put(place & 255)
    for half in range(2):
        packed[pl.ds(64 + half, targets, stride=size), :] = cells[:, half * LANE : (half + 1) * LANE]
    for extra in range(66, size):
        packed[pl.ds(extra, targets, stride=size), :] = jnp.zeros((targets, LANE), f32)

    step = 16

    @pl.loop(0, count // step)
    def _(i):
        for u in range(step):
            j = i * step + u
            big[pl.ds(slots[j], 1), :] = rows[pl.ds(j, 1), :]

    quarter = lax.broadcasted_iota(jnp.int32, (64, LANE), 1) // 32

    @pl.loop(0, targets)
    def _(d):
        start = pl.multiple_of(d * 256, 256)
        out = big[pl.ds(start, 64), :]
        for k in range(1, 4):
            out = jnp.where(quarter == k, big[pl.ds(start + 64 * k, 64), :], out)
        packed[pl.ds(pl.multiple_of(d * size, 8), 64), :] = out


def pack(slots, table, values, targets):
    count = values.shape[1]
    total = targets * 256
    whole = pl.BlockSpec(memory_space=pltpu.VMEM)
    return pl.pallas_call(
        pack_kernel,
        out_shape=jax.ShapeDtypeStruct((targets * 72, LANE), f32),
        in_specs=[pl.BlockSpec(memory_space=pltpu.SMEM), whole, whole],
        out_specs=whole,
        scratch_shapes=[pltpu.VMEM((count, LANE), f32), pltpu.VMEM((total, LANE), f32)],
        compiler_params=vmem(60),
        cost_estimate=cost(0, 4 << 20),
        name="pack",
    )(slots, table, values)


def lat_sweeps(rows, decay, starts):
    count = len(rows)
    ends = []
    for sweep in range(4):
        order = range(count) if sweep % 2 == 0 else range(count - 1, -1, -1)
        state = starts[sweep]
        out = [None] * count
        for r in order:
            state = rows[r] + decay(r) * (state - rows[r])
            out[r] = state
        ends.append(state)
        rows = out
    return rows, ends


CHAINS = 8


def forced_kernel(row_count, groups, places, got, quarters, background, decay, forced, moments, spread, *chains):
    step_id = pl.program_id(0)
    total = spread.shape[0]
    depth = chains[0].shape[0]
    sources = got.shape[0]

    @pl.when(step_id == 0)
    def _():
        @pl.loop(0, depth // 64)
        def _(i):
            at = pl.ds(pl.multiple_of(i * 64, 64), 64)
            for chain in chains:
                chain[at, :] = jnp.zeros((64, LANE), f32)

        lane = lax.broadcasted_iota(jnp.int32, (8, LANE), 1) // 32
        pick = (lane == lax.broadcasted_iota(jnp.int32, (8, LANE), 0)).astype(bf16)
        quarter = lax.broadcasted_iota(jnp.int32, (64, LANE), 1) // 32
        wanted = quarter.astype(f32)

        def turns(x):
            return [x] + [pltpu.roll(x, 32 * k, 1) for k in range(1, 4)]

        def repeat(turned, k):
            out = turned[(3 - k) % 4]
            for q in range(3):
                out = jnp.where(quarter == q, turned[(q - k) % 4], out)
            return out

        @pl.loop(0, sources)
        def _(d):
            part = turns(got[d, :64, :])
            mark = turns(
                lax.dot_general(
                    quarters[d].astype(bf16), pick, (((0,), (0,)), ((), ())), preferred_element_type=f32
                )
            )
            for k in range(4):
                one = jnp.where(repeat(mark, k) == wanted, repeat(part, k), 0.0)
                spread[pl.ds(pl.multiple_of(d * 256 + k * 64, 64), 64), :] = one

        step = 4

        @pl.loop(0, total // (CHAINS * step))
        def _(i):
            for u in range(step):
                spots = [(i * step + u) * CHAINS + c for c in range(CHAINS)]
                where = [pl.ds(places[j], 1) for j in spots]
                adds = [spread[pl.ds(j, 1), :] for j in spots]
                olds = [chains[c][where[c], :] for c in range(CHAINS)]
                for c in range(CHAINS):
                    chains[c][where[c], :] = olds[c] + adds[c]

    @pl.when(step_id > 0)
    def _():
        ct = step_id - 1
        columns = depth // (row_count // 4)
        for rr in range(row_count // 4):
            at = pl.ds(pl.multiple_of(rr * columns + ct * LANE, LANE), LANE)
            parts = [chain[at, :] for chain in chains]
            while len(parts) > 1:
                parts = [a + b for a, b in zip(parts[::2], parts[1::2])]
            turned = parts[0].T
            for q in range(4):
                for o in range(groups // 8):
                    at = pl.ds(o * 8 * row_count + rr * 4 + q, 8, stride=row_count)
                    first = q * groups + o * 8
                    forced[at, :] = background[at, :] + turned[first : first + 8, :]
        zero = jnp.zeros((8, LANE), f32)
        per_group = moments.shape[0] // groups
        for o in range(groups // 8):
            rows = [
                forced[pl.ds(o * 8 * row_count + r, 8, stride=row_count), :]
                for r in range(row_count)
            ]
            _, ends = lat_sweeps(
                rows, lambda r: decay[r * groups + o * 8 : r * groups + o * 8 + 8, :], [zero] * 4
            )
            for k in range(4):
                start = o * 8 * per_group + k * (per_group // 4) + ct
                moments[pl.ds(start, 8, stride=per_group), :] = ends[k]


def force(places, got, quarters, background, decay, row_count, groups):
    rows, columns = background.shape
    tiles = columns // LANE
    total = places.shape[0]
    depth = rows * columns // LANE
    block = pl.BlockSpec((rows, LANE), lambda i: (0, jnp.maximum(i - 1, 0)))
    return pl.pallas_call(
        functools.partial(forced_kernel, row_count, groups),
        grid=(tiles + 1,),
        out_shape=(
            jax.ShapeDtypeStruct((tiles, rows, LANE), f32),
            jax.ShapeDtypeStruct((groups * 4 * tiles, LANE), f32),
        ),
        in_specs=[
            pl.BlockSpec(memory_space=pltpu.SMEM),
            pl.BlockSpec(got.shape, lambda i: (0, 0, 0), pipeline_mode=pl.Buffered(1)),
            pl.BlockSpec(quarters.shape, lambda i: (0, 0, 0), pipeline_mode=pl.Buffered(1)),
            block,
            pl.BlockSpec((rows, LANE), lambda i: (0, 0), pipeline_mode=pl.Buffered(1)),
        ],
        out_specs=(
            pl.BlockSpec((None, rows, LANE), lambda i: (jnp.maximum(i - 1, 0), 0, 0)),
            pl.BlockSpec((groups * 4 * tiles, LANE), lambda i: (0, 0)),
        ),
        scratch_shapes=[pltpu.VMEM((total, LANE), f32)] + [pltpu.VMEM((depth, LANE), f32)] * CHAINS,
        compiler_params=vmem(60),
        cost_estimate=cost(0, 16 << 20),
        name="force",
    )(places, got, quarters, background, decay)


def lon_weights(length, columns):
    blocks = columns // LANE
    length = length[:, None, None]
    kappa = jnp.tanh(0.5 / length)
    beta = kappa * kappa
    alpha = beta / jnp.tanh(1.0 / length)
    i = jnp.arange(LANE, dtype=f32)

    def power(n):
        return jnp.exp(-n / length)

    gap = jnp.abs(i[:, None] - i[None, :])[None]
    local = (alpha + beta * gap) * power(gap)
    up, down = i[None, :, None], (LANE - 1.0) - i[None, :, None]
    sums = jnp.concatenate(
        [power(down), down * power(down), power(up), up * power(up)], axis=2
    )
    sums = jnp.pad(sums, ((0, 0), (0, 0), (0, LANE - 4)))
    first = jnp.concatenate([local, sums], axis=2)
    index = jnp.arange(LANE)
    src, dst = index[:, None], index[None, :]
    source, target = src // 4, dst // 4
    backward = (src % 4) >= 2
    steps = jnp.where(backward, source - target - 1, target - source - 1) % blocks
    gap = (LANE * steps).astype(f32)[None]
    turn = power(float(columns))
    left = -jnp.expm1(-float(columns) / length)
    same = power(gap) / left
    cross = (gap + columns * turn / left) * same
    used = (source < blocks) & (target < blocks)
    mix = jnp.where((used & (src % 4 == dst % 4))[None], same, 0.0)
    mix = jnp.where((used & (src % 2 == 0) & (dst % 4 == src % 4 + 1))[None], cross, mix)
    near, far = i[None, None, :] + 1.0, LANE - i[None, None, :]
    back = jnp.concatenate(
        [
            (alpha + beta * near) * power(near),
            beta * power(near),
            (alpha + beta * far) * power(far),
            beta * power(far),
        ],
        axis=1,
    )
    back = jnp.pad(back, ((0, 0), (0, LANE - 4), (0, 0)))
    return thirds(first), thirds(mix), thirds(back)


def thirds(w):
    high = lax.reduce_precision(w, 8, 7)
    low = (w - high).astype(bf16)
    high = high.astype(bf16)
    return jnp.concatenate([high, high, low], axis=1)


def dot3(x, w):
    high = x.astype(bf16)
    low = (x - high.astype(f32)).astype(bf16)
    return jnp.dot(jnp.concatenate([high, low, high], axis=1), w, preferred_element_type=f32)


def lon_apply(parts, first, mix, back):
    count, blocks = parts[0].shape[0], len(parts)
    both = dot3(jnp.concatenate(parts, axis=0), first)
    local, sums = both[:, :LANE], both[:, LANE:]
    line = sums[:count]
    for b in range(1, blocks):
        line = line + pltpu.roll(sums[b * count : (b + 1) * count], 4 * b, 1)
    states = dot3(line, mix)
    spread = jnp.concatenate(
        [states] + [pltpu.roll(states, LANE - 4 * b, 1) for b in range(1, blocks)], axis=0
    )
    out = local + dot3(spread, back)
    return [out[b * count : (b + 1) * count] for b in range(blocks)]


def lon_kernel(x, first, mix, back, out):
    tiles = x.shape[0]
    count = x.shape[1] // first.shape[0]
    for g in range(first.shape[0]):
        at = slice(g * count, (g + 1) * count)
        done = lon_apply([x[b, at, :] for b in range(tiles)], first[g], mix[g], back[g])
        for b in range(tiles):
            out[b, at, :] = done[b]


def lon_filter(x, weights, row_count, half):
    tiles, rows, _ = x.shape
    per_step = 4
    steps = rows // row_count // per_step // 2
    return pl.pallas_call(
        lon_kernel,
        grid=(steps,),
        out_shape=jax.ShapeDtypeStruct((tiles, rows // 2, LANE), f32),
        in_specs=[pl.BlockSpec((tiles, per_step * row_count, LANE), lambda i: (0, i + half * steps, 0))]
        + [
            pl.BlockSpec((per_step,) + w.shape[1:], lambda i: (i + half * steps, 0, 0))
            for w in weights
        ],
        out_specs=pl.BlockSpec((tiles, per_step * row_count, LANE), lambda i: (0, i, 0)),
        compiler_params=vmem(60),
        cost_estimate=cost(3 * rows * tiles * LANE * 3 * LANE, 30 << 20),
        name="lon",
    )(x, *weights)


def hub_kernel(decay, moments, first, mix, back, states, work):
    blocks = 32
    depth = moments.shape[0] // blocks
    tiles = depth // 4
    count = decay.shape[0]
    coef = [decay[r : r + 1, :] for r in range(count)]

    def forward(rows):
        state, out = jnp.zeros((1, LANE), f32), []
        for r in range(count):
            state = rows[r] + coef[r] * (state - rows[r])
            out.append(state)
        return out

    def backward(rows):
        state, out = jnp.zeros((1, LANE), f32), [None] * count
        for r in range(count - 1, -1, -1):
            state = rows[r] + coef[r] * (state - rows[r])
            out[r] = state
        return out

    state, down = jnp.ones((1, LANE), f32), []
    for r in range(count):
        state = coef[r] * state
        down.append(state)
    full = state
    state, up = jnp.ones((1, LANE), f32), [None] * count
    for r in range(count - 1, -1, -1):
        state = coef[r] * state
        up[r] = state
    bp = backward(down)
    fbp = forward(bp)
    bfbp = backward(fbp)
    fq = forward(up)
    bfq = backward(fq)
    t21, t31, t41, t32, t42 = bp[0], fbp[-1], bfbp[0], fq[-1], bfq[0]

    def at(table, d):
        return jnp.broadcast_to(table[:, d : d + 1], (tiles, LANE))

    def moment(d, k):
        return moments[d * depth + k * tiles : d * depth + (k + 1) * tiles, :]

    def put(d, k, value):
        for t in range(tiles):
            work[t, k * blocks + d, :] = value[t]

    zero = jnp.zeros((tiles, LANE), f32)
    s = [[None] * blocks for _ in range(4)]
    carry = zero
    for d in range(blocks):
        s[0][d] = carry
        carry = at(full, d) * carry + moment(d, 0)
    carry = zero
    for d in range(blocks - 1, -1, -1):
        s[1][d] = carry
        carry = at(full, d) * carry + (moment(d, 1) + at(t21, d) * s[0][d])
    carry = zero
    for d in range(blocks):
        s[2][d] = carry
        carry = at(full, d) * carry + (
            moment(d, 2) + at(t31, d) * s[0][d] + at(t32, d) * s[1][d]
        )
    carry = zero
    for d in range(blocks - 1, -1, -1):
        s[3][d] = carry
        carry = at(full, d) * carry + (
            moment(d, 3) + at(t41, d) * s[0][d] + at(t42, d) * s[1][d] + at(t21, d) * s[2][d]
        )
    for k in range(4):
        for d in range(blocks):
            put(d, k, s[k][d])
    done = lon_apply([work[t] for t in range(tiles)], first[0], mix[0], back[0])
    for t in range(tiles):
        for k in range(4):
            states[pl.ds(k * tiles + t, blocks, stride=depth), :] = done[t][
                k * blocks : (k + 1) * blocks
            ]


def hub(decay, moments, weights):
    depth = moments.shape[0] // 32
    return pl.pallas_call(
        hub_kernel,
        out_shape=jax.ShapeDtypeStruct(moments.shape, f32),
        in_specs=[pl.BlockSpec(memory_space=pltpu.VMEM)] * 5,
        out_specs=pl.BlockSpec(memory_space=pltpu.VMEM),
        scratch_shapes=[pltpu.VMEM((depth // 4, 128, LANE), f32)],
        compiler_params=vmem(60),
        cost_estimate=cost(0, 4 << 20),
        name="hub",
    )(decay, moments, *weights)


def level_sweeps(rows, decay, starts):
    count = len(rows)
    ends = []
    for sweep in range(2):
        order = range(count) if sweep == 0 else range(count - 1, -1, -1)
        state = starts[sweep]
        out = [None] * count
        for r in order:
            state = rows[r] + decay(r) * (state - rows[r])
            out[r] = state
        ends.append(state)
        rows = out
    return rows, ends


def lat_states_kernel(row_count, groups, variables, low, high, decay, states, vert, coef, out, sums):
    ct = pl.program_id(0)
    per_group = states.shape[0] // groups
    half = low.shape[0]
    for o in range(groups // 8):
        base = o * 8 * row_count
        x, first = (low, base) if base < half else (high, base - half)
        rows = [x[pl.ds(first + r, 8, stride=row_count), :] for r in range(row_count)]
        starts = [
            states[pl.ds(o * 8 * per_group + k * (per_group // 4) + ct, 8, stride=per_group), :]
            for k in range(4)
        ]
        rows, _ = lat_sweeps(
            rows, lambda r: decay[r * groups + o * 8 : r * groups + o * 8 + 8, :], starts
        )
        for r in range(row_count):
            out[pl.ds(base + r, 8, stride=row_count), :] = rows[r]
    zero = jnp.zeros((8, LANE), f32)
    levels = groups // variables
    halves = pl.num_programs(0) // 2
    depth = halves * row_count
    size = sums.shape[0] // (2 * variables)
    for var in range(variables):
        for t in range(row_count // 8):
            rows = []
            for lev in range(levels):
                base = (lev * variables + var) * row_count + t * 8
                rows.append(out[base : base + 8, :])
            _, ends = level_sweeps(rows, lambda lev: vert[lev * variables + var], [zero, zero])
            for k in range(2):
                start = (var * 2 + ct // halves) * size + k * depth + (ct % halves) * row_count + t * 8
                sums[pl.ds(pl.multiple_of(start, 8), 8), :] = ends[k]

    @pl.when(ct == 0)
    def _():
        for target in range(2 * variables):
            start = target * size + 2 * depth
            sums[start : start + 8, :] = coef[target // 2]


def lat_states(low, high, decay, states, vert, coef, row_count, groups, variables):
    tiles, rows = low.shape[0], 2 * low.shape[1]
    part = pl.BlockSpec((None, rows // 2, LANE), lambda i: (i, 0, 0))
    block = pl.BlockSpec((None, rows, LANE), lambda i: (i, 0, 0))
    size = 2 * variables * (tiles * row_count + 8)
    return pl.pallas_call(
        functools.partial(lat_states_kernel, row_count, groups, variables),
        grid=(tiles,),
        out_shape=(
            jax.ShapeDtypeStruct((tiles, rows, LANE), f32),
            jax.ShapeDtypeStruct((size, LANE), f32),
        ),
        in_specs=[
            part,
            part,
            pl.BlockSpec((rows, LANE), lambda i: (0, 0)),
            pl.BlockSpec(states.shape, lambda i: (0, 0)),
            pl.BlockSpec(memory_space=pltpu.SMEM),
            pl.BlockSpec(coef.shape, lambda i: (0, 0, 0)),
        ],
        out_specs=(block, pl.BlockSpec((size, LANE), lambda i: (0, 0))),
        compiler_params=vmem(60),
        cost_estimate=cost(0, 12 << 20),
        name="lat_states",
    )(low, high, decay, states, vert, coef)


def level_exchange_kernel(sums, out, beside, merged, arrived, replies, entering, passed, *sems):
    pair_send, pair_recv, hub_send, hub_recv, back_send, back_recv, last_send, last_recv = sems
    band = lax.axis_index("band")
    chip, core = band // 2, band % 2
    depth = out.shape[1] // 2
    tail = 2 * depth
    mine_first = core * 4

    def other(step):
        return lax.rem(chip + step, 4) * 2 + core

    def remote(src, dst, send, recv, target):
        return pltpu.make_async_remote_copy(
            src_ref=src,
            dst_ref=dst,
            send_sem=send,
            recv_sem=recv,
            device_id={"band": target},
            device_id_type=pl.DeviceIdType.MESH,
        )

    sibling = chip * 2 + (1 - core)
    barrier = pltpu.get_barrier_semaphore()
    for target in [sibling] + [other(step) for step in (1, 2, 3)]:
        pl.semaphore_signal(
            barrier, inc=1, device_id={"band": target}, device_id_type=pl.DeviceIdType.MESH
        )
    pl.semaphore_wait(barrier, 4)

    pair = remote(
        sums.at[pl.ds((1 - core) * 4, 4)], beside, pair_send.at[0], pair_recv.at[0], sibling
    )
    pair.start()
    pair.wait_recv()

    def lower(a, b):
        return jnp.where(core == 0, a, b)

    def row(ref, chunk, at):
        return jnp.broadcast_to(ref[chunk, at : at + 1, :], (8, LANE))

    def bands_of(chunk, at):
        a, b = sums[mine_first + chunk, at, :], beside[chunk, at, :]
        return lower(a, b), lower(b, a)

    def coefficients(chunk):
        both = []
        for at in (tail, tail + 1):
            a, b = row(sums, mine_first + chunk, at), row(beside, chunk, at)
            both.append((lower(a, b), lower(b, a)))
        return both

    def merge(chunk):
        (full0, full1), (both0, both1) = coefficients(chunk)

        @pl.loop(0, depth // 8)
        def _(t):
            at = pl.ds(pl.multiple_of(t * 8, 8), 8)
            later = pl.ds(pl.multiple_of(depth + t * 8, 8), 8)
            up0, up1 = bands_of(chunk, at)
            down0, down1 = bands_of(chunk, later)
            merged[chunk, at, :] = full1 * up0 + up1
            merged[chunk, later, :] = down0 + full0 * (down1 + both1 * up0)

        index = lax.broadcasted_iota(jnp.int32, (8, LANE), 0)
        full = full0 * full1
        both = both0 + full0 * both1 * full0
        merged[chunk, tail : tail + 8, :] = jnp.where(index == 0, full, both)

    sends = []
    for step in (1, 2, 3):
        chunk = lax.rem(chip + step, 4)
        merge(chunk)
        copy = remote(
            merged.at[chunk], arrived.at[chip], hub_send.at[step - 1], hub_recv.at[step - 1], other(step)
        )
        copy.start()
        sends.append(copy)
    merge(chip)
    arrived[chip] = merged[chip]
    for copy in sends:
        copy.wait_recv()

    full = [row(arrived, c, tail) for c in range(4)]
    both = [row(arrived, c, tail + 1) for c in range(4)]

    @pl.loop(0, depth // 8)
    def _(t):
        at = pl.ds(pl.multiple_of(t * 8, 8), 8)
        later = pl.ds(pl.multiple_of(depth + t * 8, 8), 8)
        state = jnp.zeros((8, LANE), f32)
        ups = []
        for c in range(4):
            ups.append(state)
            replies[c, at, :] = state
            state = full[c] * state + arrived[c, at, :]
        state = jnp.zeros((8, LANE), f32)
        for c in (3, 2, 1, 0):
            replies[c, later, :] = state
            state = full[c] * state + (arrived[c, later, :] + both[c] * ups[c])

    backs = []
    for step in (1, 2, 3):
        copy = remote(
            replies.at[lax.rem(chip + step, 4)],
            entering.at[chip],
            back_send.at[step - 1],
            back_recv.at[step - 1],
            other(step),
        )
        copy.start()
        backs.append(copy)
    entering[chip] = replies[chip]
    for copy in backs:
        copy.wait_recv()

    for chunk in range(4):
        (full0, full1), (both0, both1) = coefficients(chunk)

        @pl.loop(0, depth // 8)
        def _(t):
            at = pl.ds(pl.multiple_of(t * 8, 8), 8)
            later = pl.ds(pl.multiple_of(depth + t * 8, 8), 8)
            up0, _ = bands_of(chunk, at)
            _, down1 = bands_of(chunk, later)
            first = entering[chunk, at, :]
            last = entering[chunk, later, :]
            middle = full0 * first + up0
            turned = full1 * last + (down1 + both1 * middle)
            out[mine_first + chunk, at, :] = lower(first, middle)
            out[mine_first + chunk, later, :] = lower(turned, last)
            passed[chunk, at, :] = lower(middle, first)
            passed[chunk, later, :] = lower(last, turned)

    final = remote(passed, out.at[pl.ds(mine_first, 4)], last_send.at[0], last_recv.at[0], sibling)
    final.start()
    pair.wait_send()
    for copy in sends + backs:
        copy.wait_send()
    final.wait()


def level_exchange(sums):
    bands, size, _ = sums.shape
    depth = (size - 8) // 2
    whole = pl.BlockSpec(memory_space=pltpu.VMEM)
    dma = pltpu.SemaphoreType.DMA
    return pl.pallas_call(
        level_exchange_kernel,
        out_shape=jax.ShapeDtypeStruct((bands, 2 * depth, LANE), f32),
        in_specs=[whole],
        out_specs=whole,
        scratch_shapes=[
            pltpu.VMEM((4, size, LANE), f32),
            pltpu.VMEM((4, size, LANE), f32),
            pltpu.VMEM((4, size, LANE), f32),
            pltpu.VMEM((4, 2 * depth, LANE), f32),
            pltpu.VMEM((4, 2 * depth, LANE), f32),
            pltpu.VMEM((4, 2 * depth, LANE), f32),
            dma((1,)),
            dma((1,)),
            dma((3,)),
            dma((3,)),
            dma((3,)),
            dma((3,)),
            dma((1,)),
            dma((1,)),
        ],
        compiler_params=pltpu.CompilerParams(
            vmem_limit_bytes=60 << 20, collective_id=0, has_side_effects=True
        ),
        cost_estimate=cost(0, 3 << 20),
        name="level_exchange",
    )(sums)


def level_states_kernel(x, vert, states, out):
    var = pl.program_id(0)
    variables = pl.num_programs(0)
    tiles, levels, row_count, _ = x.shape
    decay = [vert[lev * variables + var] for lev in range(levels)]
    for ct in range(tiles):
        for t in range(row_count // 8):
            at = slice(t * 8, t * 8 + 8)
            rows = [x[ct, lev, at, :] for lev in range(levels)]
            starts = [states[ct // (tiles // 2), k, ct % (tiles // 2), at, :] for k in range(2)]
            rows, _ = level_sweeps(rows, lambda lev: decay[lev], starts)
            for lev in range(levels):
                out[lev, at, ct * LANE : (ct + 1) * LANE] = rows[lev]


def level_states(x, vert, states, shape):
    levels, variables, row_count, columns = shape
    tiles = columns // LANE
    return pl.pallas_call(
        level_states_kernel,
        grid=(variables,),
        out_shape=jax.ShapeDtypeStruct(shape, f32),
        in_specs=[
            pl.BlockSpec((tiles, levels, None, row_count, LANE), lambda i: (0, 0, i, 0, 0)),
            pl.BlockSpec(memory_space=pltpu.SMEM),
            pl.BlockSpec((None, 2, 2, tiles // 2, row_count, LANE), lambda i: (i, 0, 0, 0, 0, 0)),
        ],
        out_specs=pl.BlockSpec((levels, None, row_count, columns), lambda i: (0, i, 0, 0)),
        compiler_params=vmem(60),
        cost_estimate=cost(0, 11 << 20),
        name="level_states",
    )(x.reshape(tiles, levels, variables, row_count, LANE), vert, states)


def level_coefficients(decays):
    levels = decays.shape[0]
    state, down = jnp.ones_like(decays[0]), []
    for r in range(levels):
        state = decays[r] * state
        down.append(state)
    full = state
    state = jnp.zeros_like(full)
    for r in range(levels - 1, -1, -1):
        state = down[r] + decays[r] * (state - down[r])
    both = jnp.stack([full, state], axis=1)
    both = jnp.pad(both, ((0, 0), (0, 6)))
    return jnp.broadcast_to(both[:, :, None], both.shape + (LANE,))


def per_device(background, obs_columns, obs_owner, obs_cell, lat_length, lon_length, vert_length):
    level_count, var_count, row_count, lon_count = background.shape
    sub_count = lax.axis_size("sub")
    band_count = lax.axis_size("band")
    sub_index = lax.axis_index("sub")
    groups = level_count * var_count
    tiles = lon_count // LANE
    tile_field = background.reshape(groups * row_count, lon_count)
    obs_values = obs_columns.reshape(groups, -1)
    owners = obs_owner[:, 0]
    capacity = 2 * owners.shape[0] // sub_count

    ranks = route_ranks(owners, sub_count)
    row, column = obs_cell // lon_count, obs_cell % lon_count
    place = ((row // 4) * lon_count + column) * 4 + row % 4
    table = jnp.stack([owners, ranks, place] + [jnp.zeros_like(place)] * 5)
    lines = capacity // LANE
    message = pack(owners * capacity + ranks, table, obs_values, sub_count)
    got = lax.all_to_all(message.reshape(sub_count, -1, LANE), "sub", 0, 0, tiled=True)

    vert_decay = jnp.exp(-1.0 / vert_length)
    coef = level_coefficients(vert_decay)
    vert_decay = vert_decay.reshape(groups)

    lat_all = jnp.exp(-1.0 / lat_length).reshape(groups, sub_count, row_count)
    own_lat = lax.dynamic_index_in_dim(lat_all, sub_index, 1, False)
    decay = jnp.broadcast_to(own_lat.T.reshape(row_count * groups, 1), (row_count * groups, LANE))
    hub_lat = lax.dynamic_index_in_dim(lat_all, sub_index, 0, False)
    hub_lat = jnp.pad(hub_lat.T, ((0, 0), (0, LANE - sub_count)))

    lengths = lon_length.reshape(groups)
    weights = lon_weights(lengths, lon_count)
    own_weights = [lax.dynamic_slice_in_dim(w, sub_index, 1, 0) for w in weights]

    places = got[:, capacity // 4 : capacity // 4 + lines, :].reshape(-1).astype(jnp.int32)
    quarters = (places & 3).astype(f32).reshape(sub_count, 4, capacity // 4)
    quarters = jnp.pad(quarters, ((0, 0), (0, 4), (0, 0)))
    forced, moments = force(places >> 2, got, quarters, tile_field, decay, row_count, groups)
    moments = lax.all_to_all(
        moments.reshape(sub_count, 4 * tiles, LANE), "sub", 0, 0, tiled=True
    )
    low = lon_filter(forced, weights, row_count, 0)
    moments, low = lax.optimization_barrier((moments, low))
    states = hub(hub_lat, moments.reshape(-1, LANE), own_weights)
    states, forced = lax.optimization_barrier((states, forced))
    states = lax.all_to_all(states.reshape(sub_count, 4 * tiles, LANE), "sub", 0, 0, tiled=True)
    high = lon_filter(forced, weights, row_count, 1)
    smooth, sums = lat_states(
        low, high, decay, states.reshape(-1, LANE), vert_decay, coef, row_count, groups, var_count
    )
    entering = level_exchange(sums.reshape(band_count, -1, LANE))
    return level_states(
        smooth,
        vert_decay,
        entering.reshape(var_count, 2, 2, tiles // 2, row_count, LANE),
        background.shape,
    )


def solution(mesh):
    placed = (
        P("band", None, "sub", None),
        P("band", None, "sub"),
        P("sub", None),
        P("sub"),
        P("band", None, None),
        P("band", None),
        P("band", None),
    )
    return jax.shard_map(
        per_device,
        mesh=mesh,
        in_specs=placed,
        out_specs=P("band", None, "sub", None),
        check_vma=False,
    )
```

```python
import functools

import jax
import jax.numpy as jnp
from jax import lax
from jax.experimental import pallas as pl
from jax.experimental.pallas import tpu as pltpu
from jax.sharding import PartitionSpec as P

LANE = 128
f32 = jnp.float32
bf16 = jnp.bfloat16


def vmem(mib):
    return pltpu.CompilerParams(vmem_limit_bytes=mib << 20)


def cost(flops, moved):
    return pl.CostEstimate(flops=flops, bytes_accessed=moved, transcendentals=0)


def route_ranks(owners, sub_count):
    count = owners.shape[0]
    block = 128
    owner_block = owners.reshape(count // block, block)
    match = (owner_block[:, :, None] == jnp.arange(sub_count, dtype=jnp.int32)).astype(bf16)
    position = jnp.arange(block)
    lower = (position[:, None] > position[None, :]).astype(bf16)
    ahead = jnp.einsum("ij,bjo->bio", lower, match, preferred_element_type=f32)
    totals = jnp.sum(match.astype(f32), axis=1)
    base = jnp.cumsum(totals, axis=0) - totals
    rank = jnp.sum((ahead + base[:, None, :]) * match.astype(f32), axis=2)
    return rank.reshape(count).astype(jnp.int32)


def pack_kernel(slots, table, values, packed, rows, big):
    levels, _, count = values.shape
    total = big.shape[0]
    targets = total // 256
    size = packed.shape[0] // targets

    @pl.loop(0, total // 64)
    def _(i):
        big[pl.ds(pl.multiple_of(i * 64, 64), 64), :] = jnp.zeros((64, LANE), f32)

    for j in range(count // LANE):
        part = jnp.concatenate(
            [values[lev, :, j * LANE : (j + 1) * LANE] for lev in range(levels)], axis=0
        )
        rows[j * LANE : (j + 1) * LANE, :] = jnp.concatenate([part] * 4, axis=0).T

    owner, rank, place = table[0:1, :], table[1:2, :], table[2:3, :]
    mine = owner == lax.broadcasted_iota(jnp.int32, (targets, count), 0)
    spot = (rank == lax.broadcasted_iota(jnp.int32, (256, count), 0)).astype(f32).astype(bf16)

    def put(half):
        left = jnp.where(mine, half, 0).astype(f32).astype(bf16)
        return lax.dot_general(
            left, spot, (((1,), (1,)), ((), ())), preferred_element_type=f32
        )

    cells = put(lax.shift_right_logical(place, 8)) * 256.0 + put(place & 255)
    for half in range(2):
        packed[pl.ds(64 + half, targets, stride=size), :] = cells[:, half * LANE : (half + 1) * LANE]
    for extra in range(66, size):
        packed[pl.ds(extra, targets, stride=size), :] = jnp.zeros((targets, LANE), f32)

    step = 16

    @pl.loop(0, count // step)
    def _(i):
        for u in range(step):
            j = i * step + u
            big[pl.ds(slots[j], 1), :] = rows[pl.ds(j, 1), :]

    quarter = lax.broadcasted_iota(jnp.int32, (64, LANE), 1) // 32

    @pl.loop(0, targets)
    def _(d):
        start = pl.multiple_of(d * 256, 256)
        out = big[pl.ds(start, 64), :]
        for k in range(1, 4):
            out = jnp.where(quarter == k, big[pl.ds(start + 64 * k, 64), :], out)
        packed[pl.ds(pl.multiple_of(d * size, 8), 64), :] = out


def pack(slots, table, values, targets):
    count = values.shape[2]
    total = targets * 256
    whole = pl.BlockSpec(memory_space=pltpu.VMEM)
    return pl.pallas_call(
        pack_kernel,
        out_shape=jax.ShapeDtypeStruct((targets * 72, LANE), f32),
        in_specs=[pl.BlockSpec(memory_space=pltpu.SMEM), whole, whole],
        out_specs=whole,
        scratch_shapes=[pltpu.VMEM((count, LANE), f32), pltpu.VMEM((total, LANE), f32)],
        compiler_params=vmem(60),
        cost_estimate=cost(0, 4 << 20),
        name="pack",
    )(slots, table, values)


def lat_sweeps(sets, decays, starts):
    count = len(sets[0])
    ends = [[] for _ in sets]
    for sweep in range(4):
        order = range(count) if sweep % 2 == 0 else range(count - 1, -1, -1)
        states = [start[sweep] for start in starts]
        outs = [[None] * count for _ in sets]
        for r in order:
            for i, rows in enumerate(sets):
                a, rest = decays[i](r)
                states[i] = a * states[i] + rest * rows[r]
                outs[i][r] = states[i]
        for i in range(len(sets)):
            ends[i].append(states[i])
        sets = outs
    return sets, ends


def decay_of_octet(decay, groups, o):
    rows = decay.shape[0] // 2

    def pair(r):
        at = r * groups + o * 8
        return decay[at : at + 8, :], decay[rows + at : rows + at + 8, :]

    return pair


CHAINS = 8
SIDE = 1


def forced_kernel(row_count, groups, places, got, quarters, background, decay, forced, moments, spread, field, sem, out_sem, *chains):
    total = spread.shape[0]
    depth = chains[0].shape[0]
    sources = got.shape[0]
    tiles = forced.shape[0]
    fetches = [
        pltpu.make_async_copy(
            background.at[:, ct * LANE : (ct + 1) * LANE], field.at[ct], sem.at[ct]
        )
        for ct in range(tiles)
    ]
    for fetch in fetches:
        fetch.start()

    @pl.loop(0, depth // 64)
    def _(i):
        at = pl.ds(pl.multiple_of(i * 64, 64), 64)
        for chain in chains:
            chain[at, :] = jnp.zeros((64, LANE), f32)

    lane = lax.broadcasted_iota(jnp.int32, (8, LANE), 1) // 32
    pick = (lane == lax.broadcasted_iota(jnp.int32, (8, LANE), 0)).astype(bf16)
    quarter = lax.broadcasted_iota(jnp.int32, (64, LANE), 1) // 32
    wanted = quarter.astype(f32)

    def turns(x):
        return [x] + [pltpu.roll(x, 32 * k, 1) for k in range(1, 4)]

    def repeat(turned, k):
        out = turned[(3 - k) % 4]
        for q in range(3):
            out = jnp.where(quarter == q, turned[(q - k) % 4], out)
        return out

    @pl.loop(0, sources)
    def _(d):
        part = turns(got[d, :64, :])
        mark = turns(
            lax.dot_general(
                quarters[d].astype(bf16), pick, (((0,), (0,)), ((), ())), preferred_element_type=f32
            )
        )
        for k in range(4):
            one = jnp.where(repeat(mark, k) == wanted, repeat(part, k), 0.0)
            spread[pl.ds(pl.multiple_of(d * 256 + k * 64, 64), 64), :] = one

    step = 4

    @pl.loop(0, total // (CHAINS * step))
    def _(i):
        for u in range(step):
            spots = [(i * step + u) * CHAINS + c for c in range(CHAINS)]
            where = [pl.ds(places[j], 1) for j in spots]
            adds = [spread[pl.ds(j, 1), :] for j in spots]
            olds = [chains[c][where[c], :] for c in range(CHAINS)]
            for c in range(CHAINS):
                chains[c][where[c], :] = olds[c] + adds[c]

    for fetch in fetches:
        fetch.wait()
    columns = depth // (row_count // 4)

    @pl.loop(0, tiles)
    def _(ct):
        out = field.at[ct]
        for rr in range(row_count // 4):
            at = pl.ds(pl.multiple_of(rr * columns + ct * LANE, LANE), LANE)
            parts = [chain[at, :] for chain in chains]
            while len(parts) > 1:
                parts = [a + b for a, b in zip(parts[::2], parts[1::2])]
            turned = parts[0].T
            for q in range(4):
                for o in range(groups // 8):
                    at = pl.ds(o * 8 * row_count + rr * 4 + q, 8, stride=row_count)
                    first = q * groups + o * 8
                    out[at, :] = out[at, :] + turned[first : first + 8, :]
        pltpu.make_async_copy(field.at[ct], forced.at[ct], out_sem.at[ct]).start()
        zero = jnp.zeros((8, LANE), f32)
        per_group = moments.shape[0] // groups
        for first in range(0, groups // 8, SIDE):
            octets = range(first, first + SIDE)
            sets = [
                [
                    out[pl.ds(o * 8 * row_count + r, 8, stride=row_count), :]
                    for r in range(row_count)
                ]
                for o in octets
            ]
            _, ends = lat_sweeps(
                sets, [decay_of_octet(decay, groups, o) for o in octets], [[zero] * 4] * SIDE
            )
            for i, o in enumerate(octets):
                for k in range(4):
                    start = o * 8 * per_group + k * (per_group // 4) + ct
                    moments[pl.ds(start, 8, stride=per_group), :] = ends[i][k]

    for ct in range(tiles):
        pltpu.make_async_copy(field.at[ct], forced.at[ct], out_sem.at[ct]).wait()


def force(places, got, quarters, background, decay, row_count, groups):
    rows, columns = background.shape
    tiles = columns // LANE
    total = places.shape[0]
    depth = rows * columns // LANE
    whole = pl.BlockSpec(memory_space=pltpu.VMEM)
    return pl.pallas_call(
        functools.partial(forced_kernel, row_count, groups),
        out_shape=(
            jax.ShapeDtypeStruct((tiles, rows, LANE), f32),
            jax.ShapeDtypeStruct((groups * 4 * tiles, LANE), f32),
        ),
        in_specs=[
            pl.BlockSpec(memory_space=pltpu.SMEM),
            whole,
            whole,
            pl.BlockSpec(memory_space=pl.ANY),
            whole,
        ],
        out_specs=(pl.BlockSpec(memory_space=pl.ANY), whole),
        scratch_shapes=[
            pltpu.VMEM((total, LANE), f32),
            pltpu.VMEM((tiles, rows, LANE), f32),
            pltpu.SemaphoreType.DMA((tiles,)),
            pltpu.SemaphoreType.DMA((tiles,)),
        ]
        + [pltpu.VMEM((depth, LANE), f32)] * CHAINS,
        compiler_params=vmem(58),
        cost_estimate=cost(0, 16 << 20),
        name="force",
    )(places, got, quarters, background, decay)


def lon_weights(length, columns):
    blocks = columns // LANE
    length = length[:, None, None]
    kappa = jnp.tanh(0.5 / length)
    beta = kappa * kappa
    alpha = beta / jnp.tanh(1.0 / length)
    i = jnp.arange(LANE, dtype=f32)

    def power(n):
        return jnp.exp(-n / length)

    gap = jnp.abs(i[:, None] - i[None, :])[None]
    local = (alpha + beta * gap) * power(gap)
    up, down = i[None, :, None], (LANE - 1.0) - i[None, :, None]
    sums = jnp.concatenate(
        [power(down), down * power(down), power(up), up * power(up)], axis=2
    )
    sums = jnp.pad(sums, ((0, 0), (0, 0), (0, LANE - 4)))
    first = jnp.concatenate([local, sums], axis=2)
    index = jnp.arange(LANE)
    src, dst = index[:, None], index[None, :]
    source, target = src // 4, dst // 4
    backward = (src % 4) >= 2
    steps = jnp.where(backward, source - target - 1, target - source - 1) % blocks
    gap = (LANE * steps).astype(f32)[None]
    turn = power(float(columns))
    left = -jnp.expm1(-float(columns) / length)
    same = power(gap) / left
    cross = (gap + columns * turn / left) * same
    used = (source < blocks) & (target < blocks)
    mix = jnp.where((used & (src % 4 == dst % 4))[None], same, 0.0)
    mix = jnp.where((used & (src % 2 == 0) & (dst % 4 == src % 4 + 1))[None], cross, mix)
    near, far = i[None, None, :] + 1.0, LANE - i[None, None, :]
    back = jnp.concatenate(
        [
            (alpha + beta * near) * power(near),
            beta * power(near),
            (alpha + beta * far) * power(far),
            beta * power(far),
        ],
        axis=1,
    )
    back = jnp.pad(back, ((0, 0), (0, LANE - 4), (0, 0)))
    return thirds(first), thirds(mix), thirds(back)


def thirds(w):
    high = lax.reduce_precision(w, 8, 7)
    low = (w - high).astype(bf16)
    high = high.astype(bf16)
    return jnp.concatenate([high, high, low], axis=1)


def dot3(x, w):
    high = x.astype(bf16)
    low = (x - high.astype(f32)).astype(bf16)
    return jnp.dot(jnp.concatenate([high, low, high], axis=1), w, preferred_element_type=f32)


def lon_apply(parts, first, mix, back):
    count, blocks = parts[0].shape[0], len(parts)
    both = dot3(jnp.concatenate(parts, axis=0), first)
    local, sums = both[:, :LANE], both[:, LANE:]
    line = sums[:count]
    for b in range(1, blocks):
        line = line + pltpu.roll(sums[b * count : (b + 1) * count], 4 * b, 1)
    states = dot3(line, mix)
    spread = jnp.concatenate(
        [states] + [pltpu.roll(states, LANE - 4 * b, 1) for b in range(1, blocks)], axis=0
    )
    out = local + dot3(spread, back)
    return [out[b * count : (b + 1) * count] for b in range(blocks)]


LON_STEP = 4


def lon_kernel(count, first_group, x, first, mix, back, out, xs, ws, ms, bs, done, sems, out_sem):
    tiles, rows, _ = out.shape
    steps = rows // count // LON_STEP
    size = LON_STEP * count

    def fetches(i):
        group = first_group + i * LON_STEP
        source = pl.ds(pl.multiple_of(group * count, 8), size)
        target = pl.ds(pl.multiple_of(i * size, 8), size)
        inside = pl.ds(i * LON_STEP, LON_STEP)
        outside = pl.ds(group, LON_STEP)
        return [
            pltpu.make_async_copy(x.at[:, source], xs.at[:, target], sems.at[0, i]),
            pltpu.make_async_copy(first.at[outside], ws.at[inside], sems.at[1, i]),
            pltpu.make_async_copy(mix.at[outside], ms.at[inside], sems.at[2, i]),
            pltpu.make_async_copy(back.at[outside], bs.at[inside], sems.at[3, i]),
        ]

    def write(i):
        at = pl.ds(pl.multiple_of(i * size, 8), size)
        return pltpu.make_async_copy(done.at[:, at], out.at[:, at], out_sem.at[i])

    for i in range(steps):
        for fetch in fetches(i):
            fetch.start()

    @pl.loop(0, steps)
    def _(i):
        for fetch in fetches(i):
            fetch.wait()
        for u in range(LON_STEP):
            g = i * LON_STEP + u
            at = pl.ds(pl.multiple_of(g * count, 8), count)
            parts = lon_apply([xs[b, at, :] for b in range(tiles)], ws[g], ms[g], bs[g])
            for b in range(tiles):
                done[b, at, :] = parts[b]
        write(i).start()

    for i in range(steps):
        write(i).wait()


def lon_filter(x, weights, row_count, half):
    tiles, rows, _ = x.shape
    groups = rows // row_count // 2
    steps = groups // LON_STEP
    any_space = pl.BlockSpec(memory_space=pl.ANY)
    return pl.pallas_call(
        functools.partial(lon_kernel, row_count, half * groups),
        out_shape=jax.ShapeDtypeStruct((tiles, rows // 2, LANE), f32),
        in_specs=[any_space] * 4,
        out_specs=any_space,
        scratch_shapes=[pltpu.VMEM((tiles, rows // 2, LANE), f32)]
        + [pltpu.VMEM((groups,) + w.shape[1:], w.dtype) for w in weights]
        + [
            pltpu.VMEM((tiles, rows // 2, LANE), f32),
            pltpu.SemaphoreType.DMA((4, steps)),
            pltpu.SemaphoreType.DMA((steps,)),
        ],
        compiler_params=vmem(60),
        cost_estimate=cost(3 * rows * tiles * LANE * 3 * LANE, 30 << 20),
        name="lon",
    )(x, *weights)


def hub_kernel(decay, moments, first, mix, back, states, work):
    blocks = 32
    depth = moments.shape[0] // blocks
    tiles = depth // 4
    count = decay.shape[0]
    coef = [decay[r : r + 1, :] for r in range(count)]

    def forward(rows):
        state, out = jnp.zeros((1, LANE), f32), []
        for r in range(count):
            state = rows[r] + coef[r] * (state - rows[r])
            out.append(state)
        return out

    def backward(rows):
        state, out = jnp.zeros((1, LANE), f32), [None] * count
        for r in range(count - 1, -1, -1):
            state = rows[r] + coef[r] * (state - rows[r])
            out[r] = state
        return out

    state, down = jnp.ones((1, LANE), f32), []
    for r in range(count):
        state = coef[r] * state
        down.append(state)
    full = state
    state, up = jnp.ones((1, LANE), f32), [None] * count
    for r in range(count - 1, -1, -1):
        state = coef[r] * state
        up[r] = state
    bp = backward(down)
    fbp = forward(bp)
    bfbp = backward(fbp)
    fq = forward(up)
    bfq = backward(fq)
    t21, t31, t41, t32, t42 = bp[0], fbp[-1], bfbp[0], fq[-1], bfq[0]

    def at(table, d):
        return jnp.broadcast_to(table[:, d : d + 1], (tiles, LANE))

    def moment(d, k):
        return moments[d * depth + k * tiles : d * depth + (k + 1) * tiles, :]

    def put(d, k, value):
        for t in range(tiles):
            work[t, k * blocks + d, :] = value[t]

    zero = jnp.zeros((tiles, LANE), f32)
    s = [[None] * blocks for _ in range(4)]
    carry = zero
    for d in range(blocks):
        s[0][d] = carry
        carry = at(full, d) * carry + moment(d, 0)
    carry = zero
    for d in range(blocks - 1, -1, -1):
        s[1][d] = carry
        carry = at(full, d) * carry + (moment(d, 1) + at(t21, d) * s[0][d])
    carry = zero
    for d in range(blocks):
        s[2][d] = carry
        carry = at(full, d) * carry + (
            moment(d, 2) + at(t31, d) * s[0][d] + at(t32, d) * s[1][d]
        )
    carry = zero
    for d in range(blocks - 1, -1, -1):
        s[3][d] = carry
        carry = at(full, d) * carry + (
            moment(d, 3) + at(t41, d) * s[0][d] + at(t42, d) * s[1][d] + at(t21, d) * s[2][d]
        )
    for k in range(4):
        for d in range(blocks):
            put(d, k, s[k][d])
    done = lon_apply([work[t] for t in range(tiles)], first[0], mix[0], back[0])
    for t in range(tiles):
        for k in range(4):
            states[pl.ds(k * tiles + t, blocks, stride=depth), :] = done[t][
                k * blocks : (k + 1) * blocks
            ]


def hub(decay, moments, weights):
    depth = moments.shape[0] // 32
    return pl.pallas_call(
        hub_kernel,
        out_shape=jax.ShapeDtypeStruct(moments.shape, f32),
        in_specs=[pl.BlockSpec(memory_space=pltpu.VMEM)] * 5,
        out_specs=pl.BlockSpec(memory_space=pltpu.VMEM),
        scratch_shapes=[pltpu.VMEM((depth // 4, 128, LANE), f32)],
        compiler_params=vmem(60),
        cost_estimate=cost(0, 4 << 20),
        name="hub",
    )(decay, moments, *weights)


def level_sweeps(rows, decay, starts):
    count = len(rows)
    ends = []
    for sweep in range(2):
        order = range(count) if sweep == 0 else range(count - 1, -1, -1)
        state = starts[sweep]
        out = [None] * count
        for r in order:
            state = decay(r) * state + (1.0 - decay(r)) * rows[r]
            out[r] = state
        ends.append(state)
        rows = out
    return rows, ends


def lat_states_kernel(row_count, groups, variables, low, high, decay, states, vert, coef, out, sums, field, sems, out_sem):
    tiles = out.shape[0]
    per_group = states.shape[0] // groups
    half = low.shape[1]
    levels = groups // variables
    depth = tiles // 2 * row_count
    size = sums.shape[0] // (2 * variables)

    def fetches(ct):
        return [
            pltpu.make_async_copy(low.at[ct], field.at[ct, :half], sems.at[0, ct]),
            pltpu.make_async_copy(high.at[ct], field.at[ct, half:], sems.at[1, ct]),
        ]

    for ct in range(tiles):
        for fetch in fetches(ct):
            fetch.start()

    @pl.loop(0, tiles)
    def _(ct):
        for fetch in fetches(ct):
            fetch.wait()
        done = field.at[ct]
        for first in range(0, groups // 8, SIDE):
            octets = range(first, first + SIDE)
            sets = [
                [
                    done[pl.ds(o * 8 * row_count + r, 8, stride=row_count), :]
                    for r in range(row_count)
                ]
                for o in octets
            ]
            starts = [
                [
                    states[
                        pl.ds(o * 8 * per_group + k * (per_group // 4) + ct, 8, stride=per_group), :
                    ]
                    for k in range(4)
                ]
                for o in octets
            ]
            sets, _ = lat_sweeps(sets, [decay_of_octet(decay, groups, o) for o in octets], starts)
            for i, o in enumerate(octets):
                for r in range(row_count):
                    done[pl.ds(o * 8 * row_count + r, 8, stride=row_count), :] = sets[i][r]
        pltpu.make_async_copy(done, out.at[ct], out_sem.at[ct]).start()
        zero = jnp.zeros((8, LANE), f32)
        side = lax.div(ct, tiles // 2)
        spot = lax.rem(ct, tiles // 2)
        for var in range(variables):
            for t in range(row_count // 8):
                rows = []
                for lev in range(levels):
                    base = (lev * variables + var) * row_count + t * 8
                    rows.append(done[base : base + 8, :])
                _, ends = level_sweeps(rows, lambda lev: vert[lev * variables + var], [zero, zero])
                for k in range(2):
                    start = (var * 2 + side) * size + k * depth + spot * row_count + t * 8
                    sums[pl.ds(pl.multiple_of(start, 8), 8), :] = ends[k]

    for target in range(2 * variables):
        start = target * size + 2 * depth
        sums[start : start + 8, :] = coef[target // 2]
    for ct in range(tiles):
        pltpu.make_async_copy(field.at[ct], out.at[ct], out_sem.at[ct]).wait()


def lat_states(low, high, decay, states, vert, coef, row_count, groups, variables):
    tiles, rows = low.shape[0], 2 * low.shape[1]
    size = 2 * variables * (tiles * row_count + 8)
    whole = pl.BlockSpec(memory_space=pltpu.VMEM)
    any_space = pl.BlockSpec(memory_space=pl.ANY)
    return pl.pallas_call(
        functools.partial(lat_states_kernel, row_count, groups, variables),
        out_shape=(
            jax.ShapeDtypeStruct((tiles, rows, LANE), f32),
            jax.ShapeDtypeStruct((size, LANE), f32),
        ),
        in_specs=[any_space, any_space, whole, whole, pl.BlockSpec(memory_space=pltpu.SMEM), whole],
        out_specs=(any_space, whole),
        scratch_shapes=[
            pltpu.VMEM((tiles, rows, LANE), f32),
            pltpu.SemaphoreType.DMA((2, tiles)),
            pltpu.SemaphoreType.DMA((tiles,)),
        ],
        compiler_params=vmem(60),
        cost_estimate=cost(0, 12 << 20),
        name="lat_states",
    )(low, high, decay, states, vert, coef)


def level_exchange_kernel(sums, out, beside, merged, arrived, replies, entering, passed, *sems):
    pair_send, pair_recv, hub_send, hub_recv, back_send, back_recv, last_send, last_recv = sems
    band = lax.axis_index("band")
    chip, core = band // 2, band % 2
    depth = out.shape[1] // 2
    tail = 2 * depth
    mine_first = core * 4

    def other(step):
        return lax.rem(chip + step, 4) * 2 + core

    def remote(src, dst, send, recv, target):
        return pltpu.make_async_remote_copy(
            src_ref=src,
            dst_ref=dst,
            send_sem=send,
            recv_sem=recv,
            device_id={"band": target},
            device_id_type=pl.DeviceIdType.MESH,
        )

    sibling = chip * 2 + (1 - core)
    barrier = pltpu.get_barrier_semaphore()
    for target in [sibling] + [other(step) for step in (1, 2, 3)]:
        pl.semaphore_signal(
            barrier, inc=1, device_id={"band": target}, device_id_type=pl.DeviceIdType.MESH
        )
    pl.semaphore_wait(barrier, 4)

    pair = remote(
        sums.at[pl.ds((1 - core) * 4, 4)], beside, pair_send.at[0], pair_recv.at[0], sibling
    )
    pair.start()
    pair.wait_recv()

    def lower(a, b):
        return jnp.where(core == 0, a, b)

    def row(ref, chunk, at):
        return jnp.broadcast_to(ref[chunk, at : at + 1, :], (8, LANE))

    def bands_of(chunk, at):
        a, b = sums[mine_first + chunk, at, :], beside[chunk, at, :]
        return lower(a, b), lower(b, a)

    def coefficients(chunk):
        both = []
        for at in (tail, tail + 1):
            a, b = row(sums, mine_first + chunk, at), row(beside, chunk, at)
            both.append((lower(a, b), lower(b, a)))
        return both

    def merge(chunk):
        (full0, full1), (both0, both1) = coefficients(chunk)

        @pl.loop(0, depth // 8)
        def _(t):
            at = pl.ds(pl.multiple_of(t * 8, 8), 8)
            later = pl.ds(pl.multiple_of(depth + t * 8, 8), 8)
            up0, up1 = bands_of(chunk, at)
            down0, down1 = bands_of(chunk, later)
            merged[chunk, at, :] = full1 * up0 + up1
            merged[chunk, later, :] = down0 + full0 * (down1 + both1 * up0)

        index = lax.broadcasted_iota(jnp.int32, (8, LANE), 0)
        full = full0 * full1
        both = both0 + full0 * both1 * full0
        merged[chunk, tail : tail + 8, :] = jnp.where(index == 0, full, both)

    sends = []
    for step in (1, 2, 3):
        chunk = lax.rem(chip + step, 4)
        merge(chunk)
        copy = remote(
            merged.at[chunk], arrived.at[chip], hub_send.at[step - 1], hub_recv.at[step - 1], other(step)
        )
        copy.start()
        sends.append(copy)
    merge(chip)
    arrived[chip] = merged[chip]
    for copy in sends:
        copy.wait_recv()

    full = [row(arrived, c, tail) for c in range(4)]
    both = [row(arrived, c, tail + 1) for c in range(4)]

    @pl.loop(0, depth // 8)
    def _(t):
        at = pl.ds(pl.multiple_of(t * 8, 8), 8)
        later = pl.ds(pl.multiple_of(depth + t * 8, 8), 8)
        state = jnp.zeros((8, LANE), f32)
        ups = []
        for c in range(4):
            ups.append(state)
            replies[c, at, :] = state
            state = full[c] * state + arrived[c, at, :]
        state = jnp.zeros((8, LANE), f32)
        for c in (3, 2, 1, 0):
            replies[c, later, :] = state
            state = full[c] * state + (arrived[c, later, :] + both[c] * ups[c])

    backs = []
    for step in (1, 2, 3):
        copy = remote(
            replies.at[lax.rem(chip + step, 4)],
            entering.at[chip],
            back_send.at[step - 1],
            back_recv.at[step - 1],
            other(step),
        )
        copy.start()
        backs.append(copy)
    entering[chip] = replies[chip]
    for copy in backs:
        copy.wait_recv()

    for chunk in range(4):
        (full0, full1), (both0, both1) = coefficients(chunk)

        @pl.loop(0, depth // 8)
        def _(t):
            at = pl.ds(pl.multiple_of(t * 8, 8), 8)
            later = pl.ds(pl.multiple_of(depth + t * 8, 8), 8)
            up0, _ = bands_of(chunk, at)
            _, down1 = bands_of(chunk, later)
            first = entering[chunk, at, :]
            last = entering[chunk, later, :]
            middle = full0 * first + up0
            turned = full1 * last + (down1 + both1 * middle)
            out[mine_first + chunk, at, :] = lower(first, middle)
            out[mine_first + chunk, later, :] = lower(turned, last)
            passed[chunk, at, :] = lower(middle, first)
            passed[chunk, later, :] = lower(last, turned)

    final = remote(passed, out.at[pl.ds(mine_first, 4)], last_send.at[0], last_recv.at[0], sibling)
    final.start()
    pair.wait_send()
    for copy in sends + backs:
        copy.wait_send()
    final.wait()


def level_exchange(sums):
    bands, size, _ = sums.shape
    depth = (size - 8) // 2
    whole = pl.BlockSpec(memory_space=pltpu.VMEM)
    dma = pltpu.SemaphoreType.DMA
    return pl.pallas_call(
        level_exchange_kernel,
        out_shape=jax.ShapeDtypeStruct((bands, 2 * depth, LANE), f32),
        in_specs=[whole],
        out_specs=whole,
        scratch_shapes=[
            pltpu.VMEM((4, size, LANE), f32),
            pltpu.VMEM((4, size, LANE), f32),
            pltpu.VMEM((4, size, LANE), f32),
            pltpu.VMEM((4, 2 * depth, LANE), f32),
            pltpu.VMEM((4, 2 * depth, LANE), f32),
            pltpu.VMEM((4, 2 * depth, LANE), f32),
            dma((1,)),
            dma((1,)),
            dma((3,)),
            dma((3,)),
            dma((3,)),
            dma((3,)),
            dma((1,)),
            dma((1,)),
        ],
        compiler_params=pltpu.CompilerParams(
            vmem_limit_bytes=60 << 20, collective_id=0, has_side_effects=True
        ),
        cost_estimate=cost(0, 3 << 20),
        name="level_exchange",
    )(sums)


def level_states_kernel(source, vert, states, out, x, result, in_sem, sem):
    tiles, levels, variables, row_count, _ = x.shape
    fetches = [
        pltpu.make_async_copy(source.at[:, :, var], x.at[:, :, var], in_sem.at[var])
        for var in range(variables)
    ]
    for fetch in fetches:
        fetch.start()
    writes = []
    for var in range(variables):
        fetches[var].wait()
        decay = [vert[lev * variables + var] for lev in range(levels)]
        for ct in range(tiles):
            for t in range(row_count // 8):
                at = slice(t * 8, t * 8 + 8)
                rows = [x[ct, lev, var, at, :] for lev in range(levels)]
                starts = [states[var, ct // (tiles // 2), k, ct % (tiles // 2), at, :] for k in range(2)]
                rows, _ = level_sweeps(rows, lambda lev: decay[lev], starts)
                for lev in range(levels):
                    result[lev, var, at, ct * LANE : (ct + 1) * LANE] = rows[lev]
        write = pltpu.make_async_copy(result.at[:, var], out.at[:, var], sem.at[var])
        write.start()
        writes.append(write)
    for write in writes:
        write.wait()


def level_states(x, vert, states, shape):
    levels, variables, row_count, columns = shape
    tiles = columns // LANE
    whole = pl.BlockSpec(memory_space=pltpu.VMEM)
    return pl.pallas_call(
        level_states_kernel,
        out_shape=jax.ShapeDtypeStruct(shape, f32),
        in_specs=[pl.BlockSpec(memory_space=pl.ANY), pl.BlockSpec(memory_space=pltpu.SMEM), whole],
        out_specs=pl.BlockSpec(memory_space=pl.ANY),
        scratch_shapes=[
            pltpu.VMEM((tiles, levels, variables, row_count, LANE), f32),
            pltpu.VMEM(shape, f32),
            pltpu.SemaphoreType.DMA((variables,)),
            pltpu.SemaphoreType.DMA((variables,)),
        ],
        compiler_params=vmem(60),
        cost_estimate=cost(0, 11 << 20),
        name="level_states",
    )(x.reshape(tiles, levels, variables, row_count, LANE), vert, states)


def level_coefficients(decays):
    levels = decays.shape[0]
    state, down = jnp.ones_like(decays[0]), []
    for r in range(levels):
        state = decays[r] * state
        down.append(state)
    full = state
    state = jnp.zeros_like(full)
    for r in range(levels - 1, -1, -1):
        state = down[r] + decays[r] * (state - down[r])
    both = jnp.stack([full, state], axis=1)
    both = jnp.pad(both, ((0, 0), (0, 6)))
    return jnp.broadcast_to(both[:, :, None], both.shape + (LANE,))


def per_device(background, obs_columns, obs_owner, obs_cell, lat_length, lon_length, vert_length):
    level_count, var_count, row_count, lon_count = background.shape
    sub_count = lax.axis_size("sub")
    band_count = lax.axis_size("band")
    sub_index = lax.axis_index("sub")
    groups = level_count * var_count
    tiles = lon_count // LANE
    tile_field = background.reshape(groups * row_count, lon_count)
    owners = obs_owner[:, 0]
    capacity = 2 * owners.shape[0] // sub_count

    ranks = route_ranks(owners, sub_count)
    row, column = obs_cell // lon_count, obs_cell % lon_count
    place = ((row // 4) * lon_count + column) * 4 + row % 4
    table = jnp.stack([owners, ranks, place] + [jnp.zeros_like(place)] * 5)
    lines = capacity // LANE
    message = pack(owners * capacity + ranks, table, obs_columns, sub_count)
    got = lax.all_to_all(message.reshape(sub_count, -1, LANE), "sub", 0, 0, tiled=True)

    vert_decay = jnp.exp(-1.0 / vert_length)
    coef = level_coefficients(vert_decay)
    vert_decay = vert_decay.reshape(groups)

    lat_all = jnp.exp(-1.0 / lat_length).reshape(groups, sub_count, row_count)
    own_lat = lax.dynamic_index_in_dim(lat_all, sub_index, 1, False)
    own_lat = own_lat.T.reshape(row_count * groups, 1)
    own_lat = jnp.concatenate([own_lat, 1.0 - own_lat])
    decay = jnp.broadcast_to(own_lat, (2 * row_count * groups, LANE))
    hub_lat = lax.dynamic_index_in_dim(lat_all, sub_index, 0, False)
    hub_lat = jnp.pad(hub_lat.T, ((0, 0), (0, LANE - sub_count)))

    lengths = lon_length.reshape(groups)
    weights = lon_weights(lengths, lon_count)
    own_weights = [lax.dynamic_slice_in_dim(w, sub_index, 1, 0) for w in weights]

    got, weights = lax.optimization_barrier((got, weights))
    places = got[:, capacity // 4 : capacity // 4 + lines, :].reshape(-1).astype(jnp.int32)
    quarters = (places & 3).astype(f32).reshape(sub_count, 4, capacity // 4)
    quarters = jnp.pad(quarters, ((0, 0), (0, 4), (0, 0)))
    forced, moments = force(places >> 2, got, quarters, tile_field, decay, row_count, groups)
    moments = lax.all_to_all(
        moments.reshape(sub_count, 4 * tiles, LANE), "sub", 0, 0, tiled=True
    )
    low = lon_filter(forced, weights, row_count, 0)
    moments, low = lax.optimization_barrier((moments, low))
    states = hub(hub_lat, moments.reshape(-1, LANE), own_weights)
    states, forced = lax.optimization_barrier((states, forced))
    states = lax.all_to_all(states.reshape(sub_count, 4 * tiles, LANE), "sub", 0, 0, tiled=True)
    high = lon_filter(forced, weights, row_count, 1)
    smooth, sums = lat_states(
        low, high, decay, states.reshape(-1, LANE), vert_decay, coef, row_count, groups, var_count
    )
    entering = level_exchange(sums.reshape(band_count, -1, LANE))
    return level_states(
        smooth,
        vert_decay,
        entering.reshape(var_count, 2, 2, tiles // 2, row_count, LANE),
        background.shape,
    )


def solution(mesh):
    placed = (
        P("band", None, "sub", None),
        P("band", None, "sub"),
        P("sub", None),
        P("sub"),
        P("band", None, None),
        P("band", None),
        P("band", None),
    )
    return jax.shard_map(
        per_device,
        mesh=mesh,
        in_specs=placed,
        out_specs=P("band", None, "sub", None),
        check_vma=False,
    )
```

```python
import functools

import jax
import jax.numpy as jnp
from jax import lax
from jax.experimental import pallas as pl
from jax.experimental.pallas import tpu as pltpu
from jax.sharding import PartitionSpec as P

LANE = 128
f32 = jnp.float32
bf16 = jnp.bfloat16


def vmem(mib):
    return pltpu.CompilerParams(vmem_limit_bytes=mib << 20)


def cost(flops, moved):
    return pl.CostEstimate(flops=flops, bytes_accessed=moved, transcendentals=0)


def route_ranks(owners, sub_count):
    count = owners.shape[0]
    block = 128
    owner_block = owners.reshape(count // block, block)
    match = (owner_block[:, :, None] == jnp.arange(sub_count, dtype=jnp.int32)).astype(bf16)
    position = jnp.arange(block)
    lower = (position[:, None] > position[None, :]).astype(bf16)
    ahead = jnp.einsum("ij,bjo->bio", lower, match, preferred_element_type=f32)
    totals = jnp.sum(match.astype(f32), axis=1)
    base = jnp.cumsum(totals, axis=0) - totals
    rank = jnp.sum((ahead + base[:, None, :]) * match.astype(f32), axis=2)
    return rank.reshape(count).astype(jnp.int32)


def pack_kernel(slots, table, values, packed, rows, big):
    levels, _, count = values.shape
    total = big.shape[0]
    targets = total // 256
    size = packed.shape[0] // targets

    @pl.loop(0, total // 64)
    def _(i):
        big[pl.ds(pl.multiple_of(i * 64, 64), 64), :] = jnp.zeros((64, LANE), f32)

    for j in range(count // LANE):
        part = jnp.concatenate(
            [values[lev, :, j * LANE : (j + 1) * LANE] for lev in range(levels)], axis=0
        )
        rows[j * LANE : (j + 1) * LANE, :] = jnp.concatenate([part] * 4, axis=0).T

    owner, rank, place = table[0:1, :], table[1:2, :], table[2:3, :]
    mine = owner == lax.broadcasted_iota(jnp.int32, (targets, count), 0)
    spot = (rank == lax.broadcasted_iota(jnp.int32, (256, count), 0)).astype(f32).astype(bf16)

    def put(half):
        left = jnp.where(mine, half, 0).astype(f32).astype(bf16)
        return lax.dot_general(
            left, spot, (((1,), (1,)), ((), ())), preferred_element_type=f32
        )

    cells = put(lax.shift_right_logical(place, 8)) * 256.0 + put(place & 255)
    for half in range(2):
        packed[pl.ds(64 + half, targets, stride=size), :] = cells[:, half * LANE : (half + 1) * LANE]
    for extra in range(66, size):
        packed[pl.ds(extra, targets, stride=size), :] = jnp.zeros((targets, LANE), f32)

    step = 16

    @pl.loop(0, count // step)
    def _(i):
        for u in range(step):
            j = i * step + u
            big[pl.ds(slots[j], 1), :] = rows[pl.ds(j, 1), :]

    quarter = lax.broadcasted_iota(jnp.int32, (64, LANE), 1) // 32

    @pl.loop(0, targets)
    def _(d):
        start = pl.multiple_of(d * 256, 256)
        out = big[pl.ds(start, 64), :]
        for k in range(1, 4):
            out = jnp.where(quarter == k, big[pl.ds(start + 64 * k, 64), :], out)
        packed[pl.ds(pl.multiple_of(d * size, 8), 64), :] = out


def pack(slots, table, values, targets):
    count = values.shape[2]
    total = targets * 256
    whole = pl.BlockSpec(memory_space=pltpu.VMEM)
    return pl.pallas_call(
        pack_kernel,
        out_shape=jax.ShapeDtypeStruct((targets * 72, LANE), f32),
        in_specs=[pl.BlockSpec(memory_space=pltpu.SMEM), whole, whole],
        out_specs=whole,
        scratch_shapes=[pltpu.VMEM((count, LANE), f32), pltpu.VMEM((total, LANE), f32)],
        compiler_params=vmem(60),
        cost_estimate=cost(0, 4 << 20),
        name="pack",
    )(slots, table, values)


def lat_sweeps(sets, decays, starts):
    count = len(sets[0])
    ends = [[] for _ in sets]
    for sweep in range(4):
        order = range(count) if sweep % 2 == 0 else range(count - 1, -1, -1)
        states = [start[sweep] for start in starts]
        outs = [[None] * count for _ in sets]
        for r in order:
            for i, rows in enumerate(sets):
                a, rest = decays[i](r)
                states[i] = a * states[i] + rest * rows[r]
                outs[i][r] = states[i]
        for i in range(len(sets)):
            ends[i].append(states[i])
        sets = outs
    return sets, ends


def decay_of_octet(decay, groups, o):
    rows = decay.shape[0] // 2

    def pair(r):
        at = r * groups + o * 8
        return decay[at : at + 8, :], decay[rows + at : rows + at + 8, :]

    return pair


CHAINS = 8
SIDE = 1


def forced_kernel(row_count, groups, places, got, quarters, background, decay, forced, moments, spread, field, sem, out_sem, *chains):
    total = spread.shape[0]
    depth = chains[0].shape[0]
    sources = got.shape[0]
    tiles = forced.shape[0]
    fetches = [
        pltpu.make_async_copy(
            background.at[:, ct * LANE : (ct + 1) * LANE], field.at[ct], sem.at[ct]
        )
        for ct in range(tiles)
    ]
    for fetch in fetches:
        fetch.start()

    @pl.loop(0, depth // 64)
    def _(i):
        at = pl.ds(pl.multiple_of(i * 64, 64), 64)
        for chain in chains:
            chain[at, :] = jnp.zeros((64, LANE), f32)

    lane = lax.broadcasted_iota(jnp.int32, (8, LANE), 1) // 32
    pick = (lane == lax.broadcasted_iota(jnp.int32, (8, LANE), 0)).astype(bf16)
    quarter = lax.broadcasted_iota(jnp.int32, (64, LANE), 1) // 32
    wanted = quarter.astype(f32)

    def turns(x):
        return [x] + [pltpu.roll(x, 32 * k, 1) for k in range(1, 4)]

    def repeat(turned, k):
        out = turned[(3 - k) % 4]
        for q in range(3):
            out = jnp.where(quarter == q, turned[(q - k) % 4], out)
        return out

    @pl.loop(0, sources)
    def _(d):
        part = turns(got[d, :64, :])
        mark = turns(
            lax.dot_general(
                quarters[d].astype(bf16), pick, (((0,), (0,)), ((), ())), preferred_element_type=f32
            )
        )
        for k in range(4):
            one = jnp.where(repeat(mark, k) == wanted, repeat(part, k), 0.0)
            spread[pl.ds(pl.multiple_of(d * 256 + k * 64, 64), 64), :] = one

    step = 4

    @pl.loop(0, total // (CHAINS * step))
    def _(i):
        for u in range(step):
            spots = [(i * step + u) * CHAINS + c for c in range(CHAINS)]
            where = [pl.ds(places[j], 1) for j in spots]
            adds = [spread[pl.ds(j, 1), :] for j in spots]
            olds = [chains[c][where[c], :] for c in range(CHAINS)]
            for c in range(CHAINS):
                chains[c][where[c], :] = olds[c] + adds[c]

    for fetch in fetches:
        fetch.wait()
    columns = depth // (row_count // 4)

    @pl.loop(0, tiles)
    def _(ct):
        out = field.at[ct]
        for rr in range(row_count // 4):
            at = pl.ds(pl.multiple_of(rr * columns + ct * LANE, LANE), LANE)
            parts = [chain[at, :] for chain in chains]
            while len(parts) > 1:
                parts = [a + b for a, b in zip(parts[::2], parts[1::2])]
            turned = parts[0].T
            for q in range(4):
                for o in range(groups // 8):
                    at = pl.ds(o * 8 * row_count + rr * 4 + q, 8, stride=row_count)
                    first = q * groups + o * 8
                    out[at, :] = out[at, :] + turned[first : first + 8, :]
        pltpu.make_async_copy(field.at[ct], forced.at[ct], out_sem.at[ct]).start()
        zero = jnp.zeros((8, LANE), f32)
        per_group = moments.shape[0] // groups
        for first in range(0, groups // 8, SIDE):
            octets = range(first, first + SIDE)
            sets = [
                [
                    out[pl.ds(o * 8 * row_count + r, 8, stride=row_count), :]
                    for r in range(row_count)
                ]
                for o in octets
            ]
            _, ends = lat_sweeps(
                sets, [decay_of_octet(decay, groups, o) for o in octets], [[zero] * 4] * SIDE
            )
            for i, o in enumerate(octets):
                for k in range(4):
                    start = o * 8 * per_group + k * (per_group // 4) + ct
                    moments[pl.ds(start, 8, stride=per_group), :] = ends[i][k]

    for ct in range(tiles):
        pltpu.make_async_copy(field.at[ct], forced.at[ct], out_sem.at[ct]).wait()


def force(places, got, quarters, background, decay, row_count, groups):
    rows, columns = background.shape
    tiles = columns // LANE
    total = places.shape[0]
    depth = rows * columns // LANE
    whole = pl.BlockSpec(memory_space=pltpu.VMEM)
    return pl.pallas_call(
        functools.partial(forced_kernel, row_count, groups),
        out_shape=(
            jax.ShapeDtypeStruct((tiles, rows, LANE), f32),
            jax.ShapeDtypeStruct((groups * 4 * tiles, LANE), f32),
        ),
        in_specs=[
            pl.BlockSpec(memory_space=pltpu.SMEM),
            whole,
            whole,
            pl.BlockSpec(memory_space=pl.ANY),
            whole,
        ],
        out_specs=(pl.BlockSpec(memory_space=pl.ANY), whole),
        scratch_shapes=[
            pltpu.VMEM((total, LANE), f32),
            pltpu.VMEM((tiles, rows, LANE), f32),
            pltpu.SemaphoreType.DMA((tiles,)),
            pltpu.SemaphoreType.DMA((tiles,)),
        ]
        + [pltpu.VMEM((depth, LANE), f32)] * CHAINS,
        compiler_params=vmem(58),
        cost_estimate=cost(0, 16 << 20),
        name="force",
    )(places, got, quarters, background, decay)


def lon_weights(length, columns):
    blocks = columns // LANE
    length = length[:, None, None]
    kappa = jnp.tanh(0.5 / length)
    beta = kappa * kappa
    alpha = beta / jnp.tanh(1.0 / length)
    i = jnp.arange(LANE, dtype=f32)

    def power(n):
        return jnp.exp(-n / length)

    gap = jnp.abs(i[:, None] - i[None, :])[None]
    local = (alpha + beta * gap) * power(gap)
    up, down = i[None, :, None], (LANE - 1.0) - i[None, :, None]
    sums = jnp.concatenate(
        [power(down), down * power(down), power(up), up * power(up)], axis=2
    )
    sums = jnp.pad(sums, ((0, 0), (0, 0), (0, LANE - 4)))
    first = jnp.concatenate([local, sums], axis=2)
    index = jnp.arange(LANE)
    src, dst = index[:, None], index[None, :]
    source, target = src // 4, dst // 4
    backward = (src % 4) >= 2
    steps = jnp.where(backward, source - target - 1, target - source - 1) % blocks
    gap = (LANE * steps).astype(f32)[None]
    turn = power(float(columns))
    left = -jnp.expm1(-float(columns) / length)
    same = power(gap) / left
    cross = (gap + columns * turn / left) * same
    used = (source < blocks) & (target < blocks)
    mix = jnp.where((used & (src % 4 == dst % 4))[None], same, 0.0)
    mix = jnp.where((used & (src % 2 == 0) & (dst % 4 == src % 4 + 1))[None], cross, mix)
    near, far = i[None, None, :] + 1.0, LANE - i[None, None, :]
    back = jnp.concatenate(
        [
            (alpha + beta * near) * power(near),
            beta * power(near),
            (alpha + beta * far) * power(far),
            beta * power(far),
        ],
        axis=1,
    )
    back = jnp.pad(back, ((0, 0), (0, LANE - 4), (0, 0)))
    return thirds(first), thirds(mix), thirds(back)


def thirds(w):
    high = lax.reduce_precision(w, 8, 7)
    low = (w - high).astype(bf16)
    high = high.astype(bf16)
    return jnp.concatenate([high, high, low], axis=1)


def dot3(x, w):
    high = x.astype(bf16)
    low = (x - high.astype(f32)).astype(bf16)
    return jnp.dot(jnp.concatenate([high, low, high], axis=1), w, preferred_element_type=f32)


def lon_apply(parts, first, mix, back):
    count, blocks = parts[0].shape[0], len(parts)
    both = dot3(jnp.concatenate(parts, axis=0), first)
    local, sums = both[:, :LANE], both[:, LANE:]
    line = sums[:count]
    for b in range(1, blocks):
        line = line + pltpu.roll(sums[b * count : (b + 1) * count], 4 * b, 1)
    states = dot3(line, mix)
    spread = jnp.concatenate(
        [states] + [pltpu.roll(states, LANE - 4 * b, 1) for b in range(1, blocks)], axis=0
    )
    out = local + dot3(spread, back)
    return [out[b * count : (b + 1) * count] for b in range(blocks)]


LON_STEP = 4


def hub_coefficients(decay):
    count = decay.shape[0]
    coef = [decay[r : r + 1, :] for r in range(count)]

    def forward(rows):
        state, out = jnp.zeros((1, LANE), f32), []
        for r in range(count):
            state = rows[r] + coef[r] * (state - rows[r])
            out.append(state)
        return out

    def backward(rows):
        state, out = jnp.zeros((1, LANE), f32), [None] * count
        for r in range(count - 1, -1, -1):
            state = rows[r] + coef[r] * (state - rows[r])
            out[r] = state
        return out

    state, down = jnp.ones((1, LANE), f32), []
    for r in range(count):
        state = coef[r] * state
        down.append(state)
    full = state
    state, up = jnp.ones((1, LANE), f32), [None] * count
    for r in range(count - 1, -1, -1):
        state = coef[r] * state
        up[r] = state
    bp = backward(down)
    fbp = forward(bp)
    bfbp = backward(fbp)
    fq = forward(up)
    bfq = backward(fq)
    return full, bp[0], fbp[-1], bfbp[0], fq[-1], bfq[0]


def state_exchange_kernel(
    count, field, moments, decay, first, mix, back, own_first, own_mix, own_back, out, states,
    arrived, replies, work, xs, ws, ms, bs, sems, out_sem, send, recv, back_send, back_recv,
):
    tiles, rows, _ = out.shape
    blocks = arrived.shape[0]
    me = lax.axis_index("sub")
    steps = rows // count // LON_STEP
    size = LON_STEP * count

    def fetches(i):
        group = i * LON_STEP
        at = pl.ds(pl.multiple_of(group * count, 8), size)
        inside = pl.ds(group, LON_STEP)
        return [
            pltpu.make_async_copy(field.at[:, at], xs.at[:, at], sems.at[0, i]),
            pltpu.make_async_copy(first.at[inside], ws.at[inside], sems.at[1, i]),
            pltpu.make_async_copy(mix.at[inside], ms.at[inside], sems.at[2, i]),
            pltpu.make_async_copy(back.at[inside], bs.at[inside], sems.at[3, i]),
        ]

    def write(i):
        at = pl.ds(pl.multiple_of(i * size, 8), size)
        return pltpu.make_async_copy(xs.at[:, at], out.at[:, at], out_sem.at[i])

    for i in range(steps):
        for fetch in fetches(i):
            fetch.start()

    def lon_steps(start, stop):
        @pl.loop(start, stop)
        def _(i):
            for fetch in fetches(i):
                fetch.wait()
            for u in range(LON_STEP):
                g = i * LON_STEP + u
                at = pl.ds(pl.multiple_of(g * count, 8), count)
                parts = lon_apply([xs[b, at, :] for b in range(tiles)], ws[g], ms[g], bs[g])
                for b in range(tiles):
                    xs[b, at, :] = parts[b]
            write(i).start()

    barrier = pltpu.get_barrier_semaphore()

    @pl.loop(1, blocks)
    def _(step):
        target = lax.rem(me + step, blocks)
        pl.semaphore_signal(
            barrier, inc=1, device_id={"sub": target}, device_id_type=pl.DeviceIdType.MESH
        )

    pl.semaphore_wait(barrier, blocks - 1)

    def outward(step):
        target = lax.rem(me + step, blocks)
        return pltpu.make_async_remote_copy(
            src_ref=moments.at[target],
            dst_ref=arrived.at[me],
            send_sem=send.at[step - 1],
            recv_sem=recv.at[step - 1],
            device_id={"sub": target},
            device_id_type=pl.DeviceIdType.MESH,
        )

    def homeward(step):
        target = lax.rem(me + step, blocks)
        return pltpu.make_async_remote_copy(
            src_ref=replies.at[target],
            dst_ref=states.at[me],
            send_sem=back_send.at[step - 1],
            recv_sem=back_recv.at[step - 1],
            device_id={"sub": target},
            device_id_type=pl.DeviceIdType.MESH,
        )

    @pl.loop(1, blocks)
    def _(step):
        outward(step).start()

    arrived[me] = moments[me]
    lon_steps(0, steps // 2)

    @pl.loop(1, blocks)
    def _(step):
        outward(step).wait_recv()

    full, t21, t31, t41, t32, t42 = hub_coefficients(decay)

    def at(table, d):
        return jnp.broadcast_to(table[:, d : d + 1], (tiles, LANE))

    def moment(d, k):
        return arrived[d, k * tiles : (k + 1) * tiles, :]

    carry = jnp.zeros((tiles, LANE), f32)
    s = [[None] * blocks for _ in range(4)]
    for d in range(blocks):
        s[0][d] = carry
        carry = at(full, d) * carry + moment(d, 0)
    carry = jnp.zeros((tiles, LANE), f32)
    for d in range(blocks - 1, -1, -1):
        s[1][d] = carry
        carry = at(full, d) * carry + (moment(d, 1) + at(t21, d) * s[0][d])
    carry = jnp.zeros((tiles, LANE), f32)
    for d in range(blocks):
        s[2][d] = carry
        carry = at(full, d) * carry + (
            moment(d, 2) + at(t31, d) * s[0][d] + at(t32, d) * s[1][d]
        )
    carry = jnp.zeros((tiles, LANE), f32)
    for d in range(blocks - 1, -1, -1):
        s[3][d] = carry
        carry = at(full, d) * carry + (
            moment(d, 3) + at(t41, d) * s[0][d] + at(t42, d) * s[1][d] + at(t21, d) * s[2][d]
        )
    for k in range(4):
        for d in range(blocks):
            for t in range(tiles):
                work[t, k * blocks + d : k * blocks + d + 1, :] = s[k][d][t : t + 1, :]
    done = lon_apply([work[t] for t in range(tiles)], own_first[0], own_mix[0], own_back[0])
    for t in range(tiles):
        for k in range(4):
            replies[:, k * tiles + t, :] = done[t][k * blocks : (k + 1) * blocks]

    @pl.loop(1, blocks)
    def _(step):
        homeward(step).start()

    states[me] = replies[me]
    lon_steps(steps // 2, steps)

    @pl.loop(1, blocks)
    def _(step):
        homeward(step).wait_recv()

    @pl.loop(1, blocks)
    def _(step):
        outward(step).wait_send()
        homeward(step).wait_send()

    for i in range(steps):
        write(i).wait()


def state_exchange(field, moments, decay, weights, own_weights, row_count):
    tiles, rows, _ = field.shape
    blocks, depth, _ = moments.shape
    groups = rows // row_count
    steps = groups // LON_STEP
    any_space = pl.BlockSpec(memory_space=pl.ANY)
    whole = pl.BlockSpec(memory_space=pltpu.VMEM)
    dma = pltpu.SemaphoreType.DMA
    return pl.pallas_call(
        functools.partial(state_exchange_kernel, row_count),
        out_shape=(
            jax.ShapeDtypeStruct(field.shape, f32),
            jax.ShapeDtypeStruct(moments.shape, f32),
        ),
        in_specs=[any_space, whole, whole] + [any_space] * 3 + [whole] * 3,
        out_specs=(any_space, whole),
        scratch_shapes=[
            pltpu.VMEM(moments.shape, f32),
            pltpu.VMEM(moments.shape, f32),
            pltpu.VMEM((tiles, 4 * blocks, LANE), f32),
            pltpu.VMEM(field.shape, f32),
        ]
        + [pltpu.VMEM(w.shape, w.dtype) for w in weights]
        + [dma((4, steps)), dma((steps,))]
        + [dma((blocks - 1,))] * 4,
        compiler_params=pltpu.CompilerParams(
            vmem_limit_bytes=60 << 20, collective_id=1, has_side_effects=True
        ),
        cost_estimate=cost(6 * rows * tiles * LANE * 3 * LANE, 60 << 20),
        name="state_exchange",
    )(field, moments, decay, *weights, *own_weights)


def level_sweeps(rows, decay, starts):
    count = len(rows)
    ends = []
    for sweep in range(2):
        order = range(count) if sweep == 0 else range(count - 1, -1, -1)
        state = starts[sweep]
        out = [None] * count
        for r in order:
            state = decay(r) * state + (1.0 - decay(r)) * rows[r]
            out[r] = state
        ends.append(state)
        rows = out
    return rows, ends


def lat_states_kernel(row_count, groups, variables, source, decay, states, vert, coef, out, sums, field, sems, out_sem):
    tiles = out.shape[0]
    per_group = states.shape[0] // groups
    levels = groups // variables
    depth = tiles // 2 * row_count
    size = sums.shape[0] // (2 * variables)

    def fetch(ct):
        return pltpu.make_async_copy(source.at[ct], field.at[ct], sems.at[ct])

    for ct in range(tiles):
        fetch(ct).start()

    @pl.loop(0, tiles)
    def _(ct):
        fetch(ct).wait()
        done = field.at[ct]
        for first in range(0, groups // 8, SIDE):
            octets = range(first, first + SIDE)
            sets = [
                [
                    done[pl.ds(o * 8 * row_count + r, 8, stride=row_count), :]
                    for r in range(row_count)
                ]
                for o in octets
            ]
            starts = [
                [
                    states[
                        pl.ds(o * 8 * per_group + k * (per_group // 4) + ct, 8, stride=per_group), :
                    ]
                    for k in range(4)
                ]
                for o in octets
            ]
            sets, _ = lat_sweeps(sets, [decay_of_octet(decay, groups, o) for o in octets], starts)
            for i, o in enumerate(octets):
                for r in range(row_count):
                    done[pl.ds(o * 8 * row_count + r, 8, stride=row_count), :] = sets[i][r]
        pltpu.make_async_copy(done, out.at[ct], out_sem.at[ct]).start()
        zero = jnp.zeros((8, LANE), f32)
        side = lax.div(ct, tiles // 2)
        spot = lax.rem(ct, tiles // 2)
        for var in range(variables):
            for t in range(row_count // 8):
                rows = []
                for lev in range(levels):
                    base = (lev * variables + var) * row_count + t * 8
                    rows.append(done[base : base + 8, :])
                _, ends = level_sweeps(rows, lambda lev: vert[lev * variables + var], [zero, zero])
                for k in range(2):
                    start = (var * 2 + side) * size + k * depth + spot * row_count + t * 8
                    sums[pl.ds(pl.multiple_of(start, 8), 8), :] = ends[k]

    for target in range(2 * variables):
        start = target * size + 2 * depth
        sums[start : start + 8, :] = coef[target // 2]
    for ct in range(tiles):
        pltpu.make_async_copy(field.at[ct], out.at[ct], out_sem.at[ct]).wait()


def lat_states(x, decay, states, vert, coef, row_count, groups, variables):
    tiles, rows, _ = x.shape
    size = 2 * variables * (tiles * row_count + 8)
    whole = pl.BlockSpec(memory_space=pltpu.VMEM)
    any_space = pl.BlockSpec(memory_space=pl.ANY)
    return pl.pallas_call(
        functools.partial(lat_states_kernel, row_count, groups, variables),
        out_shape=(
            jax.ShapeDtypeStruct((tiles, rows, LANE), f32),
            jax.ShapeDtypeStruct((size, LANE), f32),
        ),
        in_specs=[any_space, whole, whole, pl.BlockSpec(memory_space=pltpu.SMEM), whole],
        out_specs=(any_space, whole),
        scratch_shapes=[
            pltpu.VMEM((tiles, rows, LANE), f32),
            pltpu.SemaphoreType.DMA((tiles,)),
            pltpu.SemaphoreType.DMA((tiles,)),
        ],
        compiler_params=vmem(60),
        cost_estimate=cost(0, 12 << 20),
        name="lat_states",
    )(x, decay, states, vert, coef)


def level_exchange_kernel(sums, out, beside, merged, arrived, replies, entering, passed, *sems):
    pair_send, pair_recv, hub_send, hub_recv, back_send, back_recv, last_send, last_recv = sems
    band = lax.axis_index("band")
    chip, core = band // 2, band % 2
    depth = out.shape[1] // 2
    tail = 2 * depth
    mine_first = core * 4

    def other(step):
        return lax.rem(chip + step, 4) * 2 + core

    def remote(src, dst, send, recv, target):
        return pltpu.make_async_remote_copy(
            src_ref=src,
            dst_ref=dst,
            send_sem=send,
            recv_sem=recv,
            device_id={"band": target},
            device_id_type=pl.DeviceIdType.MESH,
        )

    sibling = chip * 2 + (1 - core)
    barrier = pltpu.get_barrier_semaphore()
    for target in [sibling] + [other(step) for step in (1, 2, 3)]:
        pl.semaphore_signal(
            barrier, inc=1, device_id={"band": target}, device_id_type=pl.DeviceIdType.MESH
        )
    pl.semaphore_wait(barrier, 4)

    pair = remote(
        sums.at[pl.ds((1 - core) * 4, 4)], beside, pair_send.at[0], pair_recv.at[0], sibling
    )
    pair.start()
    pair.wait_recv()

    def lower(a, b):
        return jnp.where(core == 0, a, b)

    def row(ref, chunk, at):
        return jnp.broadcast_to(ref[chunk, at : at + 1, :], (8, LANE))

    def bands_of(chunk, at):
        a, b = sums[mine_first + chunk, at, :], beside[chunk, at, :]
        return lower(a, b), lower(b, a)

    def coefficients(chunk):
        both = []
        for at in (tail, tail + 1):
            a, b = row(sums, mine_first + chunk, at), row(beside, chunk, at)
            both.append((lower(a, b), lower(b, a)))
        return both

    def merge(chunk):
        (full0, full1), (both0, both1) = coefficients(chunk)

        @pl.loop(0, depth // 8)
        def _(t):
            at = pl.ds(pl.multiple_of(t * 8, 8), 8)
            later = pl.ds(pl.multiple_of(depth + t * 8, 8), 8)
            up0, up1 = bands_of(chunk, at)
            down0, down1 = bands_of(chunk, later)
            merged[chunk, at, :] = full1 * up0 + up1
            merged[chunk, later, :] = down0 + full0 * (down1 + both1 * up0)

        index = lax.broadcasted_iota(jnp.int32, (8, LANE), 0)
        full = full0 * full1
        both = both0 + full0 * both1 * full0
        merged[chunk, tail : tail + 8, :] = jnp.where(index == 0, full, both)

    sends = []
    for step in (1, 2, 3):
        chunk = lax.rem(chip + step, 4)
        merge(chunk)
        copy = remote(
            merged.at[chunk], arrived.at[chip], hub_send.at[step - 1], hub_recv.at[step - 1], other(step)
        )
        copy.start()
        sends.append(copy)
    merge(chip)
    arrived[chip] = merged[chip]
    for copy in sends:
        copy.wait_recv()

    full = [row(arrived, c, tail) for c in range(4)]
    both = [row(arrived, c, tail + 1) for c in range(4)]

    @pl.loop(0, depth // 8)
    def _(t):
        at = pl.ds(pl.multiple_of(t * 8, 8), 8)
        later = pl.ds(pl.multiple_of(depth + t * 8, 8), 8)
        state = jnp.zeros((8, LANE), f32)
        ups = []
        for c in range(4):
            ups.append(state)
            replies[c, at, :] = state
            state = full[c] * state + arrived[c, at, :]
        state = jnp.zeros((8, LANE), f32)
        for c in (3, 2, 1, 0):
            replies[c, later, :] = state
            state = full[c] * state + (arrived[c, later, :] + both[c] * ups[c])

    backs = []
    for step in (1, 2, 3):
        copy = remote(
            replies.at[lax.rem(chip + step, 4)],
            entering.at[chip],
            back_send.at[step - 1],
            back_recv.at[step - 1],
            other(step),
        )
        copy.start()
        backs.append(copy)
    entering[chip] = replies[chip]
    for copy in backs:
        copy.wait_recv()

    for chunk in range(4):
        (full0, full1), (both0, both1) = coefficients(chunk)

        @pl.loop(0, depth // 8)
        def _(t):
            at = pl.ds(pl.multiple_of(t * 8, 8), 8)
            later = pl.ds(pl.multiple_of(depth + t * 8, 8), 8)
            up0, _ = bands_of(chunk, at)
            _, down1 = bands_of(chunk, later)
            first = entering[chunk, at, :]
            last = entering[chunk, later, :]
            middle = full0 * first + up0
            turned = full1 * last + (down1 + both1 * middle)
            out[mine_first + chunk, at, :] = lower(first, middle)
            out[mine_first + chunk, later, :] = lower(turned, last)
            passed[chunk, at, :] = lower(middle, first)
            passed[chunk, later, :] = lower(last, turned)

    final = remote(passed, out.at[pl.ds(mine_first, 4)], last_send.at[0], last_recv.at[0], sibling)
    final.start()
    pair.wait_send()
    for copy in sends + backs:
        copy.wait_send()
    final.wait()


def level_exchange(sums):
    bands, size, _ = sums.shape
    depth = (size - 8) // 2
    whole = pl.BlockSpec(memory_space=pltpu.VMEM)
    dma = pltpu.SemaphoreType.DMA
    return pl.pallas_call(
        level_exchange_kernel,
        out_shape=jax.ShapeDtypeStruct((bands, 2 * depth, LANE), f32),
        in_specs=[whole],
        out_specs=whole,
        scratch_shapes=[
            pltpu.VMEM((4, size, LANE), f32),
            pltpu.VMEM((4, size, LANE), f32),
            pltpu.VMEM((4, size, LANE), f32),
            pltpu.VMEM((4, 2 * depth, LANE), f32),
            pltpu.VMEM((4, 2 * depth, LANE), f32),
            pltpu.VMEM((4, 2 * depth, LANE), f32),
            dma((1,)),
            dma((1,)),
            dma((3,)),
            dma((3,)),
            dma((3,)),
            dma((3,)),
            dma((1,)),
            dma((1,)),
        ],
        compiler_params=pltpu.CompilerParams(
            vmem_limit_bytes=60 << 20, collective_id=0, has_side_effects=True
        ),
        cost_estimate=cost(0, 3 << 20),
        name="level_exchange",
    )(sums)


def level_states_kernel(source, vert, states, out, x, result, in_sem, sem):
    tiles, levels, variables, row_count, _ = x.shape
    fetches = [
        pltpu.make_async_copy(source.at[:, :, var], x.at[:, :, var], in_sem.at[var])
        for var in range(variables)
    ]
    for fetch in fetches:
        fetch.start()
    writes = []
    for var in range(variables):
        fetches[var].wait()
        decay = [vert[lev * variables + var] for lev in range(levels)]
        for ct in range(tiles):
            for t in range(row_count // 8):
                at = slice(t * 8, t * 8 + 8)
                rows = [x[ct, lev, var, at, :] for lev in range(levels)]
                starts = [states[var, ct // (tiles // 2), k, ct % (tiles // 2), at, :] for k in range(2)]
                rows, _ = level_sweeps(rows, lambda lev: decay[lev], starts)
                for lev in range(levels):
                    result[lev, var, at, ct * LANE : (ct + 1) * LANE] = rows[lev]
        write = pltpu.make_async_copy(result.at[:, var], out.at[:, var], sem.at[var])
        write.start()
        writes.append(write)
    for write in writes:
        write.wait()


def level_states(x, vert, states, shape):
    levels, variables, row_count, columns = shape
    tiles = columns // LANE
    whole = pl.BlockSpec(memory_space=pltpu.VMEM)
    return pl.pallas_call(
        level_states_kernel,
        out_shape=jax.ShapeDtypeStruct(shape, f32),
        in_specs=[pl.BlockSpec(memory_space=pl.ANY), pl.BlockSpec(memory_space=pltpu.SMEM), whole],
        out_specs=pl.BlockSpec(memory_space=pl.ANY),
        scratch_shapes=[
            pltpu.VMEM((tiles, levels, variables, row_count, LANE), f32),
            pltpu.VMEM(shape, f32),
            pltpu.SemaphoreType.DMA((variables,)),
            pltpu.SemaphoreType.DMA((variables,)),
        ],
        compiler_params=vmem(60),
        cost_estimate=cost(0, 11 << 20),
        name="level_states",
    )(x.reshape(tiles, levels, variables, row_count, LANE), vert, states)


def level_coefficients(decays):
    levels = decays.shape[0]
    state, down = jnp.ones_like(decays[0]), []
    for r in range(levels):
        state = decays[r] * state
        down.append(state)
    full = state
    state = jnp.zeros_like(full)
    for r in range(levels - 1, -1, -1):
        state = down[r] + decays[r] * (state - down[r])
    both = jnp.stack([full, state], axis=1)
    both = jnp.pad(both, ((0, 0), (0, 6)))
    return jnp.broadcast_to(both[:, :, None], both.shape + (LANE,))


def per_device(background, obs_columns, obs_owner, obs_cell, lat_length, lon_length, vert_length):
    level_count, var_count, row_count, lon_count = background.shape
    sub_count = lax.axis_size("sub")
    band_count = lax.axis_size("band")
    sub_index = lax.axis_index("sub")
    groups = level_count * var_count
    tiles = lon_count // LANE
    tile_field = background.reshape(groups * row_count, lon_count)
    owners = obs_owner[:, 0]
    capacity = 2 * owners.shape[0] // sub_count

    ranks = route_ranks(owners, sub_count)
    row, column = obs_cell // lon_count, obs_cell % lon_count
    place = ((row // 4) * lon_count + column) * 4 + row % 4
    table = jnp.stack([owners, ranks, place] + [jnp.zeros_like(place)] * 5)
    lines = capacity // LANE
    message = pack(owners * capacity + ranks, table, obs_columns, sub_count)
    got = lax.all_to_all(message.reshape(sub_count, -1, LANE), "sub", 0, 0, tiled=True)

    vert_decay = jnp.exp(-1.0 / vert_length)
    coef = level_coefficients(vert_decay)
    vert_decay = vert_decay.reshape(groups)

    lat_all = jnp.exp(-1.0 / lat_length).reshape(groups, sub_count, row_count)
    own_lat = lax.dynamic_index_in_dim(lat_all, sub_index, 1, False)
    own_lat = own_lat.T.reshape(row_count * groups, 1)
    own_lat = jnp.concatenate([own_lat, 1.0 - own_lat])
    decay = jnp.broadcast_to(own_lat, (2 * row_count * groups, LANE))
    hub_lat = lax.dynamic_index_in_dim(lat_all, sub_index, 0, False)
    hub_lat = jnp.pad(hub_lat.T, ((0, 0), (0, LANE - sub_count)))

    lengths = lon_length.reshape(groups)
    weights = lon_weights(lengths, lon_count)
    own_weights = [lax.dynamic_slice_in_dim(w, sub_index, 1, 0) for w in weights]

    got, weights, own_weights = lax.optimization_barrier((got, weights, own_weights))
    places = got[:, capacity // 4 : capacity // 4 + lines, :].reshape(-1).astype(jnp.int32)
    quarters = (places & 3).astype(f32).reshape(sub_count, 4, capacity // 4)
    quarters = jnp.pad(quarters, ((0, 0), (0, 4), (0, 0)))
    forced, moments = force(places >> 2, got, quarters, tile_field, decay, row_count, groups)
    smooth, states = state_exchange(
        forced, moments.reshape(sub_count, 4 * tiles, LANE), hub_lat, weights, own_weights, row_count
    )
    smooth, sums = lat_states(
        smooth, decay, states.reshape(-1, LANE), vert_decay, coef, row_count, groups, var_count
    )
    entering = level_exchange(sums.reshape(band_count, -1, LANE))
    return level_states(
        smooth,
        vert_decay,
        entering.reshape(var_count, 2, 2, tiles // 2, row_count, LANE),
        background.shape,
    )


def solution(mesh):
    placed = (
        P("band", None, "sub", None),
        P("band", None, "sub"),
        P("sub", None),
        P("sub"),
        P("band", None, None),
        P("band", None),
        P("band", None),
    )
    return jax.shard_map(
        per_device,
        mesh=mesh,
        in_specs=placed,
        out_specs=P("band", None, "sub", None),
        check_vma=False,
    )
```

```python
import functools

import jax
import jax.numpy as jnp
from jax import lax
from jax.experimental import pallas as pl
from jax.experimental.pallas import tpu as pltpu
from jax.sharding import PartitionSpec as P

LANE = 128
f32 = jnp.float32
bf16 = jnp.bfloat16


def vmem(mib):
    return pltpu.CompilerParams(vmem_limit_bytes=mib << 20)


def cost(flops, moved):
    return pl.CostEstimate(flops=flops, bytes_accessed=moved, transcendentals=0)


def route_ranks(owners, sub_count):
    count = owners.shape[0]
    block = 128
    owner_block = owners.reshape(count // block, block)
    match = (owner_block[:, :, None] == jnp.arange(sub_count, dtype=jnp.int32)).astype(bf16)
    position = jnp.arange(block)
    lower = (position[:, None] > position[None, :]).astype(bf16)
    ahead = jnp.einsum("ij,bjo->bio", lower, match, preferred_element_type=f32)
    totals = jnp.sum(match.astype(f32), axis=1)
    base = jnp.cumsum(totals, axis=0) - totals
    rank = jnp.sum((ahead + base[:, None, :]) * match.astype(f32), axis=2)
    return rank.reshape(count).astype(jnp.int32)


def pack_kernel(slots, table, values, packed, rows, big):
    levels, _, count = values.shape
    total = big.shape[0]
    targets = total // 256
    size = packed.shape[0] // targets

    @pl.loop(0, total // 64)
    def _(i):
        big[pl.ds(pl.multiple_of(i * 64, 64), 64), :] = jnp.zeros((64, LANE), f32)

    for j in range(count // LANE):
        part = jnp.concatenate(
            [values[lev, :, j * LANE : (j + 1) * LANE] for lev in range(levels)], axis=0
        )
        rows[j * LANE : (j + 1) * LANE, :] = jnp.concatenate([part] * 4, axis=0).T

    owner, rank, place = table[0:1, :], table[1:2, :], table[2:3, :]
    mine = owner == lax.broadcasted_iota(jnp.int32, (targets, count), 0)
    spot = (rank == lax.broadcasted_iota(jnp.int32, (256, count), 0)).astype(f32).astype(bf16)

    def put(half):
        left = jnp.where(mine, half, 0).astype(f32).astype(bf16)
        return lax.dot_general(
            left, spot, (((1,), (1,)), ((), ())), preferred_element_type=f32
        )

    cells = put(lax.shift_right_logical(place, 8)) * 256.0 + put(place & 255)
    for half in range(2):
        packed[pl.ds(64 + half, targets, stride=size), :] = cells[:, half * LANE : (half + 1) * LANE]
    for extra in range(66, size):
        packed[pl.ds(extra, targets, stride=size), :] = jnp.zeros((targets, LANE), f32)

    step = 16

    @pl.loop(0, count // step)
    def _(i):
        for u in range(step):
            j = i * step + u
            big[pl.ds(slots[j], 1), :] = rows[pl.ds(j, 1), :]

    quarter = lax.broadcasted_iota(jnp.int32, (64, LANE), 1) // 32

    @pl.loop(0, targets)
    def _(d):
        start = pl.multiple_of(d * 256, 256)
        out = big[pl.ds(start, 64), :]
        for k in range(1, 4):
            out = jnp.where(quarter == k, big[pl.ds(start + 64 * k, 64), :], out)
        packed[pl.ds(pl.multiple_of(d * size, 8), 64), :] = out


def pack(slots, table, values, targets):
    count = values.shape[2]
    total = targets * 256
    whole = pl.BlockSpec(memory_space=pltpu.VMEM)
    return pl.pallas_call(
        pack_kernel,
        out_shape=jax.ShapeDtypeStruct((targets * 72, LANE), f32),
        in_specs=[pl.BlockSpec(memory_space=pltpu.SMEM), whole, whole],
        out_specs=whole,
        scratch_shapes=[pltpu.VMEM((count, LANE), f32), pltpu.VMEM((total, LANE), f32)],
        compiler_params=vmem(60),
        cost_estimate=cost(0, 4 << 20),
        name="pack",
    )(slots, table, values)


def lat_sweeps(sets, decays, starts):
    count = len(sets[0])
    ends = [[] for _ in sets]
    for sweep in range(4):
        order = range(count) if sweep % 2 == 0 else range(count - 1, -1, -1)
        states = [start[sweep] for start in starts]
        outs = [[None] * count for _ in sets]
        for r in order:
            for i, rows in enumerate(sets):
                a, rest = decays[i](r)
                states[i] = a * states[i] + rest * rows[r]
                outs[i][r] = states[i]
        for i in range(len(sets)):
            ends[i].append(states[i])
        sets = outs
    return sets, ends


def decay_of_octet(decay, groups, o):
    rows = decay.shape[0] // 2

    def pair(r):
        at = r * groups + o * 8
        return decay[at : at + 8, :], decay[rows + at : rows + at + 8, :]

    return pair


CHAINS = 8
SIDE = 1


def forced_kernel(row_count, groups, places, got, quarters, background, decay, forced, moments, spread, field, sem, out_sem, *chains):
    total = spread.shape[0]
    depth = chains[0].shape[0]
    sources = got.shape[0]
    tiles = forced.shape[0]
    fetches = [
        pltpu.make_async_copy(
            background.at[:, ct * LANE : (ct + 1) * LANE], field.at[ct], sem.at[ct]
        )
        for ct in range(tiles)
    ]
    for fetch in fetches:
        fetch.start()

    row = lax.broadcasted_iota(jnp.int32, (8, LANE), 0)
    picks = [(row == k).astype(f32).astype(bf16) for k in range(4)]
    quarter = lax.broadcasted_iota(jnp.int32, (64, LANE), 1) // 32
    wanted = quarter.astype(f32)

    def turns(x):
        return [x] + [pltpu.roll(x, 32 * k, 1) for k in range(1, 4)]

    def repeat(turned, k):
        out = turned[(3 - k) % 4]
        for q in range(3):
            out = jnp.where(quarter == q, turned[(q - k) % 4], out)
        return out

    share = depth // sources
    together = 2

    @pl.loop(0, sources // together)
    def _(i):
        for e in range(together):
            d = i * together + e
            at = pl.ds(pl.multiple_of(d * share, 8), share)
            for chain in chains:
                chain[at, :] = jnp.zeros((share, LANE), f32)
            part = turns(got[d, :64, :])
            marks = quarters[d].astype(bf16)
            for k in range(4):
                mark = lax.dot_general(
                    marks, picks[k], (((0,), (0,)), ((), ())), preferred_element_type=f32
                )
                one = jnp.where(mark == wanted, repeat(part, k), 0.0)
                spread[pl.ds(pl.multiple_of(d * 256 + k * 64, 64), 64), :] = one

    step = 16

    @pl.loop(0, total // (CHAINS * step))
    def _(i):
        for u in range(step):
            spots = [(i * step + u) * CHAINS + c for c in range(CHAINS)]
            where = [pl.ds(places[j], 1) for j in spots]
            adds = [spread[pl.ds(j, 1), :] for j in spots]
            olds = [chains[c][where[c], :] for c in range(CHAINS)]
            for c in range(CHAINS):
                chains[c][where[c], :] = olds[c] + adds[c]

    for fetch in fetches:
        fetch.wait()
    columns = depth // (row_count // 4)

    @pl.loop(0, tiles)
    def _(ct):
        out = field.at[ct]
        for rr in range(row_count // 4):
            at = pl.ds(pl.multiple_of(rr * columns + ct * LANE, LANE), LANE)
            parts = [chain[at, :] for chain in chains]
            while len(parts) > 1:
                parts = [a + b for a, b in zip(parts[::2], parts[1::2])]
            turned = parts[0].T
            for q in range(4):
                for o in range(groups // 8):
                    at = pl.ds(o * 8 * row_count + rr * 4 + q, 8, stride=row_count)
                    first = q * groups + o * 8
                    out[at, :] = out[at, :] + turned[first : first + 8, :]
        pltpu.make_async_copy(field.at[ct], forced.at[ct], out_sem.at[ct]).start()
        zero = jnp.zeros((8, LANE), f32)
        per_group = moments.shape[0] // groups
        for first in range(0, groups // 8, SIDE):
            octets = range(first, first + SIDE)
            sets = [
                [
                    out[pl.ds(o * 8 * row_count + r, 8, stride=row_count), :]
                    for r in range(row_count)
                ]
                for o in octets
            ]
            _, ends = lat_sweeps(
                sets, [decay_of_octet(decay, groups, o) for o in octets], [[zero] * 4] * SIDE
            )
            for i, o in enumerate(octets):
                for k in range(4):
                    start = o * 8 * per_group + k * (per_group // 4) + ct
                    moments[pl.ds(start, 8, stride=per_group), :] = ends[i][k]

    for ct in range(tiles):
        pltpu.make_async_copy(field.at[ct], forced.at[ct], out_sem.at[ct]).wait()


def force(places, got, quarters, background, decay, row_count, groups):
    rows, columns = background.shape
    tiles = columns // LANE
    total = places.shape[0]
    depth = rows * columns // LANE
    whole = pl.BlockSpec(memory_space=pltpu.VMEM)
    return pl.pallas_call(
        functools.partial(forced_kernel, row_count, groups),
        out_shape=(
            jax.ShapeDtypeStruct((tiles, rows, LANE), f32),
            jax.ShapeDtypeStruct((groups * 4 * tiles, LANE), f32),
        ),
        in_specs=[
            pl.BlockSpec(memory_space=pltpu.SMEM),
            whole,
            whole,
            pl.BlockSpec(memory_space=pl.ANY),
            whole,
        ],
        out_specs=(pl.BlockSpec(memory_space=pl.ANY), whole),
        scratch_shapes=[
            pltpu.VMEM((total, LANE), f32),
            pltpu.VMEM((tiles, rows, LANE), f32),
            pltpu.SemaphoreType.DMA((tiles,)),
            pltpu.SemaphoreType.DMA((tiles,)),
        ]
        + [pltpu.VMEM((depth, LANE), f32)] * CHAINS,
        compiler_params=vmem(58),
        cost_estimate=cost(0, 16 << 20),
        name="force",
    )(places, got, quarters, background, decay)


def lon_weights(length, columns):
    blocks = columns // LANE
    length = length[:, None, None]
    kappa = jnp.tanh(0.5 / length)
    beta = kappa * kappa
    alpha = beta / jnp.tanh(1.0 / length)
    i = jnp.arange(LANE, dtype=f32)

    def power(n):
        return jnp.exp(-n / length)

    gap = jnp.abs(i[:, None] - i[None, :])[None]
    local = (alpha + beta * gap) * power(gap)
    up, down = i[None, :, None], (LANE - 1.0) - i[None, :, None]
    sums = jnp.concatenate(
        [power(down), down * power(down), power(up), up * power(up)], axis=2
    )
    sums = jnp.pad(sums, ((0, 0), (0, 0), (0, LANE - 4)))
    first = jnp.concatenate([local, sums], axis=2)
    index = jnp.arange(LANE)
    src, dst = index[:, None], index[None, :]
    source, target = src // 4, dst // 4
    backward = (src % 4) >= 2
    steps = jnp.where(backward, source - target - 1, target - source - 1) % blocks
    gap = (LANE * steps).astype(f32)[None]
    turn = power(float(columns))
    left = -jnp.expm1(-float(columns) / length)
    same = power(gap) / left
    cross = (gap + columns * turn / left) * same
    used = (source < blocks) & (target < blocks)
    mix = jnp.where((used & (src % 4 == dst % 4))[None], same, 0.0)
    mix = jnp.where((used & (src % 2 == 0) & (dst % 4 == src % 4 + 1))[None], cross, mix)
    near, far = i[None, None, :] + 1.0, LANE - i[None, None, :]
    back = jnp.concatenate(
        [
            (alpha + beta * near) * power(near),
            beta * power(near),
            (alpha + beta * far) * power(far),
            beta * power(far),
        ],
        axis=1,
    )
    back = jnp.pad(back, ((0, 0), (0, LANE - 4), (0, 0)))
    return thirds(first), thirds(mix), thirds(back)


def thirds(w):
    high = lax.reduce_precision(w, 8, 7)
    low = (w - high).astype(bf16)
    high = high.astype(bf16)
    return jnp.concatenate([high, high, low], axis=1)


def dot3(x, w):
    high = x.astype(bf16)
    low = (x - high.astype(f32)).astype(bf16)
    return jnp.dot(jnp.concatenate([high, low, high], axis=1), w, preferred_element_type=f32)


def lon_apply(parts, first, mix, back):
    count, blocks = parts[0].shape[0], len(parts)
    both = dot3(jnp.concatenate(parts, axis=0), first)
    local, sums = both[:, :LANE], both[:, LANE:]
    line = sums[:count]
    for b in range(1, blocks):
        line = line + pltpu.roll(sums[b * count : (b + 1) * count], 4 * b, 1)
    states = dot3(line, mix)
    spread = jnp.concatenate(
        [states] + [pltpu.roll(states, LANE - 4 * b, 1) for b in range(1, blocks)], axis=0
    )
    out = local + dot3(spread, back)
    return [out[b * count : (b + 1) * count] for b in range(blocks)]


LON_STEP = 4


def hub_coefficients(decay):
    count = decay.shape[0]
    coef = [decay[r : r + 1, :] for r in range(count)]

    def forward(rows):
        state, out = jnp.zeros((1, LANE), f32), []
        for r in range(count):
            state = rows[r] + coef[r] * (state - rows[r])
            out.append(state)
        return out

    def backward(rows):
        state, out = jnp.zeros((1, LANE), f32), [None] * count
        for r in range(count - 1, -1, -1):
            state = rows[r] + coef[r] * (state - rows[r])
            out[r] = state
        return out

    state, down = jnp.ones((1, LANE), f32), []
    for r in range(count):
        state = coef[r] * state
        down.append(state)
    full = state
    state, up = jnp.ones((1, LANE), f32), [None] * count
    for r in range(count - 1, -1, -1):
        state = coef[r] * state
        up[r] = state
    bp = backward(down)
    fbp = forward(bp)
    bfbp = backward(fbp)
    fq = forward(up)
    bfq = backward(fq)
    return full, bp[0], fbp[-1], bfbp[0], fq[-1], bfq[0]


def exchange_kernel(
    count, variables, field, moments, decay, table, first, mix, back, own_first, own_mix, own_back,
    vert, coef, out, entered, arrived, replies, states, work, xs, ws, ms, bs, sums, beside, merged,
    joined, answers, entering, passed, sems, out_sem, send, recv, back_send, back_recv, pair_send,
    pair_recv, hub_send, hub_recv, reply_send, reply_recv, last_send, last_recv,
):
    tiles, rows, _ = out.shape
    blocks = arrived.shape[0]
    me = lax.axis_index("sub")
    steps = rows // count // LON_STEP
    size = LON_STEP * count

    def fetches(i):
        group = i * LON_STEP
        at = pl.ds(pl.multiple_of(group * count, 8), size)
        inside = pl.ds(group, LON_STEP)
        return [
            pltpu.make_async_copy(field.at[:, at], xs.at[:, at], sems.at[0, i]),
            pltpu.make_async_copy(first.at[inside], ws.at[inside], sems.at[1, i]),
            pltpu.make_async_copy(mix.at[inside], ms.at[inside], sems.at[2, i]),
            pltpu.make_async_copy(back.at[inside], bs.at[inside], sems.at[3, i]),
        ]

    for i in range(steps):
        for fetch in fetches(i):
            fetch.start()

    def lon_steps(start, stop):
        @pl.loop(start, stop)
        def _(i):
            for fetch in fetches(i):
                fetch.wait()
            for u in range(LON_STEP):
                g = i * LON_STEP + u
                at = pl.ds(pl.multiple_of(g * count, 8), count)
                parts = lon_apply([xs[b, at, :] for b in range(tiles)], ws[g], ms[g], bs[g])
                for b in range(tiles):
                    xs[b, at, :] = parts[b]

    barrier = pltpu.get_barrier_semaphore()

    @pl.loop(1, blocks)
    def _(step):
        target = lax.rem(me + step, blocks)
        pl.semaphore_signal(
            barrier, inc=1, device_id={"sub": target}, device_id_type=pl.DeviceIdType.MESH
        )

    band = lax.axis_index("band")
    chip, core = band // 2, band % 2
    sibling = chip * 2 + (1 - core)

    def other(step):
        return lax.rem(chip + step, 4) * 2 + core

    for target in [sibling] + [other(step) for step in (1, 2, 3)]:
        pl.semaphore_signal(
            barrier, inc=1, device_id={"band": target}, device_id_type=pl.DeviceIdType.MESH
        )
    pl.semaphore_wait(barrier, blocks - 1 + 4)

    def outward(step):
        target = lax.rem(me + step, blocks)
        return pltpu.make_async_remote_copy(
            src_ref=moments.at[target],
            dst_ref=arrived.at[me],
            send_sem=send.at[step - 1],
            recv_sem=recv.at[step - 1],
            device_id={"sub": target},
            device_id_type=pl.DeviceIdType.MESH,
        )

    def homeward(step):
        target = lax.rem(me + step, blocks)
        return pltpu.make_async_remote_copy(
            src_ref=replies.at[target],
            dst_ref=states.at[me],
            send_sem=back_send.at[step - 1],
            recv_sem=back_recv.at[step - 1],
            device_id={"sub": target},
            device_id_type=pl.DeviceIdType.MESH,
        )

    @pl.loop(1, blocks)
    def _(step):
        outward(step).start()

    arrived[me] = moments[me]
    lon_steps(0, steps // 2)

    @pl.loop(1, blocks)
    def _(step):
        outward(step).wait_recv()

    full, t21, t31, t41, t32, t42 = hub_coefficients(decay)

    def at(table, d):
        return jnp.broadcast_to(table[:, d : d + 1], (tiles, LANE))

    def moment(d, k):
        return arrived[d, k * tiles : (k + 1) * tiles, :]

    carry = jnp.zeros((tiles, LANE), f32)
    s = [[None] * blocks for _ in range(4)]
    for d in range(blocks):
        s[0][d] = carry
        carry = at(full, d) * carry + moment(d, 0)
    carry = jnp.zeros((tiles, LANE), f32)
    for d in range(blocks - 1, -1, -1):
        s[1][d] = carry
        carry = at(full, d) * carry + (moment(d, 1) + at(t21, d) * s[0][d])
    carry = jnp.zeros((tiles, LANE), f32)
    for d in range(blocks):
        s[2][d] = carry
        carry = at(full, d) * carry + (
            moment(d, 2) + at(t31, d) * s[0][d] + at(t32, d) * s[1][d]
        )
    carry = jnp.zeros((tiles, LANE), f32)
    for d in range(blocks - 1, -1, -1):
        s[3][d] = carry
        carry = at(full, d) * carry + (
            moment(d, 3) + at(t41, d) * s[0][d] + at(t42, d) * s[1][d] + at(t21, d) * s[2][d]
        )
    for k in range(4):
        for d in range(blocks):
            for t in range(tiles):
                work[t, k * blocks + d : k * blocks + d + 1, :] = s[k][d][t : t + 1, :]
    done = lon_apply([work[t] for t in range(tiles)], own_first[0], own_mix[0], own_back[0])
    for t in range(tiles):
        for k in range(4):
            replies[:, k * tiles + t, :] = done[t][k * blocks : (k + 1) * blocks]

    @pl.loop(1, blocks)
    def _(step):
        homeward(step).start()

    states[me] = replies[me]
    lon_steps(steps // 2, steps)

    @pl.loop(1, blocks)
    def _(step):
        homeward(step).wait_recv()

    @pl.loop(1, blocks)
    def _(step):
        outward(step).wait_send()
        homeward(step).wait_send()

    groups = rows // count
    levels = groups // variables
    half = tiles // 2
    depth = half * count
    tail = 2 * depth
    zero = jnp.zeros((8, LANE), f32)
    mine_first = core * 4

    def level_remote(src, dst, send_sem, recv_sem, target):
        return pltpu.make_async_remote_copy(
            src_ref=src,
            dst_ref=dst,
            send_sem=send_sem,
            recv_sem=recv_sem,
            device_id={"band": target},
            device_id_type=pl.DeviceIdType.MESH,
        )

    def pair(j):
        return level_remote(
            sums.at[(1 - core) * 4 + j], beside.at[j], pair_send.at[j], pair_recv.at[j], sibling
        )

    for target in range(2 * variables):
        sums[target, tail : tail + 8, :] = coef[target // 2]

    for side in range(2):

        @pl.loop(0, half)
        def _(spot):
            ct = side * half + spot
            done = xs.at[ct]
            for o in range(groups // 8):
                lines = [
                    done[pl.ds(o * 8 * count + r, 8, stride=count), :] for r in range(count)
                ]
                starts = [states[o * 8 : o * 8 + 8, k * tiles + ct, :] for k in range(4)]
                lines, _ = lat_sweeps([lines], [decay_of_octet(table, groups, o)], [starts])
                for r in range(count):
                    done[pl.ds(o * 8 * count + r, 8, stride=count), :] = lines[0][r]
            pltpu.make_async_copy(done, out.at[ct], out_sem.at[ct]).start()
            for var in range(variables):
                for t in range(count // 8):
                    lines = []
                    for lev in range(levels):
                        base = (lev * variables + var) * count + t * 8
                        lines.append(done[base : base + 8, :])
                    _, ends = level_sweeps(
                        lines, lambda lev: vert[lev * variables + var], [zero, zero]
                    )
                    for k in range(2):
                        at = pl.ds(pl.multiple_of(k * depth + spot * count + t * 8, 8), 8)
                        sums[var * 2 + side, at, :] = ends[k]

        for j in (side, side + 2):
            pair(j).start()

    def lower(a, b):
        return jnp.where(core == 0, a, b)

    def row(ref, chunk, at):
        return jnp.broadcast_to(ref[chunk, at : at + 1, :], (8, LANE))

    def bands_of(chunk, at):
        a, b = sums[mine_first + chunk, at, :], beside[chunk, at, :]
        return lower(a, b), lower(b, a)

    def coefficients(chunk):
        both = []
        for at in (tail, tail + 1):
            a, b = row(sums, mine_first + chunk, at), row(beside, chunk, at)
            both.append((lower(a, b), lower(b, a)))
        return both

    def hub_copy(j):
        step = lax.rem(j - chip + 4, 4)
        return level_remote(
            merged.at[j], joined.at[chip], hub_send.at[step - 1], hub_recv.at[step - 1], j * 2 + core
        )

    for j in (0, 2, 1, 3):
        pair(j).wait_recv()
        (full0, full1), (both0, both1) = coefficients(j)

        @pl.loop(0, depth // 8)
        def _(t):
            at = pl.ds(pl.multiple_of(t * 8, 8), 8)
            later = pl.ds(pl.multiple_of(depth + t * 8, 8), 8)
            up0, up1 = bands_of(j, at)
            down0, down1 = bands_of(j, later)
            merged[j, at, :] = full1 * up0 + up1
            merged[j, later, :] = down0 + full0 * (down1 + both1 * up0)

        index = lax.broadcasted_iota(jnp.int32, (8, LANE), 0)
        merged[j, tail : tail + 8, :] = jnp.where(
            index == 0, full0 * full1, both0 + full0 * both1 * full0
        )

        @pl.when(chip != j)
        def _():
            hub_copy(j).start()

    joined[chip] = merged[chip]
    for step in (1, 2, 3):
        hub_copy(lax.rem(chip + step, 4)).wait_recv()

    fulls = [row(joined, c, tail) for c in range(4)]
    boths = [row(joined, c, tail + 1) for c in range(4)]

    @pl.loop(0, depth // 8)
    def _(t):
        at = pl.ds(pl.multiple_of(t * 8, 8), 8)
        later = pl.ds(pl.multiple_of(depth + t * 8, 8), 8)
        state = jnp.zeros((8, LANE), f32)
        ups = []
        for c in range(4):
            ups.append(state)
            answers[c, at, :] = state
            state = fulls[c] * state + joined[c, at, :]
        state = jnp.zeros((8, LANE), f32)
        for c in (3, 2, 1, 0):
            answers[c, later, :] = state
            state = fulls[c] * state + (joined[c, later, :] + boths[c] * ups[c])

    answer_copies = []
    for step in (2, 1, 3):
        copy = level_remote(
            answers.at[lax.rem(chip + step, 4)],
            entering.at[chip],
            reply_send.at[step - 1],
            reply_recv.at[step - 1],
            other(step),
        )
        copy.start()
        answer_copies.append(copy)
    entering[chip] = answers[chip]
    for copy in answer_copies:
        copy.wait_recv()

    last = []
    for j in range(4):
        (full0, full1), (both0, both1) = coefficients(j)

        @pl.loop(0, depth // 8)
        def _(t):
            at = pl.ds(pl.multiple_of(t * 8, 8), 8)
            later = pl.ds(pl.multiple_of(depth + t * 8, 8), 8)
            up0, _ = bands_of(j, at)
            _, down1 = bands_of(j, later)
            below = entering[j, at, :]
            above = entering[j, later, :]
            middle = full0 * below + up0
            turned = full1 * above + (down1 + both1 * middle)
            entered[mine_first + j, at, :] = lower(below, middle)
            entered[mine_first + j, later, :] = lower(turned, above)
            passed[j, at, :] = lower(middle, below)
            passed[j, later, :] = lower(above, turned)

        copy = level_remote(
            passed.at[j], entered.at[mine_first + j], last_send.at[j], last_recv.at[j], sibling
        )
        copy.start()
        last.append(copy)

    for j in range(4):
        pair(j).wait_send()
    for step in (1, 2, 3):
        hub_copy(lax.rem(chip + step, 4)).wait_send()
    for copy in answer_copies:
        copy.wait_send()
    for copy in last:
        copy.wait()
    for ct in range(tiles):
        pltpu.make_async_copy(xs.at[ct], out.at[ct], out_sem.at[ct]).wait()


def exchange(field, moments, decay, table, weights, own_weights, vert, coef, row_count, variables):
    tiles, rows, _ = field.shape
    blocks, depth, _ = moments.shape
    groups = rows // row_count
    steps = groups // LON_STEP
    chunk = tiles * row_count
    any_space = pl.BlockSpec(memory_space=pl.ANY)
    whole = pl.BlockSpec(memory_space=pltpu.VMEM)
    dma = pltpu.SemaphoreType.DMA
    return pl.pallas_call(
        functools.partial(exchange_kernel, row_count, variables),
        out_shape=(
            jax.ShapeDtypeStruct(field.shape, f32),
            jax.ShapeDtypeStruct((2 * variables, chunk, LANE), f32),
        ),
        in_specs=[any_space, whole, whole, whole]
        + [any_space] * 3
        + [whole] * 3
        + [pl.BlockSpec(memory_space=pltpu.SMEM), whole],
        out_specs=(any_space, whole),
        scratch_shapes=[
            pltpu.VMEM(moments.shape, f32),
            pltpu.VMEM(moments.shape, f32),
            pltpu.VMEM(moments.shape, f32),
            pltpu.VMEM((tiles, 4 * blocks, LANE), f32),
            pltpu.VMEM(field.shape, f32),
        ]
        + [pltpu.VMEM(w.shape, w.dtype) for w in weights]
        + [pltpu.VMEM((2 * variables, chunk + 8, LANE), f32)]
        + [pltpu.VMEM((4, chunk + 8, LANE), f32)] * 3
        + [pltpu.VMEM((4, chunk, LANE), f32)] * 3
        + [dma((4, steps)), dma((tiles,))]
        + [dma((blocks - 1,))] * 4
        + [dma((4,)), dma((4,)), dma((3,)), dma((3,)), dma((3,)), dma((3,)), dma((4,)), dma((4,))],
        compiler_params=pltpu.CompilerParams(
            vmem_limit_bytes=60 << 20, collective_id=0, has_side_effects=True
        ),
        cost_estimate=cost(6 * rows * tiles * LANE * 3 * LANE, 60 << 20),
        name="exchange",
    )(field, moments, decay, table, *weights, *own_weights, vert, coef)


def level_sweeps(rows, decay, starts):
    count = len(rows)
    ends = []
    for sweep in range(2):
        order = range(count) if sweep == 0 else range(count - 1, -1, -1)
        state = starts[sweep]
        out = [None] * count
        for r in order:
            state = decay(r) * state + (1.0 - decay(r)) * rows[r]
            out[r] = state
        ends.append(state)
        rows = out
    return rows, ends


def level_states_kernel(source, vert, states, out, x, result, in_sem, sem):
    tiles, levels, variables, row_count, _ = x.shape
    fetches = [
        pltpu.make_async_copy(source.at[:, :, var], x.at[:, :, var], in_sem.at[var])
        for var in range(variables)
    ]
    for fetch in fetches:
        fetch.start()
    writes = []
    for var in range(variables):
        fetches[var].wait()
        decay = [vert[lev * variables + var] for lev in range(levels)]
        for ct in range(tiles):
            for t in range(row_count // 8):
                at = slice(t * 8, t * 8 + 8)
                rows = [x[ct, lev, var, at, :] for lev in range(levels)]
                starts = [states[var, ct // (tiles // 2), k, ct % (tiles // 2), at, :] for k in range(2)]
                rows, _ = level_sweeps(rows, lambda lev: decay[lev], starts)
                for lev in range(levels):
                    result[lev, var, at, ct * LANE : (ct + 1) * LANE] = rows[lev]
        write = pltpu.make_async_copy(result.at[:, var], out.at[:, var], sem.at[var])
        write.start()
        writes.append(write)
    for write in writes:
        write.wait()


def level_states(x, vert, states, shape):
    levels, variables, row_count, columns = shape
    tiles = columns // LANE
    whole = pl.BlockSpec(memory_space=pltpu.VMEM)
    return pl.pallas_call(
        level_states_kernel,
        out_shape=jax.ShapeDtypeStruct(shape, f32),
        in_specs=[pl.BlockSpec(memory_space=pl.ANY), pl.BlockSpec(memory_space=pltpu.SMEM), whole],
        out_specs=pl.BlockSpec(memory_space=pl.ANY),
        scratch_shapes=[
            pltpu.VMEM((tiles, levels, variables, row_count, LANE), f32),
            pltpu.VMEM(shape, f32),
            pltpu.SemaphoreType.DMA((variables,)),
            pltpu.SemaphoreType.DMA((variables,)),
        ],
        compiler_params=vmem(60),
        cost_estimate=cost(0, 11 << 20),
        name="level_states",
    )(x.reshape(tiles, levels, variables, row_count, LANE), vert, states)


def level_coefficients(decays):
    levels = decays.shape[0]
    state, down = jnp.ones_like(decays[0]), []
    for r in range(levels):
        state = decays[r] * state
        down.append(state)
    full = state
    state = jnp.zeros_like(full)
    for r in range(levels - 1, -1, -1):
        state = down[r] + decays[r] * (state - down[r])
    both = jnp.stack([full, state], axis=1)
    both = jnp.pad(both, ((0, 0), (0, 6)))
    return jnp.broadcast_to(both[:, :, None], both.shape + (LANE,))


def per_device(background, obs_columns, obs_owner, obs_cell, lat_length, lon_length, vert_length):
    level_count, var_count, row_count, lon_count = background.shape
    sub_count = lax.axis_size("sub")
    band_count = lax.axis_size("band")
    sub_index = lax.axis_index("sub")
    groups = level_count * var_count
    tiles = lon_count // LANE
    tile_field = background.reshape(groups * row_count, lon_count)
    owners = obs_owner[:, 0]
    capacity = 2 * owners.shape[0] // sub_count

    ranks = route_ranks(owners, sub_count)
    row, column = obs_cell // lon_count, obs_cell % lon_count
    place = ((row // 4) * lon_count + column) * 4 + row % 4
    table = jnp.stack([owners, ranks, place] + [jnp.zeros_like(place)] * 5)
    lines = capacity // LANE
    message = pack(owners * capacity + ranks, table, obs_columns, sub_count)
    got = lax.all_to_all(message.reshape(sub_count, -1, LANE), "sub", 0, 0, tiled=True)

    vert_decay = jnp.exp(-1.0 / vert_length)
    coef = level_coefficients(vert_decay)
    vert_decay = vert_decay.reshape(groups)

    lat_all = jnp.exp(-1.0 / lat_length).reshape(groups, sub_count, row_count)
    own_lat = lax.dynamic_index_in_dim(lat_all, sub_index, 1, False)
    own_lat = own_lat.T.reshape(row_count * groups, 1)
    own_lat = jnp.concatenate([own_lat, 1.0 - own_lat])
    decay = jnp.broadcast_to(own_lat, (2 * row_count * groups, LANE))
    hub_lat = lax.dynamic_index_in_dim(lat_all, sub_index, 0, False)
    hub_lat = jnp.pad(hub_lat.T, ((0, 0), (0, LANE - sub_count)))

    lengths = lon_length.reshape(groups)
    weights = lon_weights(lengths, lon_count)
    own_weights = [lax.dynamic_slice_in_dim(w, sub_index, 1, 0) for w in weights]

    got, weights, own_weights = lax.optimization_barrier((got, weights, own_weights))
    places = got[:, capacity // 4 : capacity // 4 + lines, :].reshape(-1).astype(jnp.int32)
    quarters = (places & 3).astype(f32).reshape(sub_count, 4, capacity // 4)
    quarters = jnp.pad(quarters, ((0, 0), (0, 4), (0, 0)))
    forced, moments = force(places >> 2, got, quarters, tile_field, decay, row_count, groups)
    smooth, entering = exchange(
        forced,
        moments.reshape(sub_count, 4 * tiles, LANE),
        hub_lat,
        decay,
        weights,
        own_weights,
        vert_decay,
        coef,
        row_count,
        var_count,
    )
    return level_states(
        smooth,
        vert_decay,
        entering.reshape(var_count, 2, 2, tiles // 2, row_count, LANE),
        background.shape,
    )


def solution(mesh):
    placed = (
        P("band", None, "sub", None),
        P("band", None, "sub"),
        P("sub", None),
        P("sub"),
        P("band", None, None),
        P("band", None),
        P("band", None),
    )
    return jax.shard_map(
        per_device,
        mesh=mesh,
        in_specs=placed,
        out_specs=P("band", None, "sub", None),
        check_vma=False,
    )
```

```python
import functools

import jax
import jax.numpy as jnp
from jax import lax
from jax.experimental import pallas as pl
from jax.experimental.pallas import tpu as pltpu
from jax.sharding import PartitionSpec as P

LANE = 128
f32 = jnp.float32
bf16 = jnp.bfloat16


def vmem(mib):
    return pltpu.CompilerParams(vmem_limit_bytes=mib << 20)


def cost(flops, moved):
    return pl.CostEstimate(flops=flops, bytes_accessed=moved, transcendentals=0)


def route_ranks(owners, sub_count):
    count = owners.shape[0]
    block = 128
    owner_block = owners.reshape(count // block, block)
    match = (owner_block[:, :, None] == jnp.arange(sub_count, dtype=jnp.int32)).astype(bf16)
    position = jnp.arange(block)
    lower = (position[:, None] > position[None, :]).astype(bf16)
    ahead = jnp.einsum("ij,bjo->bio", lower, match, preferred_element_type=f32)
    totals = jnp.sum(match.astype(f32), axis=1)
    base = jnp.cumsum(totals, axis=0) - totals
    rank = jnp.sum((ahead + base[:, None, :]) * match.astype(f32), axis=2)
    return rank.reshape(count).astype(jnp.int32)


def pack_kernel(slots, slot_row, place_row, values, packed, rows, big):
    levels, _, count = values.shape
    total = big.shape[0]
    targets = total // 256
    size = packed.shape[0] // targets
    share = total // (count // LANE)

    for j in range(count // LANE):
        big[j * share : (j + 1) * share, :] = jnp.zeros((share, LANE), f32)
        part = jnp.concatenate(
            [values[lev, :, j * LANE : (j + 1) * LANE] for lev in range(levels)], axis=0
        )
        rows[j * LANE : (j + 1) * LANE, :] = jnp.concatenate([part] * 4, axis=0).T

    slot, place = slot_row[...], place_row[...]
    owner, rank = lax.shift_right_logical(slot, 8), slot & 255
    mine = owner == lax.broadcasted_iota(jnp.int32, (targets, count), 0)
    spot = (rank == lax.broadcasted_iota(jnp.int32, (256, count), 0)).astype(f32).astype(bf16)

    def put(half):
        return jnp.where(mine, half, 0).astype(f32).astype(bf16)

    both = lax.dot_general(
        jnp.concatenate([put(lax.shift_right_logical(place, 8)), put(place & 255)], axis=0),
        spot,
        (((1,), (1,)), ((), ())),
        preferred_element_type=f32,
    )
    cells = both[:targets] * 256.0 + both[targets:]
    for half in range(2):
        packed[pl.ds(64 + half, targets, stride=size), :] = cells[:, half * LANE : (half + 1) * LANE]
    for extra in range(66, size):
        packed[pl.ds(extra, targets, stride=size), :] = jnp.zeros((targets, LANE), f32)

    step = PACK_STEP

    @pl.loop(0, count // step)
    def _(i):
        for u in range(step):
            j = i * step + u
            big[pl.ds(slots[j], 1), :] = rows[pl.ds(j, 1), :]

    quarter = lax.broadcasted_iota(jnp.int32, (64, LANE), 1) // 32

    @pl.loop(0, targets // PACK_SIDE)
    def _(i):
        for e in range(PACK_SIDE):
            d = i * PACK_SIDE + e
            start = pl.multiple_of(d * 256, 256)
            out = big[pl.ds(start, 64), :]
            for k in range(1, 4):
                out = jnp.where(quarter == k, big[pl.ds(start + 64 * k, 64), :], out)
            packed[pl.ds(pl.multiple_of(d * size, 8), 64), :] = out


PACK_STEP = 64
PACK_SIDE = 8


def pack(slots, place, values, targets):
    count = values.shape[2]
    total = targets * 256
    whole = pl.BlockSpec(memory_space=pltpu.VMEM)
    return pl.pallas_call(
        pack_kernel,
        out_shape=jax.ShapeDtypeStruct((targets * 72, LANE), f32),
        in_specs=[pl.BlockSpec(memory_space=pltpu.SMEM), whole, whole, whole],
        out_specs=whole,
        scratch_shapes=[pltpu.VMEM((count, LANE), f32), pltpu.VMEM((total, LANE), f32)],
        compiler_params=vmem(60),
        cost_estimate=cost(0, 4 << 20),
        name="pack",
    )(slots, slots.reshape(1, count), place.reshape(1, count), values)


def lat_sweeps(sets, decays, starts):
    count = len(sets[0])
    ends = [[] for _ in sets]
    for sweep in range(4):
        order = range(count) if sweep % 2 == 0 else range(count - 1, -1, -1)
        states = [start[sweep] for start in starts]
        outs = [[None] * count for _ in sets]
        for r in order:
            for i, rows in enumerate(sets):
                a, rest = decays[i](r)
                states[i] = a * states[i] + rest * rows[r]
                outs[i][r] = states[i]
        for i in range(len(sets)):
            ends[i].append(states[i])
        sets = outs
    return sets, ends


def decay_of_octet(decay, groups, o):
    rows = decay.shape[0] // 2

    def pair(r):
        at = r * groups + o * 8
        return decay[at : at + 8, :], decay[rows + at : rows + at + 8, :]

    return pair


CHAINS = 8
SIDE = 1


def forced_kernel(row_count, groups, places, got, quarters, background, decay, forced, moments, spread, field, sem, out_sem, *chains):
    total = spread.shape[0]
    depth = chains[0].shape[0]
    sources = got.shape[0]
    tiles = forced.shape[0]
    fetches = [
        pltpu.make_async_copy(
            background.at[:, ct * LANE : (ct + 1) * LANE], field.at[ct], sem.at[ct]
        )
        for ct in range(tiles)
    ]
    for fetch in fetches:
        fetch.start()

    row = lax.broadcasted_iota(jnp.int32, (8, LANE), 0)
    picks = [(row == k).astype(f32).astype(bf16) for k in range(4)]
    quarter = lax.broadcasted_iota(jnp.int32, (64, LANE), 1) // 32
    wanted = quarter.astype(f32)

    def turns(x):
        return [x] + [pltpu.roll(x, 32 * k, 1) for k in range(1, 4)]

    def repeat(turned, k):
        out = turned[(3 - k) % 4]
        for q in range(3):
            out = jnp.where(quarter == q, turned[(q - k) % 4], out)
        return out

    share = depth // sources
    together = 2

    @pl.loop(0, sources // together)
    def _(i):
        for e in range(together):
            d = i * together + e
            at = pl.ds(pl.multiple_of(d * share, 8), share)
            for chain in chains:
                chain[at, :] = jnp.zeros((share, LANE), f32)
            part = turns(got[d, :64, :])
            marks = quarters[d].astype(bf16)
            for k in range(4):
                mark = lax.dot_general(
                    marks, picks[k], (((0,), (0,)), ((), ())), preferred_element_type=f32
                )
                one = jnp.where(mark == wanted, repeat(part, k), 0.0)
                spread[pl.ds(pl.multiple_of(d * 256 + k * 64, 64), 64), :] = one

    step = 16

    @pl.loop(0, total // (CHAINS * step))
    def _(i):
        for u in range(step):
            spots = [(i * step + u) * CHAINS + c for c in range(CHAINS)]
            where = [pl.ds(places[j], 1) for j in spots]
            adds = [spread[pl.ds(j, 1), :] for j in spots]
            olds = [chains[c][where[c], :] for c in range(CHAINS)]
            for c in range(CHAINS):
                chains[c][where[c], :] = olds[c] + adds[c]

    for fetch in fetches:
        fetch.wait()
    columns = depth // (row_count // 4)

    @pl.loop(0, tiles)
    def _(ct):
        out = field.at[ct]
        for rr in range(row_count // 4):
            at = pl.ds(pl.multiple_of(rr * columns + ct * LANE, LANE), LANE)
            parts = [chain[at, :] for chain in chains]
            while len(parts) > 1:
                parts = [a + b for a, b in zip(parts[::2], parts[1::2])]
            turned = parts[0].T
            for q in range(4):
                for o in range(groups // 8):
                    at = pl.ds(o * 8 * row_count + rr * 4 + q, 8, stride=row_count)
                    first = q * groups + o * 8
                    out[at, :] = out[at, :] + turned[first : first + 8, :]
        pltpu.make_async_copy(field.at[ct], forced.at[ct], out_sem.at[ct]).start()
        zero = jnp.zeros((8, LANE), f32)
        per_group = moments.shape[0] // groups
        for first in range(0, groups // 8, SIDE):
            octets = range(first, first + SIDE)
            sets = [
                [
                    out[pl.ds(o * 8 * row_count + r, 8, stride=row_count), :]
                    for r in range(row_count)
                ]
                for o in octets
            ]
            _, ends = lat_sweeps(
                sets, [decay_of_octet(decay, groups, o) for o in octets], [[zero] * 4] * SIDE
            )
            for i, o in enumerate(octets):
                for k in range(4):
                    start = o * 8 * per_group + k * (per_group // 4) + ct
                    moments[pl.ds(start, 8, stride=per_group), :] = ends[i][k]

    for ct in range(tiles):
        pltpu.make_async_copy(field.at[ct], forced.at[ct], out_sem.at[ct]).wait()


def force(places, got, quarters, background, decay, row_count, groups):
    rows, columns = background.shape
    tiles = columns // LANE
    total = places.shape[0]
    depth = rows * columns // LANE
    whole = pl.BlockSpec(memory_space=pltpu.VMEM)
    return pl.pallas_call(
        functools.partial(forced_kernel, row_count, groups),
        out_shape=(
            jax.ShapeDtypeStruct((tiles, rows, LANE), f32),
            jax.ShapeDtypeStruct((groups * 4 * tiles, LANE), f32),
        ),
        in_specs=[
            pl.BlockSpec(memory_space=pltpu.SMEM),
            whole,
            whole,
            pl.BlockSpec(memory_space=pl.ANY),
            whole,
        ],
        out_specs=(pl.BlockSpec(memory_space=pl.ANY), whole),
        scratch_shapes=[
            pltpu.VMEM((total, LANE), f32),
            pltpu.VMEM((tiles, rows, LANE), f32),
            pltpu.SemaphoreType.DMA((tiles,)),
            pltpu.SemaphoreType.DMA((tiles,)),
        ]
        + [pltpu.VMEM((depth, LANE), f32)] * CHAINS,
        compiler_params=vmem(58),
        cost_estimate=cost(0, 16 << 20),
        name="force",
    )(places, got, quarters, background, decay)


def lon_weights(length, columns):
    blocks = columns // LANE
    length = length[:, None, None]
    kappa = jnp.tanh(0.5 / length)
    beta = kappa * kappa
    alpha = beta / jnp.tanh(1.0 / length)
    i = jnp.arange(LANE, dtype=f32)

    def power(n):
        return jnp.exp(-n / length)

    gap = jnp.abs(i[:, None] - i[None, :])[None]
    local = (alpha + beta * gap) * power(gap)
    up, down = i[None, :, None], (LANE - 1.0) - i[None, :, None]
    sums = jnp.concatenate(
        [power(down), down * power(down), power(up), up * power(up)], axis=2
    )
    sums = jnp.pad(sums, ((0, 0), (0, 0), (0, LANE - 4)))
    first = jnp.concatenate([local, sums], axis=2)
    index = jnp.arange(LANE)
    src, dst = index[:, None], index[None, :]
    source, target = src // 4, dst // 4
    backward = (src % 4) >= 2
    steps = jnp.where(backward, source - target - 1, target - source - 1) % blocks
    gap = (LANE * steps).astype(f32)[None]
    turn = power(float(columns))
    left = -jnp.expm1(-float(columns) / length)
    same = power(gap) / left
    cross = (gap + columns * turn / left) * same
    used = (source < blocks) & (target < blocks)
    mix = jnp.where((used & (src % 4 == dst % 4))[None], same, 0.0)
    mix = jnp.where((used & (src % 2 == 0) & (dst % 4 == src % 4 + 1))[None], cross, mix)
    near, far = i[None, None, :] + 1.0, LANE - i[None, None, :]
    back = jnp.concatenate(
        [
            (alpha + beta * near) * power(near),
            beta * power(near),
            (alpha + beta * far) * power(far),
            beta * power(far),
        ],
        axis=1,
    )
    back = jnp.pad(back, ((0, 0), (0, LANE - 4), (0, 0)))
    return thirds(first), thirds(mix), thirds(back)


def thirds(w):
    high = lax.reduce_precision(w, 8, 7)
    low = (w - high).astype(bf16)
    high = high.astype(bf16)
    return jnp.concatenate([high, high, low], axis=1)


def dot3(x, w):
    high = x.astype(bf16)
    low = (x - high.astype(f32)).astype(bf16)
    return jnp.dot(jnp.concatenate([high, low, high], axis=1), w, preferred_element_type=f32)


def lon_apply(parts, first, mix, back):
    count, blocks = parts[0].shape[0], len(parts)
    both = dot3(jnp.concatenate(parts, axis=0), first)
    local, sums = both[:, :LANE], both[:, LANE:]
    line = sums[:count]
    for b in range(1, blocks):
        line = line + pltpu.roll(sums[b * count : (b + 1) * count], 4 * b, 1)
    states = dot3(line, mix)
    spread = jnp.concatenate(
        [states] + [pltpu.roll(states, LANE - 4 * b, 1) for b in range(1, blocks)], axis=0
    )
    out = local + dot3(spread, back)
    return [out[b * count : (b + 1) * count] for b in range(blocks)]


LON_STEP = 4


def hub_coefficients(decay):
    count = decay.shape[0]
    coef = [decay[r : r + 1, :] for r in range(count)]

    def forward(rows):
        state, out = jnp.zeros((1, LANE), f32), []
        for r in range(count):
            state = rows[r] + coef[r] * (state - rows[r])
            out.append(state)
        return out

    def backward(rows):
        state, out = jnp.zeros((1, LANE), f32), [None] * count
        for r in range(count - 1, -1, -1):
            state = rows[r] + coef[r] * (state - rows[r])
            out[r] = state
        return out

    state, down = jnp.ones((1, LANE), f32), []
    for r in range(count):
        state = coef[r] * state
        down.append(state)
    full = state
    state, up = jnp.ones((1, LANE), f32), [None] * count
    for r in range(count - 1, -1, -1):
        state = coef[r] * state
        up[r] = state
    bp = backward(down)
    fbp = forward(bp)
    bfbp = backward(fbp)
    fq = forward(up)
    bfq = backward(fq)
    return full, bp[0], fbp[-1], bfbp[0], fq[-1], bfq[0]


def exchange_kernel(
    count, variables, field, moments, decay, table, first, mix, back, own_first, own_mix, own_back,
    vert, coef, out, entered, arrived, replies, states, work, xs, ws, ms, bs, sums, beside, merged,
    joined, answers, entering, passed, sems, out_sem, send, recv, back_send, back_recv, pair_send,
    pair_recv, hub_send, hub_recv, reply_send, reply_recv, last_send, last_recv,
):
    tiles, rows, _ = out.shape
    blocks = arrived.shape[0]
    me = lax.axis_index("sub")
    steps = rows // count // LON_STEP
    size = LON_STEP * count

    def fetches(i):
        group = i * LON_STEP
        at = pl.ds(pl.multiple_of(group * count, 8), size)
        inside = pl.ds(group, LON_STEP)
        return [
            pltpu.make_async_copy(field.at[:, at], xs.at[:, at], sems.at[0, i]),
            pltpu.make_async_copy(first.at[inside], ws.at[inside], sems.at[1, i]),
            pltpu.make_async_copy(mix.at[inside], ms.at[inside], sems.at[2, i]),
            pltpu.make_async_copy(back.at[inside], bs.at[inside], sems.at[3, i]),
        ]

    for i in range(steps):
        for fetch in fetches(i):
            fetch.start()

    def lon_steps(start, stop):
        @pl.loop(start, stop)
        def _(i):
            for fetch in fetches(i):
                fetch.wait()
            for u in range(LON_STEP):
                g = i * LON_STEP + u
                at = pl.ds(pl.multiple_of(g * count, 8), count)
                parts = lon_apply([xs[b, at, :] for b in range(tiles)], ws[g], ms[g], bs[g])
                for b in range(tiles):
                    xs[b, at, :] = parts[b]

    barrier = pltpu.get_barrier_semaphore()

    @pl.loop(1, blocks)
    def _(step):
        target = lax.rem(me + step, blocks)
        pl.semaphore_signal(
            barrier, inc=1, device_id={"sub": target}, device_id_type=pl.DeviceIdType.MESH
        )

    band = lax.axis_index("band")
    chip, core = band // 2, band % 2
    sibling = chip * 2 + (1 - core)

    def other(step):
        return lax.rem(chip + step, 4) * 2 + core

    for target in [sibling] + [other(step) for step in (1, 2, 3)]:
        pl.semaphore_signal(
            barrier, inc=1, device_id={"band": target}, device_id_type=pl.DeviceIdType.MESH
        )
    pl.semaphore_wait(barrier, blocks - 1 + 4)

    def outward(step):
        target = lax.rem(me + step, blocks)
        return pltpu.make_async_remote_copy(
            src_ref=moments.at[target],
            dst_ref=arrived.at[me],
            send_sem=send.at[step - 1],
            recv_sem=recv.at[step - 1],
            device_id={"sub": target},
            device_id_type=pl.DeviceIdType.MESH,
        )

    def homeward(step):
        target = lax.rem(me + step, blocks)
        return pltpu.make_async_remote_copy(
            src_ref=replies.at[target],
            dst_ref=states.at[me],
            send_sem=back_send.at[step - 1],
            recv_sem=back_recv.at[step - 1],
            device_id={"sub": target},
            device_id_type=pl.DeviceIdType.MESH,
        )

    @pl.loop(1, blocks)
    def _(step):
        outward(step).start()

    arrived[me] = moments[me]
    full, t21, t31, t41, t32, t42 = hub_coefficients(decay)
    lon_steps(0, steps // 2)

    @pl.loop(1, blocks)
    def _(step):
        outward(step).wait_recv()

    def at(table, d):
        return jnp.broadcast_to(table[:, d : d + 1], (tiles, LANE))

    def moment(d, k):
        return arrived[d, k * tiles : (k + 1) * tiles, :]

    carry = jnp.zeros((tiles, LANE), f32)
    s = [[None] * blocks for _ in range(4)]
    for d in range(blocks):
        s[0][d] = carry
        carry = at(full, d) * carry + moment(d, 0)
    carry = jnp.zeros((tiles, LANE), f32)
    for d in range(blocks - 1, -1, -1):
        s[1][d] = carry
        carry = at(full, d) * carry + (moment(d, 1) + at(t21, d) * s[0][d])
    carry = jnp.zeros((tiles, LANE), f32)
    for d in range(blocks):
        s[2][d] = carry
        carry = at(full, d) * carry + (
            moment(d, 2) + at(t31, d) * s[0][d] + at(t32, d) * s[1][d]
        )
    carry = jnp.zeros((tiles, LANE), f32)
    for d in range(blocks - 1, -1, -1):
        s[3][d] = carry
        carry = at(full, d) * carry + (
            moment(d, 3) + at(t41, d) * s[0][d] + at(t42, d) * s[1][d] + at(t21, d) * s[2][d]
        )
    for k in range(4):
        for d in range(blocks):
            for t in range(tiles):
                work[t, k * blocks + d : k * blocks + d + 1, :] = s[k][d][t : t + 1, :]
    done = lon_apply([work[t] for t in range(tiles)], own_first[0], own_mix[0], own_back[0])
    for t in range(tiles):
        for k in range(4):
            replies[:, k * tiles + t, :] = done[t][k * blocks : (k + 1) * blocks]

    @pl.loop(1, blocks)
    def _(step):
        homeward(step).start()

    states[me] = replies[me]
    lon_steps(steps // 2, steps)

    @pl.loop(1, blocks)
    def _(step):
        homeward(step).wait_recv()

    @pl.loop(1, blocks)
    def _(step):
        outward(step).wait_send()
        homeward(step).wait_send()

    groups = rows // count
    levels = groups // variables
    half = tiles // 2
    depth = half * count
    tail = 2 * depth
    zero = jnp.zeros((8, LANE), f32)
    mine_first = core * 4

    def level_remote(src, dst, send_sem, recv_sem, target):
        return pltpu.make_async_remote_copy(
            src_ref=src,
            dst_ref=dst,
            send_sem=send_sem,
            recv_sem=recv_sem,
            device_id={"band": target},
            device_id_type=pl.DeviceIdType.MESH,
        )

    def pair(j):
        return level_remote(
            sums.at[(1 - core) * 4 + j], beside.at[j], pair_send.at[j], pair_recv.at[j], sibling
        )

    for target in range(2 * variables):
        sums[target, tail : tail + 8, :] = coef[target // 2]

    for side in range(2):

        @pl.loop(0, half)
        def _(spot):
            ct = side * half + spot
            done = xs.at[ct]
            for o in range(groups // 8):
                lines = [
                    done[pl.ds(o * 8 * count + r, 8, stride=count), :] for r in range(count)
                ]
                starts = [states[o * 8 : o * 8 + 8, k * tiles + ct, :] for k in range(4)]
                lines, _ = lat_sweeps([lines], [decay_of_octet(table, groups, o)], [starts])
                for r in range(count):
                    done[pl.ds(o * 8 * count + r, 8, stride=count), :] = lines[0][r]
            pltpu.make_async_copy(done, out.at[ct], out_sem.at[ct]).start()
            for var in range(variables):
                for t in range(count // 8):
                    lines = []
                    for lev in range(levels):
                        base = (lev * variables + var) * count + t * 8
                        lines.append(done[base : base + 8, :])
                    _, ends = level_sweeps(
                        lines, lambda lev: vert[lev * variables + var], [zero, zero]
                    )
                    for k in range(2):
                        at = pl.ds(pl.multiple_of(k * depth + spot * count + t * 8, 8), 8)
                        sums[var * 2 + side, at, :] = ends[k]

        for j in (side, side + 2):
            pair(j).start()

    def lower(a, b):
        return jnp.where(core == 0, a, b)

    def row(ref, chunk, at):
        return jnp.broadcast_to(ref[chunk, at : at + 1, :], (8, LANE))

    def bands_of(chunk, at):
        a, b = sums[mine_first + chunk, at, :], beside[chunk, at, :]
        return lower(a, b), lower(b, a)

    def coefficients(chunk):
        both = []
        for at in (tail, tail + 1):
            a, b = row(sums, mine_first + chunk, at), row(beside, chunk, at)
            both.append((lower(a, b), lower(b, a)))
        return both

    def hub_copy(j):
        step = lax.rem(j - chip + 4, 4)
        return level_remote(
            merged.at[j], joined.at[chip], hub_send.at[step - 1], hub_recv.at[step - 1], j * 2 + core
        )

    for j in (0, 2, 1, 3):
        pair(j).wait_recv()
        (full0, full1), (both0, both1) = coefficients(j)

        @pl.loop(0, depth // 8)
        def _(t):
            at = pl.ds(pl.multiple_of(t * 8, 8), 8)
            later = pl.ds(pl.multiple_of(depth + t * 8, 8), 8)
            up0, up1 = bands_of(j, at)
            down0, down1 = bands_of(j, later)
            merged[j, at, :] = full1 * up0 + up1
            merged[j, later, :] = down0 + full0 * (down1 + both1 * up0)

        index = lax.broadcasted_iota(jnp.int32, (8, LANE), 0)
        merged[j, tail : tail + 8, :] = jnp.where(
            index == 0, full0 * full1, both0 + full0 * both1 * full0
        )

        @pl.when(chip != j)
        def _():
            hub_copy(j).start()

    joined[chip] = merged[chip]
    for step in (1, 2, 3):
        hub_copy(lax.rem(chip + step, 4)).wait_recv()

    fulls = [row(joined, c, tail) for c in range(4)]
    boths = [row(joined, c, tail + 1) for c in range(4)]

    @pl.loop(0, depth // 8)
    def _(t):
        at = pl.ds(pl.multiple_of(t * 8, 8), 8)
        later = pl.ds(pl.multiple_of(depth + t * 8, 8), 8)
        state = jnp.zeros((8, LANE), f32)
        ups = []
        for c in range(4):
            ups.append(state)
            answers[c, at, :] = state
            state = fulls[c] * state + joined[c, at, :]
        state = jnp.zeros((8, LANE), f32)
        for c in (3, 2, 1, 0):
            answers[c, later, :] = state
            state = fulls[c] * state + (joined[c, later, :] + boths[c] * ups[c])

    answer_copies = []
    for step in (2, 1, 3):
        copy = level_remote(
            answers.at[lax.rem(chip + step, 4)],
            entering.at[chip],
            reply_send.at[step - 1],
            reply_recv.at[step - 1],
            other(step),
        )
        copy.start()
        answer_copies.append(copy)
    entering[chip] = answers[chip]
    for copy in answer_copies:
        copy.wait_recv()

    last = []
    for j in range(4):
        (full0, full1), (both0, both1) = coefficients(j)

        @pl.loop(0, depth // 8)
        def _(t):
            at = pl.ds(pl.multiple_of(t * 8, 8), 8)
            later = pl.ds(pl.multiple_of(depth + t * 8, 8), 8)
            up0, _ = bands_of(j, at)
            _, down1 = bands_of(j, later)
            below = entering[j, at, :]
            above = entering[j, later, :]
            middle = full0 * below + up0
            turned = full1 * above + (down1 + both1 * middle)
            entered[mine_first + j, at, :] = lower(below, middle)
            entered[mine_first + j, later, :] = lower(turned, above)
            passed[j, at, :] = lower(middle, below)
            passed[j, later, :] = lower(above, turned)

        copy = level_remote(
            passed.at[j], entered.at[mine_first + j], last_send.at[j], last_recv.at[j], sibling
        )
        copy.start()
        last.append(copy)

    for j in range(4):
        pair(j).wait_send()
    for step in (1, 2, 3):
        hub_copy(lax.rem(chip + step, 4)).wait_send()
    for copy in answer_copies:
        copy.wait_send()
    for copy in last:
        copy.wait()
    for ct in range(tiles):
        pltpu.make_async_copy(xs.at[ct], out.at[ct], out_sem.at[ct]).wait()


def exchange(field, moments, decay, table, weights, own_weights, vert, coef, row_count, variables):
    tiles, rows, _ = field.shape
    blocks, depth, _ = moments.shape
    groups = rows // row_count
    steps = groups // LON_STEP
    chunk = tiles * row_count
    any_space = pl.BlockSpec(memory_space=pl.ANY)
    whole = pl.BlockSpec(memory_space=pltpu.VMEM)
    dma = pltpu.SemaphoreType.DMA
    return pl.pallas_call(
        functools.partial(exchange_kernel, row_count, variables),
        out_shape=(
            jax.ShapeDtypeStruct(field.shape, f32),
            jax.ShapeDtypeStruct((2 * variables, chunk, LANE), f32),
        ),
        in_specs=[any_space, whole, whole, whole]
        + [any_space] * 3
        + [whole] * 3
        + [pl.BlockSpec(memory_space=pltpu.SMEM), whole],
        out_specs=(any_space, whole),
        scratch_shapes=[
            pltpu.VMEM(moments.shape, f32),
            pltpu.VMEM(moments.shape, f32),
            pltpu.VMEM(moments.shape, f32),
            pltpu.VMEM((tiles, 4 * blocks, LANE), f32),
            pltpu.VMEM(field.shape, f32),
        ]
        + [pltpu.VMEM(w.shape, w.dtype) for w in weights]
        + [pltpu.VMEM((2 * variables, chunk + 8, LANE), f32)]
        + [pltpu.VMEM((4, chunk + 8, LANE), f32)] * 3
        + [pltpu.VMEM((4, chunk, LANE), f32)] * 3
        + [dma((4, steps)), dma((tiles,))]
        + [dma((blocks - 1,))] * 4
        + [dma((4,)), dma((4,)), dma((3,)), dma((3,)), dma((3,)), dma((3,)), dma((4,)), dma((4,))],
        compiler_params=pltpu.CompilerParams(
            vmem_limit_bytes=60 << 20, collective_id=0, has_side_effects=True
        ),
        cost_estimate=cost(6 * rows * tiles * LANE * 3 * LANE, 60 << 20),
        name="exchange",
    )(field, moments, decay, table, *weights, *own_weights, vert, coef)


def level_sweeps(rows, decay, starts):
    count = len(rows)
    ends = []
    for sweep in range(2):
        order = range(count) if sweep == 0 else range(count - 1, -1, -1)
        state = starts[sweep]
        out = [None] * count
        for r in order:
            state = decay(r) * state + (1.0 - decay(r)) * rows[r]
            out[r] = state
        ends.append(state)
        rows = out
    return rows, ends


def level_states_kernel(source, vert, states, out, x, result, in_sem, sem):
    tiles, levels, variables, row_count, _ = x.shape
    fetches = [
        pltpu.make_async_copy(source.at[:, :, var], x.at[:, :, var], in_sem.at[var])
        for var in range(variables)
    ]
    for fetch in fetches:
        fetch.start()
    writes = []
    for var in range(variables):
        fetches[var].wait()
        decay = [vert[lev * variables + var] for lev in range(levels)]
        for ct in range(tiles):
            for t in range(row_count // 8):
                at = slice(t * 8, t * 8 + 8)
                rows = [x[ct, lev, var, at, :] for lev in range(levels)]
                starts = [states[var, ct // (tiles // 2), k, ct % (tiles // 2), at, :] for k in range(2)]
                rows, _ = level_sweeps(rows, lambda lev: decay[lev], starts)
                for lev in range(levels):
                    result[lev, var, at, ct * LANE : (ct + 1) * LANE] = rows[lev]
        write = pltpu.make_async_copy(result.at[:, var], out.at[:, var], sem.at[var])
        write.start()
        writes.append(write)
    for write in writes:
        write.wait()


def level_states(x, vert, states, shape):
    levels, variables, row_count, columns = shape
    tiles = columns // LANE
    whole = pl.BlockSpec(memory_space=pltpu.VMEM)
    return pl.pallas_call(
        level_states_kernel,
        out_shape=jax.ShapeDtypeStruct(shape, f32),
        in_specs=[pl.BlockSpec(memory_space=pl.ANY), pl.BlockSpec(memory_space=pltpu.SMEM), whole],
        out_specs=pl.BlockSpec(memory_space=pl.ANY),
        scratch_shapes=[
            pltpu.VMEM((tiles, levels, variables, row_count, LANE), f32),
            pltpu.VMEM(shape, f32),
            pltpu.SemaphoreType.DMA((variables,)),
            pltpu.SemaphoreType.DMA((variables,)),
        ],
        compiler_params=vmem(60),
        cost_estimate=cost(0, 11 << 20),
        name="level_states",
    )(x.reshape(tiles, levels, variables, row_count, LANE), vert, states)


def level_coefficients(decays):
    levels = decays.shape[0]
    state, down = jnp.ones_like(decays[0]), []
    for r in range(levels):
        state = decays[r] * state
        down.append(state)
    full = state
    state = jnp.zeros_like(full)
    for r in range(levels - 1, -1, -1):
        state = down[r] + decays[r] * (state - down[r])
    both = jnp.stack([full, state], axis=1)
    both = jnp.pad(both, ((0, 0), (0, 6)))
    return jnp.broadcast_to(both[:, :, None], both.shape + (LANE,))


def per_device(background, obs_columns, obs_owner, obs_cell, lat_length, lon_length, vert_length):
    level_count, var_count, row_count, lon_count = background.shape
    sub_count = lax.axis_size("sub")
    band_count = lax.axis_size("band")
    sub_index = lax.axis_index("sub")
    groups = level_count * var_count
    tiles = lon_count // LANE
    tile_field = background.reshape(groups * row_count, lon_count)
    owners = obs_owner[:, 0]
    capacity = 2 * owners.shape[0] // sub_count

    ranks = route_ranks(owners, sub_count)
    row, column = obs_cell // lon_count, obs_cell % lon_count
    place = ((row // 4) * lon_count + column) * 4 + row % 4
    lines = capacity // LANE
    message = pack(owners * capacity + ranks, place, obs_columns, sub_count)
    got = lax.all_to_all(message.reshape(sub_count, -1, LANE), "sub", 0, 0, tiled=True)

    vert_decay = jnp.exp(-1.0 / vert_length)
    coef = level_coefficients(vert_decay)
    vert_decay = vert_decay.reshape(groups)

    lat_all = jnp.exp(-1.0 / lat_length).reshape(groups, sub_count, row_count)
    own_lat = lax.dynamic_index_in_dim(lat_all, sub_index, 1, False)
    own_lat = own_lat.T.reshape(row_count * groups, 1)
    own_lat = jnp.concatenate([own_lat, 1.0 - own_lat])
    decay = jnp.broadcast_to(own_lat, (2 * row_count * groups, LANE))
    hub_lat = lax.dynamic_index_in_dim(lat_all, sub_index, 0, False)
    hub_lat = jnp.pad(hub_lat.T, ((0, 0), (0, LANE - sub_count)))

    lengths = lon_length.reshape(groups)
    weights = lon_weights(lengths, lon_count)
    own_weights = [lax.dynamic_slice_in_dim(w, sub_index, 1, 0) for w in weights]

    ready = (got, weights, own_weights, decay, hub_lat, coef, vert_decay)
    got, weights, own_weights, decay, hub_lat, coef, vert_decay = lax.optimization_barrier(ready)
    places = got[:, capacity // 4 : capacity // 4 + lines, :].reshape(-1).astype(jnp.int32)
    quarters = (places & 3).astype(f32).reshape(sub_count, 4, capacity // 4)
    quarters = jnp.pad(quarters, ((0, 0), (0, 4), (0, 0)))
    forced, moments = force(places >> 2, got, quarters, tile_field, decay, row_count, groups)
    smooth, entering = exchange(
        forced,
        moments.reshape(sub_count, 4 * tiles, LANE),
        hub_lat,
        decay,
        weights,
        own_weights,
        vert_decay,
        coef,
        row_count,
        var_count,
    )
    return level_states(
        smooth,
        vert_decay,
        entering.reshape(var_count, 2, 2, tiles // 2, row_count, LANE),
        background.shape,
    )


def solution(mesh):
    placed = (
        P("band", None, "sub", None),
        P("band", None, "sub"),
        P("sub", None),
        P("sub"),
        P("band", None, None),
        P("band", None),
        P("band", None),
    )
    return jax.shard_map(
        per_device,
        mesh=mesh,
        in_specs=placed,
        out_specs=P("band", None, "sub", None),
        check_vma=False,
    )
```

```python
import functools

import jax
import jax.numpy as jnp
from jax import lax
from jax.experimental import pallas as pl
from jax.experimental.pallas import tpu as pltpu
from jax.sharding import PartitionSpec as P

LANE = 128
f32 = jnp.float32
bf16 = jnp.bfloat16


def vmem(mib):
    return pltpu.CompilerParams(vmem_limit_bytes=mib << 20)


def cost(flops, moved):
    return pl.CostEstimate(flops=flops, bytes_accessed=moved, transcendentals=0)


def route_ranks(owners, sub_count):
    count = owners.shape[0]
    block = 128
    owner_block = owners.reshape(count // block, block)
    match = (owner_block[:, :, None] == jnp.arange(sub_count, dtype=jnp.int32)).astype(bf16)
    position = jnp.arange(block)
    lower = (position[:, None] > position[None, :]).astype(bf16)
    ahead = jnp.einsum("ij,bjo->bio", lower, match, preferred_element_type=f32)
    totals = jnp.sum(match.astype(f32), axis=1)
    base = jnp.cumsum(totals, axis=0) - totals
    rank = jnp.sum((ahead + base[:, None, :]) * match.astype(f32), axis=2)
    return rank.reshape(count).astype(jnp.int32)


def pack_kernel(slots, slot_row, place_row, values, packed, rows, big):
    levels, _, count = values.shape
    total = big.shape[0]
    targets = total // 256
    size = packed.shape[0] // targets
    share = total // (count // LANE)

    for j in range(count // LANE):
        big[j * share : (j + 1) * share, :] = jnp.zeros((share, LANE), f32)
        part = jnp.concatenate(
            [values[lev, :, j * LANE : (j + 1) * LANE] for lev in range(levels)], axis=0
        )
        rows[j * LANE : (j + 1) * LANE, :] = jnp.concatenate([part] * 4, axis=0).T

    slot, place = slot_row[...], place_row[...]
    owner, rank = lax.shift_right_logical(slot, 8), slot & 255
    mine = owner == lax.broadcasted_iota(jnp.int32, (targets, count), 0)
    spot = (rank == lax.broadcasted_iota(jnp.int32, (256, count), 0)).astype(f32).astype(bf16)

    def put(half):
        return jnp.where(mine, half, 0).astype(f32).astype(bf16)

    both = lax.dot_general(
        jnp.concatenate([put(lax.shift_right_logical(place, 8)), put(place & 255)], axis=0),
        spot,
        (((1,), (1,)), ((), ())),
        preferred_element_type=f32,
    )
    cells = both[:targets] * 256.0 + both[targets:]
    for half in range(2):
        packed[pl.ds(64 + half, targets, stride=size), :] = cells[:, half * LANE : (half + 1) * LANE]

    step = PACK_STEP

    @pl.loop(0, count // step)
    def _(i):
        for u in range(step):
            j = i * step + u
            big[pl.ds(slots[j], 1), :] = rows[pl.ds(j, 1), :]

    quarter = lax.broadcasted_iota(jnp.int32, (64, LANE), 1) // 32

    @pl.loop(0, targets // PACK_SIDE)
    def _(i):
        run = packed.at[pl.ds(pl.multiple_of(i * PACK_SIDE * size, 8), PACK_SIDE * size), :]
        for e in range(PACK_SIDE):
            start = pl.multiple_of((i * PACK_SIDE + e) * 256, 256)
            out = big[pl.ds(start, 64), :]
            for k in range(1, 4):
                out = jnp.where(quarter == k, big[pl.ds(start + 64 * k, 64), :], out)
            run[e * size : e * size + 64, :] = out


PACK_STEP = 64
PACK_SIDE = 8


def pack(slots, place, values, targets):
    count = values.shape[2]
    total = targets * 256
    whole = pl.BlockSpec(memory_space=pltpu.VMEM)
    return pl.pallas_call(
        pack_kernel,
        out_shape=jax.ShapeDtypeStruct((targets * 66, LANE), f32),
        in_specs=[pl.BlockSpec(memory_space=pltpu.SMEM), whole, whole, whole],
        out_specs=whole,
        scratch_shapes=[pltpu.VMEM((count, LANE), f32), pltpu.VMEM((total, LANE), f32)],
        compiler_params=vmem(60),
        cost_estimate=cost(0, 4 << 20),
        name="pack",
    )(slots, slots.reshape(1, count), place.reshape(1, count), values)


def lat_sweeps(sets, decays, starts):
    count = len(sets[0])
    ends = [[] for _ in sets]
    for sweep in range(4):
        order = range(count) if sweep % 2 == 0 else range(count - 1, -1, -1)
        states = [start[sweep] for start in starts]
        outs = [[None] * count for _ in sets]
        for r in order:
            for i, rows in enumerate(sets):
                a, rest = decays[i](r)
                states[i] = a * states[i] + rest * rows[r]
                outs[i][r] = states[i]
        for i in range(len(sets)):
            ends[i].append(states[i])
        sets = outs
    return sets, ends


def decay_of_octet(decay, groups, o):
    rows = decay.shape[0] // 2

    def pair(r):
        at = r * groups + o * 8
        return decay[at : at + 8, :], decay[rows + at : rows + at + 8, :]

    return pair


CHAINS = 8
SIDE = 1


def forced_kernel(row_count, groups, places, got, background, decay, forced, moments, spread, field, sem, out_sem, *chains):
    total = spread.shape[0]
    depth = chains[0].shape[0]
    sources = spread.shape[0] // 256
    size = got.shape[0] // sources
    tiles = forced.shape[0]
    fetches = [
        pltpu.make_async_copy(
            background.at[:, ct * LANE : (ct + 1) * LANE], field.at[ct], sem.at[ct]
        )
        for ct in range(tiles)
    ]
    for fetch in fetches:
        fetch.start()

    row = lax.broadcasted_iota(jnp.int32, (8, LANE), 0)
    pick = (row == 0).astype(f32).astype(bf16)
    quarter = lax.broadcasted_iota(jnp.int32, (64, LANE), 1) // 32
    wanted = quarter.astype(f32)

    def turns(x):
        return [x] + [pltpu.roll(x, 32 * k, 1) for k in range(1, 4)]

    def repeat(turned, k):
        out = turned[(3 - k) % 4]
        for q in range(3):
            out = jnp.where(quarter == q, turned[(q - k) % 4], out)
        return out

    share = depth // sources
    together = 4

    @pl.loop(0, sources // together)
    def _(i):
        run = got.at[pl.ds(pl.multiple_of(i * together * size, 8), together * size), :]
        for e in range(together):
            d = i * together + e
            at = pl.ds(pl.multiple_of(d * share, 8), share)
            for chain in chains:
                chain[at, :] = jnp.zeros((share, LANE), f32)
            part = turns(run[e * size : e * size + 64, :])
            for half in range(2):
                cell = run[e * size + 64 + half : e * size + 65 + half, :]
                mark = lax.dot_general(
                    jnp.broadcast_to(cell - 4.0 * jnp.floor(cell * 0.25), (8, LANE)).astype(bf16),
                    pick,
                    (((0,), (0,)), ((), ())),
                    preferred_element_type=f32,
                )
                for k in (2 * half, 2 * half + 1):
                    first = (k % 2) * 64
                    one = jnp.where(mark[first : first + 64] == wanted, repeat(part, k), 0.0)
                    spread[pl.ds(pl.multiple_of(d * 256 + k * 64, 64), 64), :] = one

    step = 16

    @pl.loop(0, total // (CHAINS * step))
    def _(i):
        for u in range(step):
            spots = [(i * step + u) * CHAINS + c for c in range(CHAINS)]
            where = [pl.ds(places[j], 1) for j in spots]
            adds = [spread[pl.ds(j, 1), :] for j in spots]
            olds = [chains[c][where[c], :] for c in range(CHAINS)]
            for c in range(CHAINS):
                chains[c][where[c], :] = olds[c] + adds[c]

    for fetch in fetches:
        fetch.wait()
    columns = depth // (row_count // 4)

    @pl.loop(0, tiles)
    def _(ct):
        out = field.at[ct]
        for rr in range(row_count // 4):
            at = pl.ds(pl.multiple_of(rr * columns + ct * LANE, LANE), LANE)
            parts = [chain[at, :] for chain in chains]
            while len(parts) > 1:
                parts = [a + b for a, b in zip(parts[::2], parts[1::2])]
            turned = parts[0].T
            for q in range(4):
                for o in range(groups // 8):
                    at = pl.ds(o * 8 * row_count + rr * 4 + q, 8, stride=row_count)
                    first = q * groups + o * 8
                    out[at, :] = out[at, :] + turned[first : first + 8, :]
        pltpu.make_async_copy(field.at[ct], forced.at[ct], out_sem.at[ct]).start()
        zero = jnp.zeros((8, LANE), f32)
        per_group = moments.shape[0] // groups
        for first in range(0, groups // 8, SIDE):
            octets = range(first, first + SIDE)
            sets = [
                [
                    out[pl.ds(o * 8 * row_count + r, 8, stride=row_count), :]
                    for r in range(row_count)
                ]
                for o in octets
            ]
            _, ends = lat_sweeps(
                sets, [decay_of_octet(decay, groups, o) for o in octets], [[zero] * 4] * SIDE
            )
            for i, o in enumerate(octets):
                for k in range(4):
                    start = o * 8 * per_group + k * (per_group // 4) + ct
                    moments[pl.ds(start, 8, stride=per_group), :] = ends[i][k]

    for ct in range(tiles):
        pltpu.make_async_copy(field.at[ct], forced.at[ct], out_sem.at[ct]).wait()


def force(places, got, background, decay, row_count, groups):
    rows, columns = background.shape
    tiles = columns // LANE
    total = places.shape[0]
    depth = rows * columns // LANE
    whole = pl.BlockSpec(memory_space=pltpu.VMEM)
    return pl.pallas_call(
        functools.partial(forced_kernel, row_count, groups),
        out_shape=(
            jax.ShapeDtypeStruct((tiles, rows, LANE), f32),
            jax.ShapeDtypeStruct((groups * 4 * tiles, LANE), f32),
        ),
        in_specs=[
            pl.BlockSpec(memory_space=pltpu.SMEM),
            whole,
            pl.BlockSpec(memory_space=pl.ANY),
            whole,
        ],
        out_specs=(pl.BlockSpec(memory_space=pl.ANY), whole),
        scratch_shapes=[
            pltpu.VMEM((total, LANE), f32),
            pltpu.VMEM((tiles, rows, LANE), f32),
            pltpu.SemaphoreType.DMA((tiles,)),
            pltpu.SemaphoreType.DMA((tiles,)),
        ]
        + [pltpu.VMEM((depth, LANE), f32)] * CHAINS,
        compiler_params=vmem(58),
        cost_estimate=cost(0, 16 << 20),
        name="force",
    )(places, got, background, decay)


def lon_weights(length, columns):
    blocks = columns // LANE
    length = length[:, None, None]
    kappa = jnp.tanh(0.5 / length)
    beta = kappa * kappa
    alpha = beta / jnp.tanh(1.0 / length)
    i = jnp.arange(LANE, dtype=f32)

    def power(n):
        return jnp.exp(-n / length)

    gap = jnp.abs(i[:, None] - i[None, :])[None]
    local = (alpha + beta * gap) * power(gap)
    up, down = i[None, :, None], (LANE - 1.0) - i[None, :, None]
    sums = jnp.concatenate(
        [power(down), down * power(down), power(up), up * power(up)], axis=2
    )
    sums = jnp.pad(sums, ((0, 0), (0, 0), (0, LANE - 4)))
    first = jnp.concatenate([local, sums], axis=2)
    index = jnp.arange(LANE)
    src, dst = index[:, None], index[None, :]
    source, target = src // 4, dst // 4
    backward = (src % 4) >= 2
    steps = jnp.where(backward, source - target - 1, target - source - 1) % blocks
    gap = (LANE * steps).astype(f32)[None]
    turn = power(float(columns))
    left = -jnp.expm1(-float(columns) / length)
    same = power(gap) / left
    cross = (gap + columns * turn / left) * same
    used = (source < blocks) & (target < blocks)
    mix = jnp.where((used & (src % 4 == dst % 4))[None], same, 0.0)
    mix = jnp.where((used & (src % 2 == 0) & (dst % 4 == src % 4 + 1))[None], cross, mix)
    near, far = i[None, None, :] + 1.0, LANE - i[None, None, :]
    back = jnp.concatenate(
        [
            (alpha + beta * near) * power(near),
            beta * power(near),
            (alpha + beta * far) * power(far),
            beta * power(far),
        ],
        axis=1,
    )
    back = jnp.pad(back, ((0, 0), (0, LANE - 4), (0, 0)))
    return thirds(first), thirds(mix), thirds(back)


def thirds(w):
    high = lax.reduce_precision(w, 8, 7)
    low = (w - high).astype(bf16)
    high = high.astype(bf16)
    return jnp.concatenate([high, high, low], axis=1)


def dot3(x, w):
    high = x.astype(bf16)
    low = (x - high.astype(f32)).astype(bf16)
    return jnp.dot(jnp.concatenate([high, low, high], axis=1), w, preferred_element_type=f32)


def lon_apply(parts, first, mix, back):
    count, blocks = parts[0].shape[0], len(parts)
    both = dot3(jnp.concatenate(parts, axis=0), first)
    local, sums = both[:, :LANE], both[:, LANE:]
    line = sums[:count]
    for b in range(1, blocks):
        line = line + pltpu.roll(sums[b * count : (b + 1) * count], 4 * b, 1)
    states = dot3(line, mix)
    spread = jnp.concatenate(
        [states] + [pltpu.roll(states, LANE - 4 * b, 1) for b in range(1, blocks)], axis=0
    )
    out = local + dot3(spread, back)
    return [out[b * count : (b + 1) * count] for b in range(blocks)]


LON_STEP = 4


def hub_coefficients(decay):
    count = decay.shape[0]
    coef = [decay[r : r + 1, :] for r in range(count)]

    def forward(rows):
        state, out = jnp.zeros((1, LANE), f32), []
        for r in range(count):
            state = rows[r] + coef[r] * (state - rows[r])
            out.append(state)
        return out

    def backward(rows):
        state, out = jnp.zeros((1, LANE), f32), [None] * count
        for r in range(count - 1, -1, -1):
            state = rows[r] + coef[r] * (state - rows[r])
            out[r] = state
        return out

    state, down = jnp.ones((1, LANE), f32), []
    for r in range(count):
        state = coef[r] * state
        down.append(state)
    full = state
    state, up = jnp.ones((1, LANE), f32), [None] * count
    for r in range(count - 1, -1, -1):
        state = coef[r] * state
        up[r] = state
    bp = backward(down)
    fbp = forward(bp)
    bfbp = backward(fbp)
    fq = forward(up)
    bfq = backward(fq)
    return full, bp[0], fbp[-1], bfbp[0], fq[-1], bfq[0]


def exchange_kernel(
    count, variables, field, moments, decay, table, first, mix, back, own_first, own_mix, own_back,
    vert, coef, out, entered, arrived, replies, states, work, xs, ws, ms, bs, sums, beside, merged,
    joined, answers, entering, passed, sems, out_sem, send, recv, back_send, back_recv, pair_send,
    pair_recv, hub_send, hub_recv, reply_send, reply_recv, last_send, last_recv,
):
    tiles, rows, _ = out.shape
    blocks = arrived.shape[0]
    me = lax.axis_index("sub")
    steps = rows // count // LON_STEP
    size = LON_STEP * count

    def fetches(i):
        group = i * LON_STEP
        at = pl.ds(pl.multiple_of(group * count, 8), size)
        inside = pl.ds(group, LON_STEP)
        return [
            pltpu.make_async_copy(field.at[:, at], xs.at[:, at], sems.at[0, i]),
            pltpu.make_async_copy(first.at[inside], ws.at[inside], sems.at[1, i]),
            pltpu.make_async_copy(mix.at[inside], ms.at[inside], sems.at[2, i]),
            pltpu.make_async_copy(back.at[inside], bs.at[inside], sems.at[3, i]),
        ]

    for i in range(steps):
        for fetch in fetches(i):
            fetch.start()

    def lon_steps(start, stop):
        @pl.loop(start, stop)
        def _(i):
            for fetch in fetches(i):
                fetch.wait()
            for u in range(LON_STEP):
                g = i * LON_STEP + u
                at = pl.ds(pl.multiple_of(g * count, 8), count)
                parts = lon_apply([xs[b, at, :] for b in range(tiles)], ws[g], ms[g], bs[g])
                for b in range(tiles):
                    xs[b, at, :] = parts[b]

    barrier = pltpu.get_barrier_semaphore()

    @pl.loop(1, blocks)
    def _(step):
        target = lax.rem(me + step, blocks)
        pl.semaphore_signal(
            barrier, inc=1, device_id={"sub": target}, device_id_type=pl.DeviceIdType.MESH
        )

    band = lax.axis_index("band")
    chip, core = band // 2, band % 2
    sibling = chip * 2 + (1 - core)

    def other(step):
        return lax.rem(chip + step, 4) * 2 + core

    for target in [sibling] + [other(step) for step in (1, 2, 3)]:
        pl.semaphore_signal(
            barrier, inc=1, device_id={"band": target}, device_id_type=pl.DeviceIdType.MESH
        )
    pl.semaphore_wait(barrier, blocks - 1 + 4)

    def outward(step):
        target = lax.rem(me + step, blocks)
        return pltpu.make_async_remote_copy(
            src_ref=moments.at[target],
            dst_ref=arrived.at[me],
            send_sem=send.at[step - 1],
            recv_sem=recv.at[step - 1],
            device_id={"sub": target},
            device_id_type=pl.DeviceIdType.MESH,
        )

    def homeward(step):
        target = lax.rem(me + step, blocks)
        return pltpu.make_async_remote_copy(
            src_ref=replies.at[target],
            dst_ref=states.at[me],
            send_sem=back_send.at[step - 1],
            recv_sem=back_recv.at[step - 1],
            device_id={"sub": target},
            device_id_type=pl.DeviceIdType.MESH,
        )

    @pl.loop(1, blocks)
    def _(step):
        outward(step).start()

    arrived[me] = moments[me]
    full, t21, t31, t41, t32, t42 = hub_coefficients(decay)
    lon_steps(0, steps // 2)

    @pl.loop(1, blocks)
    def _(step):
        outward(step).wait_recv()

    def at(table, d):
        return jnp.broadcast_to(table[:, d : d + 1], (tiles, LANE))

    def moment(d, k):
        return arrived[d, k * tiles : (k + 1) * tiles, :]

    carry = jnp.zeros((tiles, LANE), f32)
    s = [[None] * blocks for _ in range(4)]
    for d in range(blocks):
        s[0][d] = carry
        carry = at(full, d) * carry + moment(d, 0)
    carry = jnp.zeros((tiles, LANE), f32)
    for d in range(blocks - 1, -1, -1):
        s[1][d] = carry
        carry = at(full, d) * carry + (moment(d, 1) + at(t21, d) * s[0][d])
    carry = jnp.zeros((tiles, LANE), f32)
    for d in range(blocks):
        s[2][d] = carry
        carry = at(full, d) * carry + (
            moment(d, 2) + at(t31, d) * s[0][d] + at(t32, d) * s[1][d]
        )
    carry = jnp.zeros((tiles, LANE), f32)
    for d in range(blocks - 1, -1, -1):
        s[3][d] = carry
        carry = at(full, d) * carry + (
            moment(d, 3) + at(t41, d) * s[0][d] + at(t42, d) * s[1][d] + at(t21, d) * s[2][d]
        )
    for k in range(4):
        for d in range(blocks):
            for t in range(tiles):
                work[t, k * blocks + d : k * blocks + d + 1, :] = s[k][d][t : t + 1, :]
    done = lon_apply([work[t] for t in range(tiles)], own_first[0], own_mix[0], own_back[0])
    for t in range(tiles):
        for k in range(4):
            replies[:, k * tiles + t, :] = done[t][k * blocks : (k + 1) * blocks]

    @pl.loop(1, blocks)
    def _(step):
        homeward(step).start()

    states[me] = replies[me]
    lon_steps(steps // 2, steps)

    @pl.loop(1, blocks)
    def _(step):
        homeward(step).wait_recv()

    @pl.loop(1, blocks)
    def _(step):
        outward(step).wait_send()
        homeward(step).wait_send()

    groups = rows // count
    levels = groups // variables
    half = tiles // 2
    depth = half * count
    tail = 2 * depth
    zero = jnp.zeros((8, LANE), f32)
    mine_first = core * 4

    def level_remote(src, dst, send_sem, recv_sem, target):
        return pltpu.make_async_remote_copy(
            src_ref=src,
            dst_ref=dst,
            send_sem=send_sem,
            recv_sem=recv_sem,
            device_id={"band": target},
            device_id_type=pl.DeviceIdType.MESH,
        )

    def pair(j):
        return level_remote(
            sums.at[(1 - core) * 4 + j], beside.at[j], pair_send.at[j], pair_recv.at[j], sibling
        )

    for target in range(2 * variables):
        sums[target, tail : tail + 8, :] = coef[target // 2]

    for side in range(2):

        @pl.loop(0, half)
        def _(spot):
            ct = side * half + spot
            done = xs.at[ct]
            for o in range(groups // 8):
                lines = [
                    done[pl.ds(o * 8 * count + r, 8, stride=count), :] for r in range(count)
                ]
                starts = [states[o * 8 : o * 8 + 8, k * tiles + ct, :] for k in range(4)]
                lines, _ = lat_sweeps([lines], [decay_of_octet(table, groups, o)], [starts])
                for r in range(count):
                    done[pl.ds(o * 8 * count + r, 8, stride=count), :] = lines[0][r]
            pltpu.make_async_copy(done, out.at[ct], out_sem.at[ct]).start()
            for var in range(variables):
                for t in range(count // 8):
                    lines = []
                    for lev in range(levels):
                        base = (lev * variables + var) * count + t * 8
                        lines.append(done[base : base + 8, :])
                    _, ends = level_sweeps(
                        lines, lambda lev: vert[lev * variables + var], [zero, zero]
                    )
                    for k in range(2):
                        at = pl.ds(pl.multiple_of(k * depth + spot * count + t * 8, 8), 8)
                        sums[var * 2 + side, at, :] = ends[k]

        for j in (side, side + 2):
            pair(j).start()

    def lower(a, b):
        return jnp.where(core == 0, a, b)

    def row(ref, chunk, at):
        return jnp.broadcast_to(ref[chunk, at : at + 1, :], (8, LANE))

    def bands_of(chunk, at):
        a, b = sums[mine_first + chunk, at, :], beside[chunk, at, :]
        return lower(a, b), lower(b, a)

    def coefficients(chunk):
        both = []
        for at in (tail, tail + 1):
            a, b = row(sums, mine_first + chunk, at), row(beside, chunk, at)
            both.append((lower(a, b), lower(b, a)))
        return both

    def hub_copy(j):
        step = lax.rem(j - chip + 4, 4)
        return level_remote(
            merged.at[j], joined.at[chip], hub_send.at[step - 1], hub_recv.at[step - 1], j * 2 + core
        )

    for j in (0, 2, 1, 3):
        pair(j).wait_recv()
        (full0, full1), (both0, both1) = coefficients(j)

        @pl.loop(0, depth // 8)
        def _(t):
            at = pl.ds(pl.multiple_of(t * 8, 8), 8)
            later = pl.ds(pl.multiple_of(depth + t * 8, 8), 8)
            up0, up1 = bands_of(j, at)
            down0, down1 = bands_of(j, later)
            merged[j, at, :] = full1 * up0 + up1
            merged[j, later, :] = down0 + full0 * (down1 + both1 * up0)

        index = lax.broadcasted_iota(jnp.int32, (8, LANE), 0)
        merged[j, tail : tail + 8, :] = jnp.where(
            index == 0, full0 * full1, both0 + full0 * both1 * full0
        )

        @pl.when(chip != j)
        def _():
            hub_copy(j).start()

    joined[chip] = merged[chip]
    for step in (1, 2, 3):
        hub_copy(lax.rem(chip + step, 4)).wait_recv()

    fulls = [row(joined, c, tail) for c in range(4)]
    boths = [row(joined, c, tail + 1) for c in range(4)]

    @pl.loop(0, depth // 8)
    def _(t):
        at = pl.ds(pl.multiple_of(t * 8, 8), 8)
        later = pl.ds(pl.multiple_of(depth + t * 8, 8), 8)
        state = jnp.zeros((8, LANE), f32)
        ups = []
        for c in range(4):
            ups.append(state)
            answers[c, at, :] = state
            state = fulls[c] * state + joined[c, at, :]
        state = jnp.zeros((8, LANE), f32)
        for c in (3, 2, 1, 0):
            answers[c, later, :] = state
            state = fulls[c] * state + (joined[c, later, :] + boths[c] * ups[c])

    answer_copies = []
    for step in (2, 1, 3):
        copy = level_remote(
            answers.at[lax.rem(chip + step, 4)],
            entering.at[chip],
            reply_send.at[step - 1],
            reply_recv.at[step - 1],
            other(step),
        )
        copy.start()
        answer_copies.append(copy)
    entering[chip] = answers[chip]
    for copy in answer_copies:
        copy.wait_recv()

    last = []
    for j in range(4):
        (full0, full1), (both0, both1) = coefficients(j)

        @pl.loop(0, depth // 8)
        def _(t):
            at = pl.ds(pl.multiple_of(t * 8, 8), 8)
            later = pl.ds(pl.multiple_of(depth + t * 8, 8), 8)
            up0, _ = bands_of(j, at)
            _, down1 = bands_of(j, later)
            below = entering[j, at, :]
            above = entering[j, later, :]
            middle = full0 * below + up0
            turned = full1 * above + (down1 + both1 * middle)
            entered[mine_first + j, at, :] = lower(below, middle)
            entered[mine_first + j, later, :] = lower(turned, above)
            passed[j, at, :] = lower(middle, below)
            passed[j, later, :] = lower(above, turned)

        copy = level_remote(
            passed.at[j], entered.at[mine_first + j], last_send.at[j], last_recv.at[j], sibling
        )
        copy.start()
        last.append(copy)

    for j in range(4):
        pair(j).wait_send()
    for step in (1, 2, 3):
        hub_copy(lax.rem(chip + step, 4)).wait_send()
    for copy in answer_copies:
        copy.wait_send()
    for copy in last:
        copy.wait()
    for ct in range(tiles):
        pltpu.make_async_copy(xs.at[ct], out.at[ct], out_sem.at[ct]).wait()


def exchange(field, moments, decay, table, weights, own_weights, vert, coef, row_count, variables):
    tiles, rows, _ = field.shape
    blocks, depth, _ = moments.shape
    groups = rows // row_count
    steps = groups // LON_STEP
    chunk = tiles * row_count
    any_space = pl.BlockSpec(memory_space=pl.ANY)
    whole = pl.BlockSpec(memory_space=pltpu.VMEM)
    dma = pltpu.SemaphoreType.DMA
    return pl.pallas_call(
        functools.partial(exchange_kernel, row_count, variables),
        out_shape=(
            jax.ShapeDtypeStruct(field.shape, f32),
            jax.ShapeDtypeStruct((2 * variables, chunk, LANE), f32),
        ),
        in_specs=[any_space, whole, whole, whole]
        + [any_space] * 3
        + [whole] * 3
        + [pl.BlockSpec(memory_space=pltpu.SMEM), whole],
        out_specs=(any_space, whole),
        scratch_shapes=[
            pltpu.VMEM(moments.shape, f32),
            pltpu.VMEM(moments.shape, f32),
            pltpu.VMEM(moments.shape, f32),
            pltpu.VMEM((tiles, 4 * blocks, LANE), f32),
            pltpu.VMEM(field.shape, f32),
        ]
        + [pltpu.VMEM(w.shape, w.dtype) for w in weights]
        + [pltpu.VMEM((2 * variables, chunk + 8, LANE), f32)]
        + [pltpu.VMEM((4, chunk + 8, LANE), f32)] * 3
        + [pltpu.VMEM((4, chunk, LANE), f32)] * 3
        + [dma((4, steps)), dma((tiles,))]
        + [dma((blocks - 1,))] * 4
        + [dma((4,)), dma((4,)), dma((3,)), dma((3,)), dma((3,)), dma((3,)), dma((4,)), dma((4,))],
        compiler_params=pltpu.CompilerParams(
            vmem_limit_bytes=60 << 20, collective_id=0, has_side_effects=True
        ),
        cost_estimate=cost(6 * rows * tiles * LANE * 3 * LANE, 60 << 20),
        name="exchange",
    )(field, moments, decay, table, *weights, *own_weights, vert, coef)


def level_sweeps(rows, decay, starts):
    count = len(rows)
    ends = []
    for sweep in range(2):
        order = range(count) if sweep == 0 else range(count - 1, -1, -1)
        state = starts[sweep]
        out = [None] * count
        for r in order:
            state = decay(r) * state + (1.0 - decay(r)) * rows[r]
            out[r] = state
        ends.append(state)
        rows = out
    return rows, ends


def level_states_kernel(source, vert, states, out, x, result, in_sem, sem):
    tiles, levels, variables, row_count, _ = x.shape
    fetches = [
        pltpu.make_async_copy(source.at[:, :, var], x.at[:, :, var], in_sem.at[var])
        for var in range(variables)
    ]
    for fetch in fetches:
        fetch.start()
    writes = []
    for var in range(variables):
        fetches[var].wait()
        decay = [vert[lev * variables + var] for lev in range(levels)]
        for ct in range(tiles):
            for t in range(row_count // 8):
                at = slice(t * 8, t * 8 + 8)
                rows = [x[ct, lev, var, at, :] for lev in range(levels)]
                starts = [states[var, ct // (tiles // 2), k, ct % (tiles // 2), at, :] for k in range(2)]
                rows, _ = level_sweeps(rows, lambda lev: decay[lev], starts)
                for lev in range(levels):
                    result[lev, var, at, ct * LANE : (ct + 1) * LANE] = rows[lev]
        write = pltpu.make_async_copy(result.at[:, var], out.at[:, var], sem.at[var])
        write.start()
        writes.append(write)
    for write in writes:
        write.wait()


def level_states(x, vert, states, shape):
    levels, variables, row_count, columns = shape
    tiles = columns // LANE
    whole = pl.BlockSpec(memory_space=pltpu.VMEM)
    return pl.pallas_call(
        level_states_kernel,
        out_shape=jax.ShapeDtypeStruct(shape, f32),
        in_specs=[pl.BlockSpec(memory_space=pl.ANY), pl.BlockSpec(memory_space=pltpu.SMEM), whole],
        out_specs=pl.BlockSpec(memory_space=pl.ANY),
        scratch_shapes=[
            pltpu.VMEM((tiles, levels, variables, row_count, LANE), f32),
            pltpu.VMEM(shape, f32),
            pltpu.SemaphoreType.DMA((variables,)),
            pltpu.SemaphoreType.DMA((variables,)),
        ],
        compiler_params=vmem(60),
        cost_estimate=cost(0, 11 << 20),
        name="level_states",
    )(x.reshape(tiles, levels, variables, row_count, LANE), vert, states)


def level_coefficients(decays):
    levels = decays.shape[0]
    state, down = jnp.ones_like(decays[0]), []
    for r in range(levels):
        state = decays[r] * state
        down.append(state)
    full = state
    state = jnp.zeros_like(full)
    for r in range(levels - 1, -1, -1):
        state = down[r] + decays[r] * (state - down[r])
    both = jnp.stack([full, state], axis=1)
    both = jnp.pad(both, ((0, 0), (0, 6)))
    return jnp.broadcast_to(both[:, :, None], both.shape + (LANE,))


def per_device(background, obs_columns, obs_owner, obs_cell, lat_length, lon_length, vert_length):
    level_count, var_count, row_count, lon_count = background.shape
    sub_count = lax.axis_size("sub")
    band_count = lax.axis_size("band")
    sub_index = lax.axis_index("sub")
    groups = level_count * var_count
    tiles = lon_count // LANE
    tile_field = background.reshape(groups * row_count, lon_count)
    owners = obs_owner[:, 0]
    capacity = 2 * owners.shape[0] // sub_count

    ranks = route_ranks(owners, sub_count)
    row, column = obs_cell // lon_count, obs_cell % lon_count
    place = ((row // 4) * lon_count + column) * 4 + row % 4
    message = pack(owners * capacity + ranks, place, obs_columns, sub_count)
    got = lax.all_to_all(message.reshape(sub_count, 1, -1), "sub", 0, 0, tiled=True)

    vert_decay = jnp.exp(-1.0 / vert_length)
    coef = level_coefficients(vert_decay)
    vert_decay = vert_decay.reshape(groups)

    lat_all = jnp.exp(-1.0 / lat_length).reshape(groups, sub_count, row_count)
    own_lat = lax.dynamic_index_in_dim(lat_all, sub_index, 1, False)
    own_lat = own_lat.T.reshape(row_count * groups, 1)
    own_lat = jnp.concatenate([own_lat, 1.0 - own_lat])
    decay = jnp.broadcast_to(own_lat, (2 * row_count * groups, LANE))
    hub_lat = lax.dynamic_index_in_dim(lat_all, sub_index, 0, False)
    hub_lat = jnp.pad(hub_lat.T, ((0, 0), (0, LANE - sub_count)))

    lengths = lon_length.reshape(groups)
    weights = lon_weights(lengths, lon_count)
    own_weights = [lax.dynamic_slice_in_dim(w, sub_index, 1, 0) for w in weights]

    ready = (got, weights, own_weights, decay, hub_lat, coef, vert_decay)
    got, weights, own_weights, decay, hub_lat, coef, vert_decay = lax.optimization_barrier(ready)
    places = got[:, 0, capacity * groups :].reshape(-1).astype(jnp.int32)
    forced, moments = force(places >> 2, got.reshape(-1, LANE), tile_field, decay, row_count, groups)
    smooth, entering = exchange(
        forced,
        moments.reshape(sub_count, 4 * tiles, LANE),
        hub_lat,
        decay,
        weights,
        own_weights,
        vert_decay,
        coef,
        row_count,
        var_count,
    )
    return level_states(
        smooth,
        vert_decay,
        entering.reshape(var_count, 2, 2, tiles // 2, row_count, LANE),
        background.shape,
    )


def solution(mesh):
    placed = (
        P("band", None, "sub", None),
        P("band", None, "sub"),
        P("sub", None),
        P("sub"),
        P("band", None, None),
        P("band", None),
        P("band", None),
    )
    return jax.shard_map(
        per_device,
        mesh=mesh,
        in_specs=placed,
        out_specs=P("band", None, "sub", None),
        check_vma=False,
    )
```

```python
import functools

import jax
import jax.numpy as jnp
from jax import lax
from jax.experimental import pallas as pl
from jax.experimental.pallas import tpu as pltpu
from jax.sharding import PartitionSpec as P

LANE = 128
f32 = jnp.float32
bf16 = jnp.bfloat16


def vmem(mib):
    return pltpu.CompilerParams(vmem_limit_bytes=mib << 20)


def cost(flops, moved):
    return pl.CostEstimate(flops=flops, bytes_accessed=moved, transcendentals=0)


def route_ranks(owners, sub_count):
    count = owners.shape[0]
    block = 128
    owner_block = owners.reshape(count // block, block)
    match = (owner_block[:, :, None] == jnp.arange(sub_count, dtype=jnp.int32)).astype(bf16)
    position = jnp.arange(block)
    lower = (position[:, None] > position[None, :]).astype(bf16)
    ahead = jnp.einsum("ij,bjo->bio", lower, match, preferred_element_type=f32)
    totals = jnp.sum(match.astype(f32), axis=1)
    base = jnp.cumsum(totals, axis=0) - totals
    rank = jnp.sum((ahead + base[:, None, :]) * match.astype(f32), axis=2)
    return rank.reshape(count).astype(jnp.int32)


def pack_kernel(lon_count, slots, slot_row, cell_row, values, packed, rows, big):
    levels, _, count = values.shape
    total = big.shape[0]
    targets = total // 256
    size = packed.shape[0] // targets
    share = total // (count // LANE)

    for j in range(count // LANE):
        big[j * share : (j + 1) * share, :] = jnp.zeros((share, LANE), f32)
        part = jnp.concatenate(
            [values[lev, :, j * LANE : (j + 1) * LANE] for lev in range(levels)], axis=0
        )
        rows[j * LANE : (j + 1) * LANE, :] = jnp.concatenate([part] * 4, axis=0).T

    slot, cell = slot_row[...], cell_row[...]
    line = ((cell.astype(f32) + 0.5) * (1.0 / lon_count)).astype(jnp.int32)
    column = cell - line * lon_count
    place = (lax.shift_right_logical(line, 2) * lon_count + column) * 4 + (line & 3)
    owner, rank = lax.shift_right_logical(slot, 8), slot & 255
    mine = owner == lax.broadcasted_iota(jnp.int32, (targets, count), 0)
    spot = (rank == lax.broadcasted_iota(jnp.int32, (256, count), 0)).astype(f32).astype(bf16)

    def put(half):
        return jnp.where(mine, half, 0).astype(f32).astype(bf16)

    both = lax.dot_general(
        jnp.concatenate([put(lax.shift_right_logical(place, 8)), put(place & 255)], axis=0),
        spot,
        (((1,), (1,)), ((), ())),
        preferred_element_type=f32,
    )
    cells = both[:targets] * 256.0 + both[targets:]
    for half in range(2):
        packed[pl.ds(64 + half, targets, stride=size), :] = cells[:, half * LANE : (half + 1) * LANE]

    step = PACK_STEP

    @pl.loop(0, count // step)
    def _(i):
        for u in range(step):
            j = i * step + u
            big[pl.ds(slots[j], 1), :] = rows[pl.ds(j, 1), :]

    quarter = lax.broadcasted_iota(jnp.int32, (64, LANE), 1) // 32

    @pl.loop(0, targets // PACK_SIDE)
    def _(i):
        run = packed.at[pl.ds(pl.multiple_of(i * PACK_SIDE * size, 8), PACK_SIDE * size), :]
        for e in range(PACK_SIDE):
            start = pl.multiple_of((i * PACK_SIDE + e) * 256, 256)
            out = big[pl.ds(start, 64), :]
            for k in range(1, 4):
                out = jnp.where(quarter == k, big[pl.ds(start + 64 * k, 64), :], out)
            run[e * size : e * size + 64, :] = out


PACK_STEP = 64
PACK_SIDE = 8


def pack(slots, cells, values, targets, lon_count):
    count = values.shape[2]
    total = targets * 256
    whole = pl.BlockSpec(memory_space=pltpu.VMEM)
    return pl.pallas_call(
        functools.partial(pack_kernel, lon_count),
        out_shape=jax.ShapeDtypeStruct((targets * 66, LANE), f32),
        in_specs=[pl.BlockSpec(memory_space=pltpu.SMEM), whole, whole, whole],
        out_specs=whole,
        scratch_shapes=[pltpu.VMEM((count, LANE), f32), pltpu.VMEM((total, LANE), f32)],
        compiler_params=vmem(60),
        cost_estimate=cost(0, 4 << 20),
        name="pack",
    )(slots, slots.reshape(1, count), cells.reshape(1, count), values)


def lat_sweeps(sets, decays, starts):
    count = len(sets[0])
    ends = [[] for _ in sets]
    for sweep in range(4):
        order = range(count) if sweep % 2 == 0 else range(count - 1, -1, -1)
        states = [start[sweep] for start in starts]
        outs = [[None] * count for _ in sets]
        for r in order:
            for i, rows in enumerate(sets):
                a, rest = decays[i](r)
                states[i] = a * states[i] + rest * rows[r]
                outs[i][r] = states[i]
        for i in range(len(sets)):
            ends[i].append(states[i])
        sets = outs
    return sets, ends


def decay_of_octet(decay, groups, o):
    rows = decay.shape[0] // 2

    def pair(r):
        at = r * groups + o * 8
        return decay[at : at + 8, :], decay[rows + at : rows + at + 8, :]

    return pair


CHAINS = 8
SIDE = 1


def forced_kernel(row_count, groups, places, got, background, decay, forced, moments, spread, field, sem, out_sem, *chains):
    total = spread.shape[0]
    depth = chains[0].shape[0]
    sources = spread.shape[0] // 256
    size = got.shape[0] // sources
    tiles = forced.shape[0]
    fetches = [
        pltpu.make_async_copy(
            background.at[:, ct * LANE : (ct + 1) * LANE], field.at[ct], sem.at[ct]
        )
        for ct in range(tiles)
    ]
    for fetch in fetches:
        fetch.start()

    row = lax.broadcasted_iota(jnp.int32, (8, LANE), 0)
    pick = (row == 0).astype(f32).astype(bf16)
    quarter = lax.broadcasted_iota(jnp.int32, (64, LANE), 1) // 32
    wanted = quarter.astype(f32)

    def turns(x):
        return [x] + [pltpu.roll(x, 32 * k, 1) for k in range(1, 4)]

    def repeat(turned, k):
        out = turned[(3 - k) % 4]
        for q in range(3):
            out = jnp.where(quarter == q, turned[(q - k) % 4], out)
        return out

    share = depth // sources
    together = 4

    @pl.loop(0, sources // together)
    def _(i):
        run = got.at[pl.ds(pl.multiple_of(i * together * size, 8), together * size), :]
        for e in range(together):
            d = i * together + e
            at = pl.ds(pl.multiple_of(d * share, 8), share)
            for chain in chains:
                chain[at, :] = jnp.zeros((share, LANE), f32)
            part = turns(run[e * size : e * size + 64, :])
            for half in range(2):
                cell = run[e * size + 64 + half : e * size + 65 + half, :]
                mark = lax.dot_general(
                    jnp.broadcast_to(cell - 4.0 * jnp.floor(cell * 0.25), (8, LANE)).astype(bf16),
                    pick,
                    (((0,), (0,)), ((), ())),
                    preferred_element_type=f32,
                )
                for k in (2 * half, 2 * half + 1):
                    first = (k % 2) * 64
                    one = jnp.where(mark[first : first + 64] == wanted, repeat(part, k), 0.0)
                    spread[pl.ds(pl.multiple_of(d * 256 + k * 64, 64), 64), :] = one

    step = 16

    @pl.loop(0, total // (CHAINS * step))
    def _(i):
        for u in range(step):
            spots = [(i * step + u) * CHAINS + c for c in range(CHAINS)]
            where = [pl.ds(places[j], 1) for j in spots]
            adds = [spread[pl.ds(j, 1), :] for j in spots]
            olds = [chains[c][where[c], :] for c in range(CHAINS)]
            for c in range(CHAINS):
                chains[c][where[c], :] = olds[c] + adds[c]

    for fetch in fetches:
        fetch.wait()
    columns = depth // (row_count // 4)

    @pl.loop(0, tiles)
    def _(ct):
        out = field.at[ct]
        for rr in range(row_count // 4):
            at = pl.ds(pl.multiple_of(rr * columns + ct * LANE, LANE), LANE)
            parts = [chain[at, :] for chain in chains]
            while len(parts) > 1:
                parts = [a + b for a, b in zip(parts[::2], parts[1::2])]
            turned = parts[0].T
            for q in range(4):
                for o in range(groups // 8):
                    at = pl.ds(o * 8 * row_count + rr * 4 + q, 8, stride=row_count)
                    first = q * groups + o * 8
                    out[at, :] = out[at, :] + turned[first : first + 8, :]
        pltpu.make_async_copy(field.at[ct], forced.at[ct], out_sem.at[ct]).start()
        zero = jnp.zeros((8, LANE), f32)
        per_group = moments.shape[0] // groups
        for first in range(0, groups // 8, SIDE):
            octets = range(first, first + SIDE)
            sets = [
                [
                    out[pl.ds(o * 8 * row_count + r, 8, stride=row_count), :]
                    for r in range(row_count)
                ]
                for o in octets
            ]
            _, ends = lat_sweeps(
                sets, [decay_of_octet(decay, groups, o) for o in octets], [[zero] * 4] * SIDE
            )
            for i, o in enumerate(octets):
                for k in range(4):
                    start = o * 8 * per_group + k * (per_group // 4) + ct
                    moments[pl.ds(start, 8, stride=per_group), :] = ends[i][k]

    for ct in range(tiles):
        pltpu.make_async_copy(field.at[ct], forced.at[ct], out_sem.at[ct]).wait()


def force(places, got, background, decay, row_count, groups):
    rows, columns = background.shape
    tiles = columns // LANE
    total = places.shape[0]
    depth = rows * columns // LANE
    whole = pl.BlockSpec(memory_space=pltpu.VMEM)
    return pl.pallas_call(
        functools.partial(forced_kernel, row_count, groups),
        out_shape=(
            jax.ShapeDtypeStruct((tiles, rows, LANE), f32),
            jax.ShapeDtypeStruct((groups * 4 * tiles, LANE), f32),
        ),
        in_specs=[
            pl.BlockSpec(memory_space=pltpu.SMEM),
            whole,
            pl.BlockSpec(memory_space=pl.ANY),
            whole,
        ],
        out_specs=(pl.BlockSpec(memory_space=pl.ANY), whole),
        scratch_shapes=[
            pltpu.VMEM((total, LANE), f32),
            pltpu.VMEM((tiles, rows, LANE), f32),
            pltpu.SemaphoreType.DMA((tiles,)),
            pltpu.SemaphoreType.DMA((tiles,)),
        ]
        + [pltpu.VMEM((depth, LANE), f32)] * CHAINS,
        compiler_params=vmem(58),
        cost_estimate=cost(0, 16 << 20),
        name="force",
    )(places, got, background, decay)


def lon_weights(length, columns):
    blocks = columns // LANE
    length = length[:, None, None]
    kappa = jnp.tanh(0.5 / length)
    beta = kappa * kappa
    alpha = beta / jnp.tanh(1.0 / length)
    i = jnp.arange(LANE, dtype=f32)

    def power(n):
        return jnp.exp(-n / length)

    gap = jnp.abs(i[:, None] - i[None, :])[None]
    local = (alpha + beta * gap) * power(gap)
    up, down = i[None, :, None], (LANE - 1.0) - i[None, :, None]
    sums = jnp.concatenate(
        [power(down), down * power(down), power(up), up * power(up)], axis=2
    )
    sums = jnp.pad(sums, ((0, 0), (0, 0), (0, LANE - 4)))
    first = jnp.concatenate([local, sums], axis=2)
    index = jnp.arange(LANE)
    src, dst = index[:, None], index[None, :]
    source, target = src // 4, dst // 4
    backward = (src % 4) >= 2
    steps = jnp.where(backward, source - target - 1, target - source - 1) % blocks
    gap = (LANE * steps).astype(f32)[None]
    turn = power(float(columns))
    left = -jnp.expm1(-float(columns) / length)
    same = power(gap) / left
    cross = (gap + columns * turn / left) * same
    used = (source < blocks) & (target < blocks)
    mix = jnp.where((used & (src % 4 == dst % 4))[None], same, 0.0)
    mix = jnp.where((used & (src % 2 == 0) & (dst % 4 == src % 4 + 1))[None], cross, mix)
    near, far = i[None, None, :] + 1.0, LANE - i[None, None, :]
    back = jnp.concatenate(
        [
            (alpha + beta * near) * power(near),
            beta * power(near),
            (alpha + beta * far) * power(far),
            beta * power(far),
        ],
        axis=1,
    )
    back = jnp.pad(back, ((0, 0), (0, LANE - 4), (0, 0)))
    return thirds(first), thirds(mix), thirds(back)


def thirds(w):
    high = lax.reduce_precision(w, 8, 7)
    low = (w - high).astype(bf16)
    high = high.astype(bf16)
    return jnp.concatenate([high, high, low], axis=1)


def dot3(x, w):
    high = x.astype(bf16)
    low = (x - high.astype(f32)).astype(bf16)
    return jnp.dot(jnp.concatenate([high, low, high], axis=1), w, preferred_element_type=f32)


def lon_apply(parts, first, mix, back):
    count, blocks = parts[0].shape[0], len(parts)
    both = dot3(jnp.concatenate(parts, axis=0), first)
    local, sums = both[:, :LANE], both[:, LANE:]
    line = sums[:count]
    for b in range(1, blocks):
        line = line + pltpu.roll(sums[b * count : (b + 1) * count], 4 * b, 1)
    states = dot3(line, mix)
    spread = jnp.concatenate(
        [states] + [pltpu.roll(states, LANE - 4 * b, 1) for b in range(1, blocks)], axis=0
    )
    out = local + dot3(spread, back)
    return [out[b * count : (b + 1) * count] for b in range(blocks)]


LON_STEP = 4


def hub_coefficients(decay):
    count = decay.shape[0]
    coef = [decay[r : r + 1, :] for r in range(count)]

    def forward(rows):
        state, out = jnp.zeros((1, LANE), f32), []
        for r in range(count):
            state = rows[r] + coef[r] * (state - rows[r])
            out.append(state)
        return out

    def backward(rows):
        state, out = jnp.zeros((1, LANE), f32), [None] * count
        for r in range(count - 1, -1, -1):
            state = rows[r] + coef[r] * (state - rows[r])
            out[r] = state
        return out

    state, down = jnp.ones((1, LANE), f32), []
    for r in range(count):
        state = coef[r] * state
        down.append(state)
    full = state
    state, up = jnp.ones((1, LANE), f32), [None] * count
    for r in range(count - 1, -1, -1):
        state = coef[r] * state
        up[r] = state
    bp = backward(down)
    fbp = forward(bp)
    bfbp = backward(fbp)
    fq = forward(up)
    bfq = backward(fq)
    return full, bp[0], fbp[-1], bfbp[0], fq[-1], bfq[0]


def exchange_kernel(
    count, variables, field, moments, decay, table, first, mix, back, own_first, own_mix, own_back,
    vert, coef, out, entered, arrived, replies, states, work, xs, ws, ms, bs, sums, beside, merged,
    joined, answers, entering, passed, sems, out_sem, send, recv, back_send, back_recv, pair_send,
    pair_recv, hub_send, hub_recv, reply_send, reply_recv, last_send, last_recv,
):
    tiles, rows, _ = out.shape
    blocks = arrived.shape[0]
    me = lax.axis_index("sub")
    steps = rows // count // LON_STEP
    size = LON_STEP * count

    def fetches(i):
        group = i * LON_STEP
        at = pl.ds(pl.multiple_of(group * count, 8), size)
        inside = pl.ds(group, LON_STEP)
        return [
            pltpu.make_async_copy(field.at[:, at], xs.at[:, at], sems.at[0, i]),
            pltpu.make_async_copy(first.at[inside], ws.at[inside], sems.at[1, i]),
            pltpu.make_async_copy(mix.at[inside], ms.at[inside], sems.at[2, i]),
            pltpu.make_async_copy(back.at[inside], bs.at[inside], sems.at[3, i]),
        ]

    for i in range(steps):
        for fetch in fetches(i):
            fetch.start()

    def lon_steps(start, stop):
        @pl.loop(start, stop)
        def _(i):
            for fetch in fetches(i):
                fetch.wait()
            for u in range(LON_STEP):
                g = i * LON_STEP + u
                at = pl.ds(pl.multiple_of(g * count, 8), count)
                parts = lon_apply([xs[b, at, :] for b in range(tiles)], ws[g], ms[g], bs[g])
                for b in range(tiles):
                    xs[b, at, :] = parts[b]

    barrier = pltpu.get_barrier_semaphore()

    @pl.loop(1, blocks)
    def _(step):
        target = lax.rem(me + step, blocks)
        pl.semaphore_signal(
            barrier, inc=1, device_id={"sub": target}, device_id_type=pl.DeviceIdType.MESH
        )

    band = lax.axis_index("band")
    chip, core = band // 2, band % 2
    sibling = chip * 2 + (1 - core)

    def other(step):
        return lax.rem(chip + step, 4) * 2 + core

    for target in [sibling] + [other(step) for step in (1, 2, 3)]:
        pl.semaphore_signal(
            barrier, inc=1, device_id={"band": target}, device_id_type=pl.DeviceIdType.MESH
        )
    pl.semaphore_wait(barrier, blocks - 1 + 4)

    def outward(step):
        target = lax.rem(me + step, blocks)
        return pltpu.make_async_remote_copy(
            src_ref=moments.at[target],
            dst_ref=arrived.at[me],
            send_sem=send.at[step - 1],
            recv_sem=recv.at[step - 1],
            device_id={"sub": target},
            device_id_type=pl.DeviceIdType.MESH,
        )

    def homeward(step):
        target = lax.rem(me + step, blocks)
        return pltpu.make_async_remote_copy(
            src_ref=replies.at[target],
            dst_ref=states.at[me],
            send_sem=back_send.at[step - 1],
            recv_sem=back_recv.at[step - 1],
            device_id={"sub": target},
            device_id_type=pl.DeviceIdType.MESH,
        )

    @pl.loop(1, blocks)
    def _(step):
        outward(step).start()

    arrived[me] = moments[me]
    full, t21, t31, t41, t32, t42 = hub_coefficients(decay)
    lon_steps(0, steps // 2)

    @pl.loop(1, blocks)
    def _(step):
        outward(step).wait_recv()

    def at(table, d):
        return jnp.broadcast_to(table[:, d : d + 1], (tiles, LANE))

    def moment(d, k):
        return arrived[d, k * tiles : (k + 1) * tiles, :]

    carry = jnp.zeros((tiles, LANE), f32)
    s = [[None] * blocks for _ in range(4)]
    for d in range(blocks):
        s[0][d] = carry
        carry = at(full, d) * carry + moment(d, 0)
    carry = jnp.zeros((tiles, LANE), f32)
    for d in range(blocks - 1, -1, -1):
        s[1][d] = carry
        carry = at(full, d) * carry + (moment(d, 1) + at(t21, d) * s[0][d])
    carry = jnp.zeros((tiles, LANE), f32)
    for d in range(blocks):
        s[2][d] = carry
        carry = at(full, d) * carry + (
            moment(d, 2) + at(t31, d) * s[0][d] + at(t32, d) * s[1][d]
        )
    carry = jnp.zeros((tiles, LANE), f32)
    for d in range(blocks - 1, -1, -1):
        s[3][d] = carry
        carry = at(full, d) * carry + (
            moment(d, 3) + at(t41, d) * s[0][d] + at(t42, d) * s[1][d] + at(t21, d) * s[2][d]
        )
    for k in range(4):
        for d in range(blocks):
            for t in range(tiles):
                work[t, k * blocks + d : k * blocks + d + 1, :] = s[k][d][t : t + 1, :]
    done = lon_apply([work[t] for t in range(tiles)], own_first[0], own_mix[0], own_back[0])
    for t in range(tiles):
        for k in range(4):
            replies[:, k * tiles + t, :] = done[t][k * blocks : (k + 1) * blocks]

    @pl.loop(1, blocks)
    def _(step):
        homeward(step).start()

    states[me] = replies[me]
    lon_steps(steps // 2, steps)

    @pl.loop(1, blocks)
    def _(step):
        homeward(step).wait_recv()

    @pl.loop(1, blocks)
    def _(step):
        outward(step).wait_send()
        homeward(step).wait_send()

    groups = rows // count
    levels = groups // variables
    half = tiles // 2
    depth = half * count
    tail = 2 * depth
    zero = jnp.zeros((8, LANE), f32)
    mine_first = core * 4

    def level_remote(src, dst, send_sem, recv_sem, target):
        return pltpu.make_async_remote_copy(
            src_ref=src,
            dst_ref=dst,
            send_sem=send_sem,
            recv_sem=recv_sem,
            device_id={"band": target},
            device_id_type=pl.DeviceIdType.MESH,
        )

    def pair(j):
        return level_remote(
            sums.at[(1 - core) * 4 + j], beside.at[j], pair_send.at[j], pair_recv.at[j], sibling
        )

    for target in range(2 * variables):
        sums[target, tail : tail + 8, :] = coef[target // 2]

    for side in range(2):

        @pl.loop(0, half)
        def _(spot):
            ct = side * half + spot
            done = xs.at[ct]
            for o in range(groups // 8):
                lines = [
                    done[pl.ds(o * 8 * count + r, 8, stride=count), :] for r in range(count)
                ]
                starts = [states[o * 8 : o * 8 + 8, k * tiles + ct, :] for k in range(4)]
                lines, _ = lat_sweeps([lines], [decay_of_octet(table, groups, o)], [starts])
                for r in range(count):
                    done[pl.ds(o * 8 * count + r, 8, stride=count), :] = lines[0][r]
            pltpu.make_async_copy(done, out.at[ct], out_sem.at[ct]).start()
            for var in range(variables):
                for t in range(count // 8):
                    lines = []
                    for lev in range(levels):
                        base = (lev * variables + var) * count + t * 8
                        lines.append(done[base : base + 8, :])
                    _, ends = level_sweeps(
                        lines, lambda lev: vert[lev * variables + var], [zero, zero]
                    )
                    for k in range(2):
                        at = pl.ds(pl.multiple_of(k * depth + spot * count + t * 8, 8), 8)
                        sums[var * 2 + side, at, :] = ends[k]

        for j in (side, side + 2):
            pair(j).start()

    def lower(a, b):
        return jnp.where(core == 0, a, b)

    def row(ref, chunk, at):
        return jnp.broadcast_to(ref[chunk, at : at + 1, :], (8, LANE))

    def bands_of(chunk, at):
        a, b = sums[mine_first + chunk, at, :], beside[chunk, at, :]
        return lower(a, b), lower(b, a)

    def coefficients(chunk):
        both = []
        for at in (tail, tail + 1):
            a, b = row(sums, mine_first + chunk, at), row(beside, chunk, at)
            both.append((lower(a, b), lower(b, a)))
        return both

    def hub_copy(j):
        step = lax.rem(j - chip + 4, 4)
        return level_remote(
            merged.at[j], joined.at[chip], hub_send.at[step - 1], hub_recv.at[step - 1], j * 2 + core
        )

    for j in (0, 2, 1, 3):
        pair(j).wait_recv()
        (full0, full1), (both0, both1) = coefficients(j)

        @pl.loop(0, depth // 8)
        def _(t):
            at = pl.ds(pl.multiple_of(t * 8, 8), 8)
            later = pl.ds(pl.multiple_of(depth + t * 8, 8), 8)
            up0, up1 = bands_of(j, at)
            down0, down1 = bands_of(j, later)
            merged[j, at, :] = full1 * up0 + up1
            merged[j, later, :] = down0 + full0 * (down1 + both1 * up0)

        index = lax.broadcasted_iota(jnp.int32, (8, LANE), 0)
        merged[j, tail : tail + 8, :] = jnp.where(
            index == 0, full0 * full1, both0 + full0 * both1 * full0
        )

        @pl.when(chip != j)
        def _():
            hub_copy(j).start()

    joined[chip] = merged[chip]
    for step in (1, 2, 3):
        hub_copy(lax.rem(chip + step, 4)).wait_recv()

    fulls = [row(joined, c, tail) for c in range(4)]
    boths = [row(joined, c, tail + 1) for c in range(4)]

    @pl.loop(0, depth // 8)
    def _(t):
        at = pl.ds(pl.multiple_of(t * 8, 8), 8)
        later = pl.ds(pl.multiple_of(depth + t * 8, 8), 8)
        state = jnp.zeros((8, LANE), f32)
        ups = []
        for c in range(4):
            ups.append(state)
            answers[c, at, :] = state
            state = fulls[c] * state + joined[c, at, :]
        state = jnp.zeros((8, LANE), f32)
        for c in (3, 2, 1, 0):
            answers[c, later, :] = state
            state = fulls[c] * state + (joined[c, later, :] + boths[c] * ups[c])

    answer_copies = []
    for step in (2, 1, 3):
        copy = level_remote(
            answers.at[lax.rem(chip + step, 4)],
            entering.at[chip],
            reply_send.at[step - 1],
            reply_recv.at[step - 1],
            other(step),
        )
        copy.start()
        answer_copies.append(copy)
    entering[chip] = answers[chip]
    for copy in answer_copies:
        copy.wait_recv()

    last = []
    for j in range(4):
        (full0, full1), (both0, both1) = coefficients(j)

        @pl.loop(0, depth // 8)
        def _(t):
            at = pl.ds(pl.multiple_of(t * 8, 8), 8)
            later = pl.ds(pl.multiple_of(depth + t * 8, 8), 8)
            up0, _ = bands_of(j, at)
            _, down1 = bands_of(j, later)
            below = entering[j, at, :]
            above = entering[j, later, :]
            middle = full0 * below + up0
            turned = full1 * above + (down1 + both1 * middle)
            entered[mine_first + j, at, :] = lower(below, middle)
            entered[mine_first + j, later, :] = lower(turned, above)
            passed[j, at, :] = lower(middle, below)
            passed[j, later, :] = lower(above, turned)

        copy = level_remote(
            passed.at[j], entered.at[mine_first + j], last_send.at[j], last_recv.at[j], sibling
        )
        copy.start()
        last.append(copy)

    for j in range(4):
        pair(j).wait_send()
    for step in (1, 2, 3):
        hub_copy(lax.rem(chip + step, 4)).wait_send()
    for copy in answer_copies:
        copy.wait_send()
    for copy in last:
        copy.wait()
    for ct in range(tiles):
        pltpu.make_async_copy(xs.at[ct], out.at[ct], out_sem.at[ct]).wait()


def exchange(field, moments, decay, table, weights, own_weights, vert, coef, row_count, variables):
    tiles, rows, _ = field.shape
    blocks, depth, _ = moments.shape
    groups = rows // row_count
    steps = groups // LON_STEP
    chunk = tiles * row_count
    any_space = pl.BlockSpec(memory_space=pl.ANY)
    whole = pl.BlockSpec(memory_space=pltpu.VMEM)
    dma = pltpu.SemaphoreType.DMA
    return pl.pallas_call(
        functools.partial(exchange_kernel, row_count, variables),
        out_shape=(
            jax.ShapeDtypeStruct(field.shape, f32),
            jax.ShapeDtypeStruct((2 * variables, chunk, LANE), f32),
        ),
        in_specs=[any_space, whole, whole, whole]
        + [any_space] * 3
        + [whole] * 3
        + [pl.BlockSpec(memory_space=pltpu.SMEM), whole],
        out_specs=(any_space, whole),
        scratch_shapes=[
            pltpu.VMEM(moments.shape, f32),
            pltpu.VMEM(moments.shape, f32),
            pltpu.VMEM(moments.shape, f32),
            pltpu.VMEM((tiles, 4 * blocks, LANE), f32),
            pltpu.VMEM(field.shape, f32),
        ]
        + [pltpu.VMEM(w.shape, w.dtype) for w in weights]
        + [pltpu.VMEM((2 * variables, chunk + 8, LANE), f32)]
        + [pltpu.VMEM((4, chunk + 8, LANE), f32)] * 3
        + [pltpu.VMEM((4, chunk, LANE), f32)] * 3
        + [dma((4, steps)), dma((tiles,))]
        + [dma((blocks - 1,))] * 4
        + [dma((4,)), dma((4,)), dma((3,)), dma((3,)), dma((3,)), dma((3,)), dma((4,)), dma((4,))],
        compiler_params=pltpu.CompilerParams(
            vmem_limit_bytes=60 << 20, collective_id=0, has_side_effects=True
        ),
        cost_estimate=cost(6 * rows * tiles * LANE * 3 * LANE, 60 << 20),
        name="exchange",
    )(field, moments, decay, table, *weights, *own_weights, vert, coef)


def level_sweeps(rows, decay, starts):
    count = len(rows)
    ends = []
    for sweep in range(2):
        order = range(count) if sweep == 0 else range(count - 1, -1, -1)
        state = starts[sweep]
        out = [None] * count
        for r in order:
            state = decay(r) * state + (1.0 - decay(r)) * rows[r]
            out[r] = state
        ends.append(state)
        rows = out
    return rows, ends


def level_states_kernel(source, vert, states, out, x, result, in_sem, sem):
    tiles, levels, variables, row_count, _ = x.shape
    fetches = [
        pltpu.make_async_copy(source.at[:, :, var], x.at[:, :, var], in_sem.at[var])
        for var in range(variables)
    ]
    for fetch in fetches:
        fetch.start()
    writes = []
    for var in range(variables):
        fetches[var].wait()
        decay = [vert[lev * variables + var] for lev in range(levels)]
        for ct in range(tiles):
            for t in range(row_count // 8):
                at = slice(t * 8, t * 8 + 8)
                rows = [x[ct, lev, var, at, :] for lev in range(levels)]
                starts = [states[var, ct // (tiles // 2), k, ct % (tiles // 2), at, :] for k in range(2)]
                rows, _ = level_sweeps(rows, lambda lev: decay[lev], starts)
                for lev in range(levels):
                    result[lev, var, at, ct * LANE : (ct + 1) * LANE] = rows[lev]
        write = pltpu.make_async_copy(result.at[:, var], out.at[:, var], sem.at[var])
        write.start()
        writes.append(write)
    for write in writes:
        write.wait()


def level_states(x, vert, states, shape):
    levels, variables, row_count, columns = shape
    tiles = columns // LANE
    whole = pl.BlockSpec(memory_space=pltpu.VMEM)
    return pl.pallas_call(
        level_states_kernel,
        out_shape=jax.ShapeDtypeStruct(shape, f32),
        in_specs=[pl.BlockSpec(memory_space=pl.ANY), pl.BlockSpec(memory_space=pltpu.SMEM), whole],
        out_specs=pl.BlockSpec(memory_space=pl.ANY),
        scratch_shapes=[
            pltpu.VMEM((tiles, levels, variables, row_count, LANE), f32),
            pltpu.VMEM(shape, f32),
            pltpu.SemaphoreType.DMA((variables,)),
            pltpu.SemaphoreType.DMA((variables,)),
        ],
        compiler_params=vmem(60),
        cost_estimate=cost(0, 11 << 20),
        name="level_states",
    )(x.reshape(tiles, levels, variables, row_count, LANE), vert, states)


def level_coefficients(decays):
    levels = decays.shape[0]
    state, down = jnp.ones_like(decays[0]), []
    for r in range(levels):
        state = decays[r] * state
        down.append(state)
    full = state
    state = jnp.zeros_like(full)
    for r in range(levels - 1, -1, -1):
        state = down[r] + decays[r] * (state - down[r])
    both = jnp.stack([full, state], axis=1)
    both = jnp.pad(both, ((0, 0), (0, 6)))
    return jnp.broadcast_to(both[:, :, None], both.shape + (LANE,))


def per_device(background, obs_columns, obs_owner, obs_cell, lat_length, lon_length, vert_length):
    level_count, var_count, row_count, lon_count = background.shape
    sub_count = lax.axis_size("sub")
    band_count = lax.axis_size("band")
    sub_index = lax.axis_index("sub")
    groups = level_count * var_count
    tiles = lon_count // LANE
    tile_field = background.reshape(groups * row_count, lon_count)
    owners = obs_owner[:, 0]
    capacity = 2 * owners.shape[0] // sub_count

    ranks = route_ranks(owners, sub_count)
    message = pack(owners * capacity + ranks, obs_cell, obs_columns, sub_count, lon_count)
    got = lax.all_to_all(message.reshape(sub_count, 1, -1), "sub", 0, 0, tiled=True)

    vert_decay = jnp.exp(-1.0 / vert_length)
    coef = level_coefficients(vert_decay)
    vert_decay = vert_decay.reshape(groups)

    lat_all = jnp.exp(-1.0 / lat_length).reshape(groups, sub_count, row_count)
    own_lat = lax.dynamic_index_in_dim(lat_all, sub_index, 1, False)
    own_lat = own_lat.T.reshape(row_count * groups, 1)
    own_lat = jnp.concatenate([own_lat, 1.0 - own_lat])
    decay = jnp.broadcast_to(own_lat, (2 * row_count * groups, LANE))
    hub_lat = lax.dynamic_index_in_dim(lat_all, sub_index, 0, False)
    hub_lat = jnp.pad(hub_lat.T, ((0, 0), (0, LANE - sub_count)))

    lengths = lon_length.reshape(groups)
    weights = lon_weights(lengths, lon_count)
    own_weights = [lax.dynamic_slice_in_dim(w, sub_index, 1, 0) for w in weights]

    ready = (got, weights, own_weights, decay, hub_lat, coef, vert_decay)
    got, weights, own_weights, decay, hub_lat, coef, vert_decay = lax.optimization_barrier(ready)
    places = got[:, 0, capacity * groups :].reshape(-1).astype(jnp.int32)
    forced, moments = force(places >> 2, got.reshape(-1, LANE), tile_field, decay, row_count, groups)
    smooth, entering = exchange(
        forced,
        moments.reshape(sub_count, 4 * tiles, LANE),
        hub_lat,
        decay,
        weights,
        own_weights,
        vert_decay,
        coef,
        row_count,
        var_count,
    )
    return level_states(
        smooth,
        vert_decay,
        entering.reshape(var_count, 2, 2, tiles // 2, row_count, LANE),
        background.shape,
    )


def solution(mesh):
    placed = (
        P("band", None, "sub", None),
        P("band", None, "sub"),
        P("sub", None),
        P("sub"),
        P("band", None, None),
        P("band", None),
        P("band", None),
    )
    return jax.shard_map(
        per_device,
        mesh=mesh,
        in_specs=placed,
        out_specs=P("band", None, "sub", None),
        check_vma=False,
    )
```
